32 devices in a mesh: dp: 8 (over z, y), kv: 4 (over x, core).
Axes of the slice: x: 2, y: 2, z: 4, core: 2. Of those that a mesh axis runs over, the one named last changes fastest.
Arguments:
- text_tokens: bfloat16 [6144, 768], P(('dp', 'kv')), may hold values from -6 to 6
- image_tokens: bfloat16 [96, 576, 768], P('dp', 'kv'), may hold values from -6 to 6
- image_lengths: int32 [96], P('dp'), may hold values from 196 to 576, as said below
- patch_mask: int32 [96, 576], P('dp', 'kv'), may hold values from 0 to 1, as said below
- self_query: bfloat16 [768, 768], P(('dp', 'kv')), may hold values from -0.21875 to 0.21875
- self_key: bfloat16 [768, 768], P(('dp', 'kv')), may hold values from -0.21875 to 0.21875
- self_value: bfloat16 [768, 768], P(('dp', 'kv')), may hold values from -0.21875 to 0.21875
- self_out: bfloat16 [768, 768], P(('dp', 'kv')), may hold values from -0.875 to 0.875
- cross_query: bfloat16 [768, 768], P(('dp', 'kv')), may hold values from -0.21875 to 0.21875
- cross_key: bfloat16 [768, 768], P(('dp', 'kv')), may hold values from -0.21875 to 0.21875
- cross_value: bfloat16 [768, 768], P(('dp', 'kv')), may hold values from -0.21875 to 0.21875
- cross_out: bfloat16 [768, 768], P(('dp', 'kv')), may hold values from -2.5 to 2.5
- mlp_up: bfloat16 [768, 3072], P(('dp', 'kv')), may hold values from -0.21875 to 0.21875
- mlp_down: bfloat16 [3072, 768], P(('dp', 'kv')), may hold values from -0.109375 to 0.109375
- norm_self: bfloat16 [768], P(('dp', 'kv')), may hold values from 0.5 to 1.5
- norm_cross: bfloat16 [768], P(('dp', 'kv')), may hold values from 0.5 to 1.5
- norm_mlp: bfloat16 [768], P(('dp', 'kv')), may hold values from 0.5 to 1.5
- out_grad: bfloat16 [6144, 768], P(('dp', 'kv')), may hold values from -6 to 6
Outputs:
- layer_out: bfloat16 [6144, 768], P(('dp', 'kv'))
- text_grad: float32 [6144, 768], P(('dp', 'kv'))
- image_grad: float32 [96, 576, 768], P('dp', 'kv')
- self_query_grad: float32 [768, 768], P(('dp', 'kv'))
- self_key_grad: float32 [768, 768], P(('dp', 'kv'))
- self_value_grad: float32 [768, 768], P(('dp', 'kv'))
- self_out_grad: float32 [768, 768], P(('dp', 'kv'))
- cross_query_grad: float32 [768, 768], P(('dp', 'kv'))
- cross_key_grad: float32 [768, 768], P(('dp', 'kv'))
- cross_value_grad: float32 [768, 768], P(('dp', 'kv'))
- cross_out_grad: float32 [768, 768], P(('dp', 'kv'))
- mlp_up_grad: float32 [768, 3072], P(('dp', 'kv'))
- mlp_down_grad: float32 [3072, 768], P(('dp', 'kv'))
- norm_self_grad: float32 [768], P(('dp', 'kv'))
- norm_cross_grad: float32 [768], P(('dp', 'kv'))
- norm_mlp_grad: float32 [768], P(('dp', 'kv'))
The draws below stay inside these ranges and needn't reach their ends.
Inputs may be any that keep to these rules, and one draw needn't show every extreme that they name: `image_lengths`: each value is 196 or 576, and both occur. `patch_mask`: the first token slot of every image is 1.
All inputs are finite; a program needn't handle non-finite values.
Results may differ from the reference program's by a relative error of at most 0.025.
Values may be sent and summed in bfloat16 or wider, within the bound.
A program may use at most 192 MiB of HBM per device.

```python
import math
import jax
import jax.numpy as jnp
from jax import lax

D = 768
FF = 3072
HEADS = 12
HD = 64
SEQ = 64
IMG = 576
LEN_SHORT = 196
CAPTIONS = 96
TOKENS = 6144


def draw_image_lengths(key, part):
    longer = jax.random.randint(key, (CAPTIONS,), 0, 2)
    lengths = LEN_SHORT + (IMG - LEN_SHORT) * longer
    return lengths.at[0].set(IMG).at[1].set(LEN_SHORT).astype(jnp.int32)


def draw_patch_mask(key, part):
    kept = (jax.random.randint(key, (CAPTIONS, IMG), 0, 8) != 0).astype(jnp.int32)
    return kept.at[:, 0].set(1)


def shard_levels(key, shape, cuts, low, high):
    def one(axis_at, parts):
        heights = jax.random.uniform(jax.random.fold_in(jax.random.fold_in(key, 6), axis_at), (parts,), jnp.float32, low / len(cuts), high / len(cuts))
        return jnp.repeat(jnp.exp(heights), shape[axis_at] // parts).reshape((-1,) + (1,) * (len(shape) - axis_at - 1))

    level = one(*cuts[0])
    for cut in cuts[1:]:
        level = level * one(*cut)
    return level


def scatter_about(key, dims, scale, most, shards=(), dtype=jnp.bfloat16):
    entries = scale * jax.random.normal(key, dims, jnp.float32)
    if shards:
        entries = entries * shard_levels(key, dims, shards, -0.22, 0.18)
    return jnp.clip(entries, -most, most).astype(dtype)


def setup_inputs(seed: int = 0) -> dict:
    seeds = jax.random.split(jax.random.key(seed), 19)
    text_tokens = scatter_about(seeds[0], (TOKENS, D), 1.0, 6.0, ((0, 32),))
    image_tokens = scatter_about(seeds[1], (CAPTIONS, IMG, D), 1.0, 6.0, ((0, 8), (1, 4)))
    image_lengths = draw_image_lengths(jax.random.fold_in(seeds[18], 71), 0)
    patch_mask = draw_patch_mask(jax.random.fold_in(seeds[18], 71), 0)
    self_query = scatter_about(seeds[4], (D, D), D ** -0.5, 0.21875, ((0, 32),))
    self_key = scatter_about(seeds[5], (D, D), D ** -0.5, 0.21875, ((0, 32),))
    self_value = scatter_about(seeds[6], (D, D), D ** -0.5, 0.21875, ((0, 32),))
    self_out = scatter_about(seeds[7], (D, D), (D // 16) ** -0.5, 0.875, ((0, 32),))
    cross_query = scatter_about(seeds[8], (D, D), D ** -0.5, 0.21875, ((0, 32),))
    cross_key = scatter_about(seeds[9], (D, D), D ** -0.5, 0.21875, ((0, 32),))
    cross_value = scatter_about(seeds[10], (D, D), D ** -0.5, 0.21875, ((0, 32),))
    cross_out = scatter_about(seeds[11], (D, D), (D // 128) ** -0.5, 2.5, ((0, 32),))
    mlp_up = scatter_about(seeds[12], (D, FF), D ** -0.5, 0.21875, ((0, 32),))
    mlp_down = scatter_about(seeds[13], (FF, D), FF ** -0.5, 0.109375, ((0, 32),))
    norm_self = jnp.clip(1.0 + 0.1 * jax.random.normal(seeds[14], (D,), jnp.float32), 0.5, 1.5).astype(jnp.bfloat16)
    norm_cross = jnp.clip(1.0 + 0.1 * jax.random.normal(seeds[15], (D,), jnp.float32), 0.5, 1.5).astype(jnp.bfloat16)
    norm_mlp = jnp.clip(1.0 + 0.1 * jax.random.normal(seeds[16], (D,), jnp.float32), 0.5, 1.5).astype(jnp.bfloat16)
    out_grad = scatter_about(seeds[17], (TOKENS, D), 1.0, 6.0, ((0, 32),))
    return {"text_tokens": text_tokens, "image_tokens": image_tokens, "image_lengths": image_lengths, "patch_mask": patch_mask, "self_query": self_query, "self_key": self_key, "self_value": self_value, "self_out": self_out, "cross_query": cross_query, "cross_key": cross_key, "cross_value": cross_value, "cross_out": cross_out, "mlp_up": mlp_up, "mlp_down": mlp_down, "norm_self": norm_self, "norm_cross": norm_cross, "norm_mlp": norm_mlp, "out_grad": out_grad}


@jax.custom_vjp
def low(v):
    return lax.optimization_barrier(v.astype(jnp.bfloat16)).astype(jnp.float32)

@jax.custom_vjp
def low_back(v):
    return v

def low_keep(v):
    return (low(v), None)

def low_pass(kept, grad):
    return (grad,)

def back_keep(v):
    return (v, None)

def back_low(kept, grad):
    return (low(grad),)
low.defvjp(low_keep, low_pass)
low_back.defvjp(back_keep, back_low)
EPS = 1e-05
NEG = -1e+30
HIGH = lax.Precision.HIGHEST
GELU_C = 0.7978845608028654
GELU_A = 0.044715

def round_both(values):
    return low(low_back(values))

def project(values, matrix):
    return jnp.einsum('...d,de->...e', values, matrix, precision=HIGH)

def layer_norm(values, gain):
    centre = values - lax.optimization_barrier(jnp.mean(values, -1, keepdims=True))
    return centre * lax.rsqrt(lax.optimization_barrier(jnp.mean(centre * centre, -1, keepdims=True)) + EPS) * gain

def gelu_tanh(values):
    return 0.5 * values * (1.0 + jnp.tanh(GELU_C * (values + GELU_A * values * values * values)))

def split_heads(values):
    return values.reshape(values.shape[:-1] + (HEADS, HD))

def attention(queries, keys_in, values_in, allowed):
    scores = low_back(jnp.einsum('cqhd,ckhd->chqk', queries, keys_in, precision=HIGH) * 0.125)
    probs = low(jax.nn.softmax(jnp.where(allowed, scores, NEG), axis=-1))
    return jnp.einsum('chqk,ckhd->cqhd', probs, values_in, precision=HIGH)

def forward(text_in, image_in, lengths, patches, params):
    query_self, key_self, value_self, out_self, query_cross, key_cross, value_cross, out_cross, up_proj, down_proj, gain_self, gain_cross, gain_mlp = params
    captions = text_in.shape[0]
    normed_one = low(layer_norm(text_in, gain_self))
    query_one = split_heads(round_both(project(normed_one, query_self)))
    key_one = split_heads(round_both(project(normed_one, key_self)))
    value_one = split_heads(round_both(project(normed_one, value_self)))
    causal = lax.broadcasted_iota(jnp.int32, (SEQ, SEQ), 0) >= lax.broadcasted_iota(jnp.int32, (SEQ, SEQ), 1)
    context_one = round_both(attention(query_one, key_one, value_one, causal[None, None])).reshape(captions, SEQ, D)
    second = text_in + low_back(project(context_one, out_self))
    normed_two = low(layer_norm(second, gain_cross))
    query_two = split_heads(round_both(project(normed_two, query_cross)))
    key_two = split_heads(round_both(project(image_in, key_cross)))
    value_two = split_heads(round_both(project(image_in, value_cross)))
    position = lax.broadcasted_iota(jnp.int32, (captions, IMG), 1)
    usable = jnp.logical_and(position < lengths[:, None], patches == 1)[:, None, None, :]
    context_two = round_both(attention(query_two, key_two, value_two, usable)).reshape(captions, SEQ, D)
    third = second + low_back(project(context_two, out_cross))
    normed_three = low(layer_norm(third, gain_mlp))
    hidden = low_back(project(normed_three, up_proj))
    active = low(gelu_tanh(hidden))
    return third + low_back(project(active, down_proj))

def add_trees(former, latter):
    return jax.tree.map(jnp.add, former, latter)

def reference(text_tokens, image_tokens, image_lengths, patch_mask, self_query, self_key, self_value, self_out, cross_query, cross_key, cross_value, cross_out, mlp_up, mlp_down, norm_self, norm_cross, norm_mlp, out_grad):
    params = tuple((weight.astype(jnp.float32) for weight in (self_query, self_key, self_value, self_out, cross_query, cross_key, cross_value, cross_out, mlp_up, mlp_down, norm_self, norm_cross, norm_mlp)))
    block_caps = math.gcd(CAPTIONS, 32)
    block_count = CAPTIONS // block_caps
    text_all = text_tokens.astype(jnp.float32).reshape(block_count, block_caps, SEQ, D)
    image_all = image_tokens.astype(jnp.float32).reshape(block_count, block_caps, IMG, D)
    length_all = image_lengths.astype(jnp.int32).reshape(block_count, block_caps)
    mask_all = patch_mask.astype(jnp.int32).reshape(block_count, block_caps, IMG)
    cotangent = out_grad.astype(jnp.float32).reshape(block_count, block_caps, SEQ, D)

    def one_block(summed, pieces):
        text_blk, image_blk, length_blk, mask_blk, cot_blk = pieces

        def apply_layer(text_in, image_in, weights):
            return forward(text_in, image_in, length_blk, mask_blk, weights)
        result, pullback = jax.vjp(apply_layer, text_blk, image_blk, params)
        grad_text, grad_image, grad_params = pullback(cot_blk)
        return (add_trees(summed, grad_params), (result.astype(jnp.bfloat16), grad_text, grad_image))
    zeros_init = jax.tree.map(jnp.zeros_like, params)
    summed, (outputs, text_grads, image_grads) = lax.scan(one_block, zeros_init, (text_all, image_all, length_all, mask_all, cotangent))
    return (outputs.reshape(TOKENS, D), text_grads.reshape(TOKENS, D), image_grads.reshape(CAPTIONS, IMG, D), summed[0], summed[1], summed[2], summed[3], summed[4], summed[5], summed[6], summed[7], summed[8], summed[9], summed[10], summed[11], summed[12])
```

```python
import functools

import jax
import jax.numpy as jnp
from jax import lax
from jax.experimental import pallas as pl
from jax.experimental.pallas import tpu as pltpu
from jax.sharding import PartitionSpec as P

MESH = pl.DeviceIdType.MESH


def ag_kernel(NDP, KV, n, *refs):
    Y = 2; Z = NDP // Y
    ins, outs = refs[:n], refs[n:2*n]
    recv, sz, s2, s3, sd, sl = refs[2*n:]
    di, ki = lax.axis_index("dp"), lax.axis_index("kv")
    z, y, x, c = di // Y, di % Y, ki // 2, ki % 2
    def slot(zz, yy, xx, cc): return (zz*Y+yy)*KV + xx*2 + cc
    up, dn = (di + Y, ki), (di - Y, ki)
    y2, x2 = y + c*(1-2*y), x + (1-c)*(1-2*x)
    y3, x3 = y + (1-c)*(1-2*y), x + c*(1-2*x)
    p2, p3, pd = (z*Y+y2, x2*2+c), (z*Y+y3, x3*2+c), (di, ki + 1 - 2*c)
    bar = pltpu.get_barrier_semaphore()
    @pl.when(z < Z-1)
    def _(): pl.semaphore_signal(bar, 1, device_id=up, device_id_type=MESH)
    @pl.when(z > 0)
    def _(): pl.semaphore_signal(bar, 1, device_id=dn, device_id_type=MESH)
    for p in (p2, p3, pd): pl.semaphore_signal(bar, 1, device_id=p, device_id_type=MESH)
    pl.semaphore_wait(bar, 3 + jnp.where(z < Z-1, 1, 0) + jnp.where(z > 0, 1, 0))
    own = slot(z, y, x, c)
    def cp(i, s, src, sem, dev):
        return pltpu.make_async_remote_copy(src_ref=src, dst_ref=outs[i].at[s], send_sem=sem, recv_sem=recv.at[i, s], device_id=dev, device_id_type=MESH)
    def send(s, sems, dev, src=None):
        for i in range(n):
            cp(i, s, ins[i] if src == "in" else outs[i].at[s], sems(i), dev).start()
    def wait_recv(s):
        for i in range(n):
            pltpu.make_async_copy(outs[i].at[s], outs[i].at[s], recv.at[i, s]).wait()
    for i in range(n):
        pltpu.make_async_copy(ins[i], outs[i].at[own], sl.at[i]).start()
    def spread2(zz, src=None):
        s = slot(zz, y, x, c)
        send(s, lambda i: s2.at[i, zz], p2, src)
        send(s, lambda i: s3.at[i, zz], p3, src)
        send(s, lambda i: sd.at[i, s//2], pd, src)
    @pl.when(z < Z-1)
    def _(): send(own, lambda i: sz.at[i, 0, z], up, "in")
    @pl.when(z > 0)
    def _(): send(own, lambda i: sz.at[i, 1, z], dn, "in")
    spread2(z, "in")
    def arrived2(zz):
        s = slot(zz, y2, x2, c)
        wait_recv(s)
        send(s, lambda i: s3.at[i, Z+zz], p3)
        send(s, lambda i: sd.at[i, s//2], pd)
    def step(t, _):
        @pl.when(z >= t)
        def _():
            s = slot(z-t, y, x, c); wait_recv(s)
            @pl.when(z < Z-1)
            def _(): send(s, lambda i: sz.at[i, 0, z-t], up)
            spread2(z-t)
        @pl.when(z + t < Z)
        def _():
            s = slot(z+t, y, x, c); wait_recv(s)
            @pl.when(z > 0)
            def _(): send(s, lambda i: sz.at[i, 1, z+t], dn)
            spread2(z+t)
        @pl.when(t == 1)
        def _(): arrived2(z)
        @pl.when(jnp.logical_and(t > 1, z >= t-1))
        def _(): arrived2(z-t+1)
        @pl.when(jnp.logical_and(t > 1, z+t-1 < Z))
        def _(): arrived2(z+t-1)
        return 0
    lax.fori_loop(1, Z+1, step, 0)
    def arrived3(zz):
        for yy, xx in ((y3, x3), (1-y, 1-x)):
            s = slot(zz, yy, xx, c)
            wait_recv(s)
            send(s, lambda i: sd.at[i, s//2], pd)
    def step3(t, _):
        @pl.when(z >= t)
        def _(): arrived3(z-t)
        @pl.when(jnp.logical_and(t > 0, z+t < Z))
        def _(): arrived3(z+t)
        return 0
    lax.fori_loop(0, Z, step3, 0)
    def fin(h, _):
        wait_recv(2*h + 1 - c)
        for i in range(n):
            o = outs[i].at[0]
            pltpu.make_async_copy(o, o, sd.at[i, h]).wait()
        return 0
    lax.fori_loop(0, NDP*KV//2, fin, 0)
    def finz(zz, _):
        for i in range(n):
            o = outs[i].at[0]
            pltpu.make_async_copy(o, o, s2.at[i, zz]).wait()
            pltpu.make_async_copy(o, o, s3.at[i, zz]).wait()
            pltpu.make_async_copy(o, o, s3.at[i, Z+zz]).wait()
            @pl.when(jnp.logical_and(z < Z-1, zz <= z))
            def _(): pltpu.make_async_copy(o, o, sz.at[i, 0, zz]).wait()
            @pl.when(jnp.logical_and(z > 0, zz >= z))
            def _(): pltpu.make_async_copy(o, o, sz.at[i, 1, zz]).wait()
        return 0
    lax.fori_loop(0, Z, finz, 0)
    for i in range(n):
        pltpu.make_async_copy(ins[i], outs[i].at[own], sl.at[i]).wait()

def all_gather(ins, NDP, KV, cid):
    n = len(ins); ND = NDP*KV; Z = NDP//2
    return pl.pallas_call(
        functools.partial(ag_kernel, NDP, KV, n),
        out_shape=[jax.ShapeDtypeStruct((ND,)+a.shape, a.dtype) for a in ins],
        in_specs=[pl.BlockSpec(memory_space=pltpu.VMEM)]*n,
        out_specs=[pl.BlockSpec(memory_space=pl.ANY)]*n,
        scratch_shapes=[pltpu.SemaphoreType.DMA((n, ND)), pltpu.SemaphoreType.DMA((n, 2, Z)), pltpu.SemaphoreType.DMA((n, Z)),
                        pltpu.SemaphoreType.DMA((n, 2*Z)), pltpu.SemaphoreType.DMA((n, ND//2)), pltpu.SemaphoreType.DMA((n,))],
        compiler_params=pltpu.CompilerParams(collective_id=cid, has_side_effects=True, vmem_limit_bytes=16<<20),
        name="gather_weights",
    )(*ins)


def rs_kernel(NDP, KV, n, *refs):
    Y = 2; Z = NDP // Y
    g, outs = refs[:n], refs[n:2*n]
    k = 2*n
    loc, r1, r2, r3, rz = (refs[k+j*n:k+(j+1)*n] for j in range(5))
    sl, sd, qd, s2, q2, s3, q3, sz, qz = refs[k+5*n:]
    di, ki = lax.axis_index("dp"), lax.axis_index("kv")
    z, y, x, c = di // Y, di % Y, ki // 2, ki % 2
    up, dn = (di + Y, ki), (di - Y, ki)
    y2, x2 = y + c*(1-2*y), x + (1-c)*(1-2*x)
    y3, x3 = y + (1-c)*(1-2*y), x + c*(1-2*x)
    p2, p3, pd = (z*Y+y2, x2*2+c), (z*Y+y3, x3*2+c), (di, ki + 1 - 2*c)
    def half(zz, yy, xx): return (zz*Y+yy)*(KV//2) + xx
    bar = pltpu.get_barrier_semaphore()
    @pl.when(z < Z-1)
    def _(): pl.semaphore_signal(bar, 1, device_id=up, device_id_type=MESH)
    @pl.when(z > 0)
    def _(): pl.semaphore_signal(bar, 1, device_id=dn, device_id_type=MESH)
    for p in (p2, p3, pd): pl.semaphore_signal(bar, 1, device_id=p, device_id_type=MESH)
    pl.semaphore_wait(bar, 3 + jnp.where(z < Z-1, 1, 0) + jnp.where(z > 0, 1, 0))
    def rc(src, dst, ss, rsem, dev):
        return pltpu.make_async_remote_copy(src_ref=src, dst_ref=dst, send_sem=ss, recv_sem=rsem, device_id=dev, device_id_type=MESH)
    def wait(ref, sem): pltpu.make_async_copy(ref, ref, sem).wait()
    def each(f):
        def body(t0, _):
            t = Z-1-t0
            @pl.when(z >= t)
            def _(): f(z-t)
            @pl.when(jnp.logical_and(t > 0, z+t < Z))
            def _(): f(z+t)
            return 0
        lax.fori_loop(0, Z, body, 0)
    def start(zz):
        for yy, xx in ((1-y, 1-x), (y2, x2), (y3, x3), (y, x)):
            h = half(zz, yy, xx)
            for i in range(n):
                rc(g[i].at[2*h+1-c], r1[i].at[h], sd.at[i, h], qd.at[i, h], pd).start()
                pltpu.make_async_copy(g[i].at[2*h+c], loc[i].at[h], sl.at[i, h]).start()
    each(start)
    def add1(h):
        for i in range(n):
            wait(loc[i].at[h], sl.at[i, h]); wait(r1[i].at[h], qd.at[i, h])
            loc[i][h] = loc[i][h] + r1[i][h]
    def stage2(zz):
        for j, (yy, xx) in enumerate(((1-y, 1-x), (y3, x3))):
            h = half(zz, yy, xx)
            add1(h)
            for i in range(n):
                rc(loc[i].at[h], r2[i].at[2*zz+j], s2.at[i, 2*zz+j], q2.at[i, 2*zz+j], p3).start()
        for yy, xx in ((y2, x2), (y, x)): add1(half(zz, yy, xx))
    each(stage2)
    def stage3(zz):
        for j, (yy, xx) in enumerate(((y2, x2), (y, x))):
            h = half(zz, yy, xx)
            for i in range(n):
                wait(r2[i].at[2*zz+j], q2.at[i, 2*zz+j])
                loc[i][h] = loc[i][h] + r2[i][2*zz+j]
                if j == 0:
                    rc(loc[i].at[h], r3[i].at[zz], s3.at[i, zz], q3.at[i, zz], p2).start()
    def stage4(zz, d, dev, has):
        h = half(zz, y, x)
        for i in range(n):
            wait(r3[i].at[zz], q3.at[i, zz])
            @pl.when(has)
            def _():
                wait(rz[i].at[d, zz], qz.at[i, d, zz])
                loc[i][h] = loc[i][h] + r3[i][zz] + rz[i][d, zz]
            @pl.when(jnp.logical_not(has))
            def _(): loc[i][h] = loc[i][h] + r3[i][zz]
            rc(loc[i].at[h], rz[i].at[d, zz], sz.at[i, d, zz], qz.at[i, d, zz], dev).start()
    def body(t0, _):
        t = Z-1-t0
        @pl.when(jnp.logical_and(t >= 0, z >= t))
        def _(): stage3(z-t)
        @pl.when(jnp.logical_and(t > 0, z+t < Z))
        def _(): stage3(z+t)
        u = t + 1
        @pl.when(z + u < Z)
        def _(): stage4(z+u, 0, up, z > 0)
        @pl.when(z >= u)
        def _(): stage4(z-u, 1, dn, z < Z-1)
        return 0
    lax.fori_loop(0, Z, body, 0)
    h = half(z, y, x)
    for i in range(n):
        wait(r3[i].at[z], q3.at[i, z])
        outs[i][...] = loc[i][h].astype(jnp.float32) + r3[i][z].astype(jnp.float32)
        @pl.when(z > 0)
        def _():
            wait(rz[i].at[0, z], qz.at[i, 0, z])
            outs[i][...] += rz[i][0, z].astype(jnp.float32)
        @pl.when(z < Z-1)
        def _():
            wait(rz[i].at[1, z], qz.at[i, 1, z])
            outs[i][...] += rz[i][1, z].astype(jnp.float32)
    def fin(h, _):
        for i in range(n): wait(r1[i].at[h], sd.at[i, h])
        return 0
    lax.fori_loop(0, NDP*KV//2, fin, 0)
    def fin2(zz, _):
        for i in range(n):
            wait(r3[i].at[zz], s3.at[i, zz])
            wait(r2[i].at[2*zz], s2.at[i, 2*zz]); wait(r2[i].at[2*zz+1], s2.at[i, 2*zz+1])
            @pl.when(zz > z)
            def _(): wait(rz[i].at[0, zz], sz.at[i, 0, zz])
            @pl.when(zz < z)
            def _(): wait(rz[i].at[1, zz], sz.at[i, 1, zz])
        return 0
    lax.fori_loop(0, Z, fin2, 0)

def reduce_scatter(gs, NDP, KV, cid):
    n = len(gs); ND = NDP*KV; Z = NDP//2
    D = pltpu.SemaphoreType.DMA
    def bufs(*lead): return [pltpu.VMEM(lead + g.shape[1:], g.dtype) for g in gs]
    return pl.pallas_call(
        functools.partial(rs_kernel, NDP, KV, n),
        out_shape=[jax.ShapeDtypeStruct(a.shape[1:], jnp.float32) for a in gs],
        in_specs=[pl.BlockSpec(memory_space=pl.ANY)]*n,
        out_specs=[pl.BlockSpec(memory_space=pltpu.VMEM)]*n,
        scratch_shapes=bufs(ND//2)+bufs(ND//2)+bufs(2*Z)+bufs(Z)+bufs(2, Z)
            +[D((n, ND//2))]*3+[D((n, 2*Z))]*2+[D((n, Z))]*2+[D((n, 2, Z))]*2,
        compiler_params=pltpu.CompilerParams(collective_id=cid, has_side_effects=True, vmem_limit_bytes=60<<20),
        name="scatter_gradients",
    )(*gs)

D = 768
FF = 3072
HEADS = 12
HD = 64
SEQ = 64


EPS = 1e-05
NEG = -1e30
GELU_C = 0.7978845608028654
GELU_A = 0.044715


def matmul(left, right):
    return jnp.dot(left, right, preferred_element_type=jnp.float32)


def matmul_tn(left, right):
    return lax.dot_general(
        left, right, (((0,), (0,)), ((), ())), preferred_element_type=jnp.float32
    )


def matmul_nt(left, right):
    return lax.dot_general(
        left, right, (((1,), (1,)), ((), ())), preferred_element_type=jnp.float32
    )


def split_heads(values):
    return values.reshape(values.shape[:-1] + (HEADS, HD))


def norm_forward(values, gain):
    centre = values - jnp.mean(values, -1, keepdims=True)
    scaled = lax.rsqrt(jnp.mean(centre * centre, -1, keepdims=True) + EPS)
    unit = centre * scaled
    return (unit * gain, unit, scaled)


def norm_backward(upstream, unit, scaled, gain):
    through = upstream * gain
    inner = (
        through
        - jnp.mean(through, -1, keepdims=True)
        - unit * jnp.mean(through * unit, -1, keepdims=True)
    )
    return inner * scaled


def gelu_forward(values):
    return 0.5 * values * (1.0 + jnp.tanh(GELU_C * (values + GELU_A * values * values * values)))


def gelu_slope(values):
    tanh_part = jnp.tanh(GELU_C * (values + GELU_A * values * values * values))
    return 0.5 * (1.0 + tanh_part) + 0.5 * values * (1.0 - tanh_part * tanh_part) * GELU_C * (
        1.0 + 3.0 * GELU_A * values * values
    )


def per_device(
    text_tokens,
    image_tokens,
    image_lengths,
    patch_mask,
    self_query,
    self_key,
    self_value,
    self_out,
    cross_query,
    cross_key,
    cross_value,
    cross_out,
    mlp_up,
    mlp_down,
    norm_self,
    norm_cross,
    norm_mlp,
    out_grad,
):
    ndp, nkv = lax.axis_size("dp"), lax.axis_size("kv")
    gains = jnp.stack([norm_self, norm_cross, norm_mlp], 1)
    packed = jnp.concatenate(
        [self_query, self_key, self_value, self_out, cross_query, cross_key, cross_value, cross_out, mlp_up,
         jnp.pad(gains, ((0, 0), (0, 125)))], 1)
    packed_full, down_full = all_gather([packed, mlp_down], ndp, nkv, 1)
    packed_full = packed_full.reshape(D, -1)
    down_full = down_full.reshape(FF, D)
    query_self, key_self, value_self, out_self, query_cross, key_cross, value_cross, out_cross = (
        packed_full[:, index * D : (index + 1) * D] for index in range(8))
    up_full = packed_full[:, 8 * D : 8 * D + FF]
    gain_self, gain_cross, gain_mlp = (packed_full[:, 8 * D + FF + index] for index in range(3))
    row_count = text_tokens.shape[0]
    captions = row_count // SEQ
    residual_one = text_tokens.astype(jnp.float32)
    normed_one, unit_one, scale_one = norm_forward(residual_one, gain_self.astype(jnp.float32))
    normed_one = normed_one.astype(jnp.bfloat16)
    query_one = split_heads(
        matmul(normed_one, query_self).astype(jnp.bfloat16).reshape(captions, SEQ, D)
    )
    key_one = split_heads(
        matmul(normed_one, key_self).astype(jnp.bfloat16).reshape(captions, SEQ, D)
    )
    value_one = split_heads(
        matmul(normed_one, value_self).astype(jnp.bfloat16).reshape(captions, SEQ, D)
    )
    causal = lax.broadcasted_iota(jnp.int32, (SEQ, SEQ), 0) >= lax.broadcasted_iota(
        jnp.int32, (SEQ, SEQ), 1
    )
    scores_one = (
        jnp.einsum("cqhd,ckhd->chqk", query_one, key_one, preferred_element_type=jnp.float32)
        * 0.125
    )
    probs_one = jax.nn.softmax(jnp.where(causal[None, None], scores_one, NEG), axis=-1)
    probs_low_one = probs_one.astype(jnp.bfloat16)
    context_one = jnp.einsum(
        "chqk,ckhd->cqhd", probs_low_one, value_one, preferred_element_type=jnp.float32
    )
    context_low_one = context_one.astype(jnp.bfloat16).reshape(row_count, D)
    residual_two = residual_one + matmul(context_low_one, out_self)
    normed_two, unit_two, scale_two = norm_forward(residual_two, gain_cross.astype(jnp.float32))
    normed_two = normed_two.astype(jnp.bfloat16)
    query_two = matmul(normed_two, query_cross).astype(jnp.bfloat16)
    query_group = lax.all_gather(query_two, "kv", axis=0, tiled=True)
    group_caps = query_group.shape[0] // SEQ
    patches = image_tokens.shape[1]
    flat_image = image_tokens.reshape(group_caps * patches, D)
    key_two = split_heads(
        matmul(flat_image, key_cross).astype(jnp.bfloat16).reshape(group_caps, patches, D)
    )
    value_two = split_heads(
        matmul(flat_image, value_cross).astype(jnp.bfloat16).reshape(group_caps, patches, D)
    )
    position = (
        lax.broadcasted_iota(jnp.int32, (group_caps, patches), 1) + lax.axis_index("kv") * patches
    )
    usable = jnp.logical_and(position < image_lengths[:, None], patch_mask == 1)[:, None, None, :]
    query_heads = split_heads(query_group.reshape(group_caps, SEQ, D))
    scores_two = (
        jnp.einsum("cqhd,ckhd->chqk", query_heads, key_two, preferred_element_type=jnp.float32)
        * 0.125
    )
    masked_two = jnp.where(usable, scores_two, NEG)
    local_max = jnp.max(masked_two, -1)
    local_sum = jnp.sum(jnp.where(usable, jnp.exp(masked_two - local_max[..., None]), 0.0), -1)
    glob_max = lax.pmax(local_max.astype(jnp.bfloat16), "kv").astype(local_max.dtype)
    glob_sum = lax.psum(
        (local_sum * jnp.exp(local_max - glob_max)).astype(jnp.bfloat16), "kv"
    ).astype(jnp.float32)
    log_total = glob_max + jnp.log(glob_sum)
    probs_two = jnp.where(usable, jnp.exp(scores_two - log_total[..., None]), 0.0)
    probs_low_two = probs_two.astype(jnp.bfloat16)
    partial_two = jnp.einsum(
        "chqk,ckhd->cqhd", probs_low_two, value_two, preferred_element_type=jnp.float32
    )
    context_two = lax.psum_scatter(
        partial_two.reshape(group_caps * SEQ, D).astype(jnp.bfloat16),
        "kv",
        scatter_dimension=0,
        tiled=True,
    )
    residual_three = residual_two + matmul(context_two, out_cross)
    normed_three, unit_three, scale_three = norm_forward(
        residual_three, gain_mlp.astype(jnp.float32)
    )
    normed_three = normed_three.astype(jnp.bfloat16)
    hidden = matmul(normed_three, up_full)
    active = gelu_forward(hidden).astype(jnp.bfloat16)
    layer_out = (residual_three + matmul(active, down_full)).astype(jnp.bfloat16)
    grad_active = matmul_nt(out_grad, down_full)
    grad_hidden = (grad_active * gelu_slope(hidden)).astype(jnp.bfloat16)
    upstream_three = matmul_nt(grad_hidden, up_full)
    back_three = norm_backward(
        upstream_three, unit_three, scale_three, gain_mlp.astype(jnp.float32)
    )
    grad_three = out_grad.astype(jnp.float32) + back_three
    branch_three = grad_three.astype(jnp.bfloat16)
    grad_context_two = matmul_nt(branch_three, out_cross).astype(jnp.bfloat16)
    grad_group = split_heads(
        lax.all_gather(grad_context_two, "kv", axis=0, tiled=True).reshape(group_caps, SEQ, D)
    )
    grad_probs_two = jnp.einsum(
        "cqhd,ckhd->chqk", grad_group, value_two, preferred_element_type=jnp.float32
    )
    row_dots = lax.psum(jnp.sum(probs_two * grad_probs_two, -1).astype(jnp.bfloat16), "kv").astype(
        jnp.float32
    )
    grad_scores_two = (probs_two * (grad_probs_two - row_dots[..., None])).astype(jnp.bfloat16)
    grad_value_two = jnp.einsum(
        "chqk,cqhd->ckhd", probs_low_two, grad_group, preferred_element_type=jnp.float32
    )
    grad_value_flat = grad_value_two.astype(jnp.bfloat16).reshape(group_caps * patches, D)
    grad_key_two = (
        jnp.einsum(
            "chqk,cqhd->ckhd", grad_scores_two, query_heads, preferred_element_type=jnp.float32
        )
        * 0.125
    )
    grad_key_flat = grad_key_two.astype(jnp.bfloat16).reshape(group_caps * patches, D)
    grad_query_part = (
        jnp.einsum("chqk,ckhd->cqhd", grad_scores_two, key_two, preferred_element_type=jnp.float32)
        * 0.125
    )
    grad_query_two = lax.psum_scatter(
        grad_query_part.reshape(group_caps * SEQ, D).astype(jnp.bfloat16),
        "kv",
        scatter_dimension=0,
        tiled=True,
    )
    image_grad = (
        matmul_nt(grad_key_flat, key_cross) + matmul_nt(grad_value_flat, value_cross)
    ).reshape(group_caps, patches, D)
    upstream_two = matmul_nt(grad_query_two, query_cross)
    back_two = norm_backward(upstream_two, unit_two, scale_two, gain_cross.astype(jnp.float32))
    grad_two = grad_three + back_two
    branch_two = grad_two.astype(jnp.bfloat16)
    grad_context_one = split_heads(
        matmul_nt(branch_two, out_self).astype(jnp.bfloat16).reshape(captions, SEQ, D)
    )
    grad_probs_one = jnp.einsum(
        "cqhd,ckhd->chqk", grad_context_one, value_one, preferred_element_type=jnp.float32
    )
    row_one = jnp.sum(probs_one * grad_probs_one, -1, keepdims=True)
    grad_scores_one = (probs_one * (grad_probs_one - row_one)).astype(jnp.bfloat16)
    grad_value_one = jnp.einsum(
        "chqk,cqhd->ckhd", probs_low_one, grad_context_one, preferred_element_type=jnp.float32
    )
    grad_value_one = grad_value_one.astype(jnp.bfloat16).reshape(row_count, D)
    grad_key_one = (
        jnp.einsum(
            "chqk,cqhd->ckhd", grad_scores_one, query_one, preferred_element_type=jnp.float32
        )
        * 0.125
    )
    grad_key_one = grad_key_one.astype(jnp.bfloat16).reshape(row_count, D)
    grad_query_one = (
        jnp.einsum("chqk,ckhd->cqhd", grad_scores_one, key_one, preferred_element_type=jnp.float32)
        * 0.125
    )
    grad_query_one = grad_query_one.astype(jnp.bfloat16).reshape(row_count, D)
    upstream_one = (
        matmul_nt(grad_query_one, query_self)
        + matmul_nt(grad_key_one, key_self)
        + matmul_nt(grad_value_one, value_self)
    )
    back_one = norm_backward(upstream_one, unit_one, scale_one, gain_self.astype(jnp.float32))
    text_grad = grad_two + back_one
    pieces = [
        matmul_tn(normed_one, grad_query_one),
        matmul_tn(normed_one, grad_key_one),
        matmul_tn(normed_one, grad_value_one),
        matmul_tn(context_low_one, branch_two),
        matmul_tn(normed_two, grad_query_two),
        matmul_tn(flat_image, grad_key_flat),
        matmul_tn(flat_image, grad_value_flat),
        matmul_tn(context_two, branch_three),
        matmul_tn(normed_three, grad_hidden),
        jnp.pad(
            jnp.stack(
                [jnp.sum(upstream_one * unit_one, 0), jnp.sum(upstream_two * unit_two, 0),
                 jnp.sum(upstream_three * unit_three, 0)], 1),
            ((0, 0), (0, 125))),
    ]
    devices = ndp * nkv
    feature_grad = jnp.concatenate([piece.astype(jnp.bfloat16) for piece in pieces], 1).reshape(devices, D // devices, -1)
    down_grad = matmul_tn(active, out_grad).astype(jnp.bfloat16).reshape(devices, FF // devices, D)
    feature_part, down_part = reduce_scatter([feature_grad, down_grad], ndp, nkv, 2)
    weight_parts = tuple((feature_part[:, index * D : (index + 1) * D] for index in range(8)))
    up_part = feature_part[:, 8 * D : 8 * D + FF]
    gain_base = 8 * D + FF
    return (
        (layer_out, text_grad, image_grad)
        + weight_parts
        + (
            up_part,
            down_part,
            feature_part[:, gain_base],
            feature_part[:, gain_base + 1],
            feature_part[:, gain_base + 2],
        )
    )


def solution(mesh):
    in_specs = (
        P(("dp", "kv"), None),
        P("dp", "kv", None),
        P("dp"),
        P("dp", "kv"),
        P(("dp", "kv"), None),
        P(("dp", "kv"), None),
        P(("dp", "kv"), None),
        P(("dp", "kv"), None),
        P(("dp", "kv"), None),
        P(("dp", "kv"), None),
        P(("dp", "kv"), None),
        P(("dp", "kv"), None),
        P(("dp", "kv"), None),
        P(("dp", "kv"), None),
        P(("dp", "kv")),
        P(("dp", "kv")),
        P(("dp", "kv")),
        P(("dp", "kv"), None),
    )
    out_specs = (
        P(("dp", "kv"), None),
        P(("dp", "kv"), None),
        P("dp", "kv", None),
        P(("dp", "kv"), None),
        P(("dp", "kv"), None),
        P(("dp", "kv"), None),
        P(("dp", "kv"), None),
        P(("dp", "kv"), None),
        P(("dp", "kv"), None),
        P(("dp", "kv"), None),
        P(("dp", "kv"), None),
        P(("dp", "kv"), None),
        P(("dp", "kv"), None),
        P(("dp", "kv")),
        P(("dp", "kv")),
        P(("dp", "kv")),
    )
    return jax.shard_map(
        per_device, mesh=mesh, in_specs=in_specs, out_specs=out_specs, check_vma=False
    )
```

```python
import functools

import jax
import jax.numpy as jnp
from jax import lax
from jax.experimental import pallas as pl
from jax.experimental.pallas import tpu as pltpu
from jax.sharding import PartitionSpec as P

MESH = pl.DeviceIdType.MESH
def ag_kernel(NDP, KV, count, *refs):
    n = 2
    parts, down = refs[:count], refs[count]
    refs = refs[count+1:]
    Y = 2; Z = NDP // Y
    outs = refs[:n]
    recv, sz, s2, s3, sd, sl, pack, fill = refs[n:]
    ins = [pack, down]
    offset, fills = 0, []
    for j, part in enumerate(parts):
        width = part.shape[1]
        fills.append(pltpu.make_async_copy(part, pack.at[:, pl.ds(offset, width)], fill.at[j]))
        offset += width
    for copy in fills: copy.start()
    di, ki = lax.axis_index("dp"), lax.axis_index("kv")
    z, y, x, c = di // Y, di % Y, ki // 2, ki % 2
    def slot(zz, yy, xx, cc): return (zz*Y+yy)*KV + xx*2 + cc
    up, dn = (di + Y, ki), (di - Y, ki)
    y2, x2 = y + c*(1-2*y), x + (1-c)*(1-2*x)
    y3, x3 = y + (1-c)*(1-2*y), x + c*(1-2*x)
    p2, p3, pd = (z*Y+y2, x2*2+c), (z*Y+y3, x3*2+c), (di, ki + 1 - 2*c)
    bar = pltpu.get_barrier_semaphore()
    @pl.when(z < Z-1)
    def _(): pl.semaphore_signal(bar, 1, device_id=up, device_id_type=MESH)
    @pl.when(z > 0)
    def _(): pl.semaphore_signal(bar, 1, device_id=dn, device_id_type=MESH)
    for p in (p2, p3, pd): pl.semaphore_signal(bar, 1, device_id=p, device_id_type=MESH)
    pl.semaphore_wait(bar, 3 + jnp.where(z < Z-1, 1, 0) + jnp.where(z > 0, 1, 0))
    own = slot(z, y, x, c)
    for copy in fills: copy.wait()
    def cp(i, s, src, sem, dev):
        return pltpu.make_async_remote_copy(src_ref=src, dst_ref=outs[i].at[s], send_sem=sem, recv_sem=recv.at[i, s], device_id=dev, device_id_type=MESH)
    def send(s, sems, dev, src=None):
        for i in range(n):
            cp(i, s, ins[i] if src == "in" else outs[i].at[s], sems(i), dev).start()
    def wait_recv(s):
        for i in range(n):
            pltpu.make_async_copy(outs[i].at[s], outs[i].at[s], recv.at[i, s]).wait()
    for i in range(n):
        pltpu.make_async_copy(ins[i], outs[i].at[own], sl.at[i]).start()
    def spread2(zz, src=None):
        s = slot(zz, y, x, c)
        send(s, lambda i: s2.at[i, zz], p2, src)
        send(s, lambda i: s3.at[i, zz], p3, src)
        send(s, lambda i: sd.at[i, s//2], pd, src)
    @pl.when(z < Z-1)
    def _(): send(own, lambda i: sz.at[i, 0, z], up, "in")
    @pl.when(z > 0)
    def _(): send(own, lambda i: sz.at[i, 1, z], dn, "in")
    spread2(z, "in")
    def arrived2(zz):
        s = slot(zz, y2, x2, c)
        wait_recv(s)
        send(s, lambda i: s3.at[i, Z+zz], p3)
        send(s, lambda i: sd.at[i, s//2], pd)
    def step(t, _):
        @pl.when(z >= t)
        def _():
            s = slot(z-t, y, x, c); wait_recv(s)
            @pl.when(z < Z-1)
            def _(): send(s, lambda i: sz.at[i, 0, z-t], up)
            spread2(z-t)
        @pl.when(z + t < Z)
        def _():
            s = slot(z+t, y, x, c); wait_recv(s)
            @pl.when(z > 0)
            def _(): send(s, lambda i: sz.at[i, 1, z+t], dn)
            spread2(z+t)
        @pl.when(t == 1)
        def _(): arrived2(z)
        @pl.when(jnp.logical_and(t > 1, z >= t-1))
        def _(): arrived2(z-t+1)
        @pl.when(jnp.logical_and(t > 1, z+t-1 < Z))
        def _(): arrived2(z+t-1)
        return 0
    lax.fori_loop(1, Z+1, step, 0)
    def arrived3(zz):
        for yy, xx in ((y3, x3), (1-y, 1-x)):
            s = slot(zz, yy, xx, c)
            wait_recv(s)
            send(s, lambda i: sd.at[i, s//2], pd)
    def step3(t, _):
        @pl.when(z >= t)
        def _(): arrived3(z-t)
        @pl.when(jnp.logical_and(t > 0, z+t < Z))
        def _(): arrived3(z+t)
        return 0
    lax.fori_loop(0, Z, step3, 0)
    def fin(h, _):
        wait_recv(2*h + 1 - c)
        for i in range(n):
            o = outs[i].at[0]
            pltpu.make_async_copy(o, o, sd.at[i, h]).wait()
        return 0
    lax.fori_loop(0, NDP*KV//2, fin, 0)
    def finz(zz, _):
        for i in range(n):
            o = outs[i].at[0]
            pltpu.make_async_copy(o, o, s2.at[i, zz]).wait()
            pltpu.make_async_copy(o, o, s3.at[i, zz]).wait()
            pltpu.make_async_copy(o, o, s3.at[i, Z+zz]).wait()
            @pl.when(jnp.logical_and(z < Z-1, zz <= z))
            def _(): pltpu.make_async_copy(o, o, sz.at[i, 0, zz]).wait()
            @pl.when(jnp.logical_and(z > 0, zz >= z))
            def _(): pltpu.make_async_copy(o, o, sz.at[i, 1, zz]).wait()
        return 0
    lax.fori_loop(0, Z, finz, 0)
    for i in range(n):
        pltpu.make_async_copy(ins[i], outs[i].at[own], sl.at[i]).wait()

def all_gather(parts, down, NDP, KV, cid):
    n = 2; ND = NDP*KV; Z = NDP//2
    rows, width = parts[0].shape[0], sum(p.shape[1] for p in parts)
    return pl.pallas_call(
        functools.partial(ag_kernel, NDP, KV, len(parts)),
        out_shape=[jax.ShapeDtypeStruct((ND, rows, width), jnp.bfloat16), jax.ShapeDtypeStruct((ND,)+down.shape, down.dtype)],
        in_specs=[pl.BlockSpec(memory_space=pl.ANY)]*(len(parts)+1),
        out_specs=[pl.BlockSpec(memory_space=pl.ANY)]*n,
        scratch_shapes=[pltpu.SemaphoreType.DMA((n, ND)), pltpu.SemaphoreType.DMA((n, 2, Z)), pltpu.SemaphoreType.DMA((n, Z)),
                        pltpu.SemaphoreType.DMA((n, 2*Z)), pltpu.SemaphoreType.DMA((n, ND//2)), pltpu.SemaphoreType.DMA((n,)),
                        pltpu.VMEM((rows, width), jnp.bfloat16), pltpu.SemaphoreType.DMA((len(parts),))],
        compiler_params=pltpu.CompilerParams(collective_id=cid, has_side_effects=True, vmem_limit_bytes=16<<20),
        name="gather_weights",
    )(*parts, down)


def rs_kernel(NDP, KV, layout, *refs):
    n, count = 2, len(layout)
    Y = 2; Z = NDP // Y
    g, outs = refs[:count], refs[count:2*count]
    k = 2*count
    loc, r1, r2, r3, rz = (refs[k+j*n:k+(j+1)*n] for j in range(5))
    sl, sd, qd, s2, q2, s3, q3, sz, qz = refs[k+5*n:]
    di, ki = lax.axis_index("dp"), lax.axis_index("kv")
    z, y, x, c = di // Y, di % Y, ki // 2, ki % 2
    up, dn = (di + Y, ki), (di - Y, ki)
    y2, x2 = y + c*(1-2*y), x + (1-c)*(1-2*x)
    y3, x3 = y + (1-c)*(1-2*y), x + c*(1-2*x)
    p2, p3, pd = (z*Y+y2, x2*2+c), (z*Y+y3, x3*2+c), (di, ki + 1 - 2*c)
    def half(zz, yy, xx): return (zz*Y+yy)*(KV//2) + xx
    bar = pltpu.get_barrier_semaphore()
    @pl.when(z < Z-1)
    def _(): pl.semaphore_signal(bar, 1, device_id=up, device_id_type=MESH)
    @pl.when(z > 0)
    def _(): pl.semaphore_signal(bar, 1, device_id=dn, device_id_type=MESH)
    for p in (p2, p3, pd): pl.semaphore_signal(bar, 1, device_id=p, device_id_type=MESH)
    pl.semaphore_wait(bar, 3 + jnp.where(z < Z-1, 1, 0) + jnp.where(z > 0, 1, 0))
    def rc(src, dst, ss, rsem, dev):
        return pltpu.make_async_remote_copy(src_ref=src, dst_ref=dst, send_sem=ss, recv_sem=rsem, device_id=dev, device_id_type=MESH)
    def wait(ref, sem): pltpu.make_async_copy(ref, ref, sem).wait()
    def each(f):
        def body(t0, _):
            t = Z-1-t0
            @pl.when(z >= t)
            def _(): f(z-t)
            @pl.when(jnp.logical_and(t > 0, z+t < Z))
            def _(): f(z+t)
            return 0
        lax.fori_loop(0, Z, body, 0)
    def start(zz):
        for yy, xx in ((1-y, 1-x), (y2, x2), (y3, x3), (y, x)):
            h = half(zz, yy, xx)
            for ref, (i, offset, width) in zip(g, layout):
                cols = pl.ds(offset, width)
                rc(ref.at[2*h+1-c], r1[i].at[h, :, cols], sd.at[i, h], qd.at[i, h], pd).start()
                pltpu.make_async_copy(ref.at[2*h+c], loc[i].at[h, :, cols], sl.at[i, h]).start()
    each(start)
    def add1(h):
        for i in range(n):
            wait(loc[i].at[h], sl.at[i, h]); wait(r1[i].at[h], qd.at[i, h])
            loc[i][h] = loc[i][h] + r1[i][h]
    def stage2(zz):
        for j, (yy, xx) in enumerate(((1-y, 1-x), (y3, x3))):
            h = half(zz, yy, xx)
            add1(h)
            for i in range(n):
                rc(loc[i].at[h], r2[i].at[2*zz+j], s2.at[i, 2*zz+j], q2.at[i, 2*zz+j], p3).start()
        for yy, xx in ((y2, x2), (y, x)): add1(half(zz, yy, xx))
    each(stage2)
    def stage3(zz):
        for j, (yy, xx) in enumerate(((y2, x2), (y, x))):
            h = half(zz, yy, xx)
            for i in range(n):
                wait(r2[i].at[2*zz+j], q2.at[i, 2*zz+j])
                loc[i][h] = loc[i][h] + r2[i][2*zz+j]
                if j == 0:
                    rc(loc[i].at[h], r3[i].at[zz], s3.at[i, zz], q3.at[i, zz], p2).start()
    def stage4(zz, d, dev, has):
        h = half(zz, y, x)
        for i in range(n):
            wait(r3[i].at[zz], q3.at[i, zz])
            @pl.when(has)
            def _():
                wait(rz[i].at[d, zz], qz.at[i, d, zz])
                loc[i][h] = loc[i][h] + r3[i][zz] + rz[i][d, zz]
            @pl.when(jnp.logical_not(has))
            def _(): loc[i][h] = loc[i][h] + r3[i][zz]
            rc(loc[i].at[h], rz[i].at[d, zz], sz.at[i, d, zz], qz.at[i, d, zz], dev).start()
    def body(t0, _):
        t = Z-1-t0
        @pl.when(jnp.logical_and(t >= 0, z >= t))
        def _(): stage3(z-t)
        @pl.when(jnp.logical_and(t > 0, z+t < Z))
        def _(): stage3(z+t)
        u = t + 1
        @pl.when(z + u < Z)
        def _(): stage4(z+u, 0, up, z > 0)
        @pl.when(z >= u)
        def _(): stage4(z-u, 1, dn, z < Z-1)
        return 0
    lax.fori_loop(0, Z, body, 0)
    h = half(z, y, x)
    for i in range(n): wait(r3[i].at[z], q3.at[i, z])
    @pl.when(z > 0)
    def _():
        for i in range(n): wait(rz[i].at[0, z], qz.at[i, 0, z])
    @pl.when(z < Z-1)
    def _():
        for i in range(n): wait(rz[i].at[1, z], qz.at[i, 1, z])
    for out, (i, offset, width) in zip(outs, layout):
        cols = slice(offset, offset+width)
        out[...] = loc[i][h, :, cols].astype(jnp.float32) + r3[i][z, :, cols].astype(jnp.float32)
        @pl.when(z > 0)
        def _(): out[...] += rz[i][0, z, :, cols].astype(jnp.float32)
        @pl.when(z < Z-1)
        def _(): out[...] += rz[i][1, z, :, cols].astype(jnp.float32)
    def fin(h, _):
        for i in range(n): wait(r1[i].at[h], sd.at[i, h])
        return 0
    lax.fori_loop(0, NDP*KV//2, fin, 0)
    def fin2(zz, _):
        for i in range(n):
            wait(r3[i].at[zz], s3.at[i, zz])
            wait(r2[i].at[2*zz], s2.at[i, 2*zz]); wait(r2[i].at[2*zz+1], s2.at[i, 2*zz+1])
            @pl.when(zz > z)
            def _(): wait(rz[i].at[0, zz], sz.at[i, 0, zz])
            @pl.when(zz < z)
            def _(): wait(rz[i].at[1, zz], sz.at[i, 1, zz])
        return 0
    lax.fori_loop(0, Z, fin2, 0)

def reduce_scatter(grads, down, NDP, KV, cid):
    ND = NDP*KV; Z = NDP//2
    split = [g.reshape(ND, g.shape[0]//ND, g.shape[1]) for g in (*grads, down)]
    layout, offset = [], 0
    for g in split[:-1]:
        layout.append((0, offset, g.shape[2]))
        offset += g.shape[2]
    layout.append((1, 0, down.shape[1]))
    D = pltpu.SemaphoreType.DMA
    shapes = [(split[0].shape[1], offset), split[-1].shape[1:]]
    def bufs(*lead): return [pltpu.VMEM(lead + s, jnp.bfloat16) for s in shapes]
    n = 2
    return pl.pallas_call(
        functools.partial(rs_kernel, NDP, KV, layout),
        out_shape=[jax.ShapeDtypeStruct(a.shape[1:], jnp.float32) for a in split],
        in_specs=[pl.BlockSpec(memory_space=pl.ANY)]*len(split),
        out_specs=[pl.BlockSpec(memory_space=pltpu.VMEM)]*len(split),
        scratch_shapes=bufs(ND//2)+bufs(ND//2)+bufs(2*Z)+bufs(Z)+bufs(2, Z)
            +[D((n, ND//2))]*3+[D((n, 2*Z))]*2+[D((n, Z))]*2+[D((n, 2, Z))]*2,
        compiler_params=pltpu.CompilerParams(collective_id=cid, has_side_effects=True, vmem_limit_bytes=60<<20),
        name="scatter_gradients",
    )(*split)


D = 768
FF = 3072
HEADS = 12
HD = 64
SEQ = 64
QUAD = 4 * HD
EPS = 1e-05
NEG = -1e30
GELU_C = 0.7978845608028654
GELU_A = 0.044715
SCALE = 0.125
BF = jnp.bfloat16
F32 = jnp.float32
VM = pl.BlockSpec(memory_space=pltpu.VMEM)
ANY = pl.BlockSpec(memory_space=pl.ANY)
DMA = pltpu.SemaphoreType.DMA


def nn(a, b):
    return lax.dot_general(a, b, (((1,), (0,)), ((), ())), preferred_element_type=F32)


def nt(a, b):
    return lax.dot_general(a, b, (((1,), (1,)), ((), ())), preferred_element_type=F32)


def tn(a, b):
    return lax.dot_general(a, b, (((0,), (0,)), ((), ())), preferred_element_type=F32)


def unit_of(values):
    centre = values - jnp.mean(values, -1, keepdims=True)
    scaled = lax.rsqrt(jnp.mean(centre * centre, -1, keepdims=True) + EPS)
    return centre * scaled, scaled


def norm_backward(upstream, unit, scaled, gain):
    through = upstream * gain
    return scaled * (
        through - jnp.mean(through, -1, keepdims=True) - unit * jnp.mean(through * unit, -1, keepdims=True)
    )


def head_masks(width):
    lane = lax.broadcasted_iota(jnp.int32, (1, width), 1) // HD
    return [(lane == head).astype(F32).astype(BF) for head in range(width // HD)]


def stacked(values, masks):
    return jnp.concatenate([values * mask for mask in masks], 0)


def own_blocks(values):
    lane = lax.broadcasted_iota(jnp.int32, (HD, QUAD), 1) // HD
    total = values[:HD]
    for head in range(1, 4):
        total = jnp.where(lane == head, values[head * HD : (head + 1) * HD], total)
    return total


def load(source, target, sem):
    return pltpu.make_async_copy(source, target, sem)


def call(kernel, name, outs, ins, specs, scratch, flops, out_specs=None, cid=None, limit=56 << 20):
    params = dict(vmem_limit_bytes=limit)
    if cid is not None:
        params.update(collective_id=cid, has_side_effects=True)
    size = lambda a: a.size * a.dtype.itemsize
    return pl.pallas_call(
        kernel,
        out_shape=outs,
        in_specs=specs,
        out_specs=out_specs or [VM] * len(outs),
        scratch_shapes=scratch,
        compiler_params=pltpu.CompilerParams(**params),
        cost_estimate=pl.CostEstimate(flops=int(flops), transcendentals=0, bytes_accessed=sum(map(size, ins)) + sum(map(size, outs))),
        name=name,
    )(*ins)


def arr(shape, dtype=BF):
    return jax.ShapeDtypeStruct(shape, dtype)


def text_forward_kernel(text, packed, h1, q1, k1, v1, p1, c1, x2, h2, q2, gains, w, gw, sem):
    weights = [load(packed.at[:, pl.ds(j * D, D)], w.at[j], sem.at[j]) for j in range(5)]
    gcopy = load(packed.at[:, pl.ds(8 * D + FF, 128)], gw, sem.at[5])
    gcopy.start()
    for copy in weights:
        copy.start()
    x = text[...].astype(F32)
    unit, _ = unit_of(x)
    gcopy.wait()
    gains[...] = gw[...].astype(F32).T[:8]
    h1[...] = (unit * gains[0:1]).astype(BF)
    for j, ref in enumerate((q1, k1, v1)):
        weights[j].wait()
        ref[...] = nn(h1[...], w[j]).astype(BF)
    rows = text.shape[0]
    first = lax.broadcasted_iota(jnp.int32, (rows, rows), 0)
    second = lax.broadcasted_iota(jnp.int32, (rows, rows), 1)
    allowed = jnp.logical_and(first >= second, first // SEQ == second // SEQ)
    masks = head_masks(128)
    for pair in range(HEADS // 2):
        lanes = slice(pair * 128, (pair + 1) * 128)
        total = None
        for j, mask in enumerate(masks):
            scores = nt(q1[:, lanes] * mask, k1[:, lanes]) * SCALE
            scores = jnp.where(allowed, scores, NEG)
            powers = jnp.exp(scores - jnp.max(scores, -1, keepdims=True))
            probs = (powers / jnp.sum(powers, -1, keepdims=True)).astype(BF)
            p1[2 * pair + j] = probs
            part = nn(probs, v1[:, lanes] * mask)
            total = part if total is None else total + part
        c1[:, lanes] = total.astype(BF)
    weights[3].wait()
    second_res = x + nn(c1[...], w[3])
    x2[...] = second_res
    unit, _ = unit_of(second_res)
    h2[...] = (unit * gains[1:2]).astype(BF)
    weights[4].wait()
    q2[...] = nn(h2[...], w[4]).astype(BF)


def text_forward(text, packed):
    rows = text.shape[0]
    low = arr((rows, D))
    return call(
        text_forward_kernel, "text_forward",
        [low, low, low, low, arr((HEADS, rows, rows)), low, arr((rows, D), F32), low, low, arr((8, D), F32)],
        [text, packed], [VM, ANY],
        [pltpu.VMEM((5, D, D), BF), pltpu.VMEM((D, 128), BF), DMA((6,))], 10 * rows * D * D)


def group_place():
    di, ki = lax.axis_index("dp"), lax.axis_index("kv")
    x, c = ki // 2, ki % 2
    return di, ki, x, c


def group_barrier(di, ki, x, c):
    bar = pltpu.get_barrier_semaphore()
    for other in (2 * x + 1 - c, 2 * (1 - x) + c, 2 * (1 - x) + 1 - c):
        pl.semaphore_signal(bar, 1, device_id=(di, other), device_id_type=MESH)
    pl.semaphore_wait(bar, 3)


def remote(src, dst, send, recv, device):
    return pltpu.make_async_remote_copy(
        src_ref=src, dst_ref=dst, send_sem=send, recv_sem=recv, device_id=device, device_id_type=MESH)


def cross_forward_kernel(q2, image, bias, packed, c2, lse, keys, vals, e, stats, qall, w, obuf, ro, rst, wsem, ssem, rsem):
    di, ki, x, c = group_place()
    caps = bias.shape[0]
    own_caps = caps // 4
    tokens = bias.shape[1]
    core, over, diag = 2 * x + 1 - c, 2 * (1 - x) + c, 2 * (1 - x) + 1 - c
    weights = [load(packed.at[:, pl.ds((5 + j) * D, D)], w.at[j], wsem.at[j]) for j in range(2)]
    for copy in weights:
        copy.start()
    own_copy = load(q2, qall.at[ki], wsem.at[2])
    own_copy.start()
    group_barrier(di, ki, x, c)
    to_core = remote(q2, qall.at[ki], ssem.at[0], rsem.at[ki], (di, core))
    to_over = remote(q2, qall.at[ki], ssem.at[1], rsem.at[ki], (di, over))
    to_over.start()
    to_core.start()
    weights[0].wait()

    def project(j, ref, i):
        rows = pl.ds(pl.multiple_of(i * tokens, 16), tokens)
        ref[rows, :] = nn(image[rows, :], w[j]).astype(BF)

    lax.fori_loop(0, caps, lambda i, _: (project(0, keys, i), 0)[1], 0)
    load(qall.at[over], qall.at[over], rsem.at[over]).wait()
    relay = remote(qall.at[over], qall.at[over], ssem.at[2], rsem.at[over], (di, core))
    relay.start()
    weights[1].wait()
    lax.fori_loop(0, caps, lambda i, _: (project(1, vals, i), 0)[1], 0)
    load(qall.at[core], qall.at[core], rsem.at[core]).wait()
    load(qall.at[diag], qall.at[diag], rsem.at[diag]).wait()
    own_copy.wait()
    masks = head_masks(QUAD)

    def owner_of(step):
        return 2 * ((x + 1 + step // 2) % 2) + (c + 1 + step % 2) % 2

    def attend(i, _):
        owner, local = owner_of(i // own_caps), i % own_caps
        cap = owner * own_caps + local
        rows = pl.ds(pl.multiple_of(cap * tokens, 16), tokens)
        queries = pl.ds(pl.multiple_of(local * SEQ, 16), SEQ)
        shift = bias[cap]
        shift = jnp.concatenate([shift, shift], 1)
        for g in range(3):
            lanes = slice(g * QUAD, (g + 1) * QUAD)
            scores = nt(keys[rows, lanes], stacked(qall[owner, queries, lanes], masks)) * SCALE
            scores = jnp.where(shift == 0.0, scores, NEG)
            top = jnp.max(scores, 0, keepdims=True)
            powers = jnp.where(shift == 0.0, jnp.exp(scores - top), 0.0)
            low = powers.astype(BF)
            e[pl.ds(pl.multiple_of((cap * 3 + g) * tokens, 16), tokens), :] = low
            stats[owner, pl.ds(3 * local + g, 1), :] = top
            stats[owner, pl.ds(16 + 3 * local + g, 1), :] = jnp.sum(powers, 0, keepdims=True)
            obuf[owner, queries, lanes] = own_blocks(tn(low, vals[rows, lanes])).astype(BF)

        @pl.when(jnp.logical_and(local == own_caps - 1, owner != ki))
        def _():
            remote(obuf.at[owner], ro.at[ki], ssem.at[3 + owner], rsem.at[4 + ki], (di, owner)).start()
            remote(stats.at[owner], rst.at[ki], ssem.at[7 + owner], rsem.at[8 + ki], (di, owner)).start()

        return 0

    lax.fori_loop(0, caps, attend, 0)
    ro[ki] = obuf[ki]
    rst[ki] = stats[ki]
    for other in (core, over, diag):
        load(ro.at[other], ro.at[other], rsem.at[4 + other]).wait()
        load(rst.at[other], rst.at[other], rsem.at[8 + other]).wait()
    lane = lax.broadcasted_iota(jnp.int32, (HD, QUAD), 1) // HD

    def combine(local, _):
        queries = pl.ds(pl.multiple_of(local * SEQ, 16), SEQ)
        for g in range(3):
            row = pl.ds(3 * local + g, 1)
            row_sum = pl.ds(16 + 3 * local + g, 1)
            tops = [rst[k, row, :] for k in range(4)]
            top = jnp.maximum(jnp.maximum(tops[0], tops[1]), jnp.maximum(tops[2], tops[3]))
            parts = [jnp.exp(t - top) for t in tops]
            total = sum(part * rst[k, row_sum, :] for k, part in enumerate(parts))
            lse[row, :] = top + jnp.log(total)
            table = jnp.concatenate([part / total for part in parts] * 2, 0).T
            mixed = 0.0
            for k in range(4):
                column = table[:, k : k + 1]
                weight = column[:HD] * jnp.ones((HD, QUAD), F32)
                for head in range(1, 4):
                    weight = jnp.where(lane == head, column[head * HD : (head + 1) * HD], weight)
                mixed = mixed + weight * ro[k, queries, g * QUAD : (g + 1) * QUAD].astype(F32)
            c2[queries, g * QUAD : (g + 1) * QUAD] = mixed
        return 0

    lax.fori_loop(0, own_caps, combine, 0)
    to_core.wait_send()
    to_over.wait_send()
    relay.wait_send()
    for other in (core, over, diag):
        load(obuf.at[other], obuf.at[other], ssem.at[3 + other]).wait()
        load(stats.at[other], stats.at[other], ssem.at[7 + other]).wait()


def cross_forward(q2, image, bias, packed, cid):
    rows, caps, tokens = q2.shape[0], bias.shape[0], bias.shape[1]
    return call(
        cross_forward_kernel, "cross_forward",
        [arr((rows, D), F32), arr((16, QUAD), F32), arr((caps * tokens, D)), arr((caps * tokens, D)),
         arr((caps * 3 * tokens, QUAD)), arr((4, 32, QUAD), F32), arr((4, rows, D))],
        [q2, image, bias, packed], [VM, VM, VM, ANY],
        [pltpu.VMEM((2, D, D), BF), pltpu.VMEM((4, rows, D), BF), pltpu.VMEM((4, rows, D), BF),
         pltpu.VMEM((4, 32, QUAD), F32), DMA((3,)), DMA((11,)), DMA((12,))],
        4 * caps * tokens * D * D, cid=cid)


def cross_backward_kernel(dc2, c2, lse, stats, qall, keys, vals, e, image, dq2, dk, dv, wk, wv,
                          dall, sall, qbuf, rq, csem, ssem, rsem):
    di, ki, x, c = group_place()
    rows_all = keys.shape[0]
    caps = 4 * (dc2.shape[0] // SEQ)
    own_caps = caps // 4
    tokens = rows_all // caps
    core, over, diag = 2 * x + 1 - c, 2 * (1 - x) + c, 2 * (1 - x) + 1 - c
    masks = head_masks(QUAD)
    sall[ki, 0:16, :] = lse[...]

    def dots(local, _):
        queries = pl.ds(pl.multiple_of(local * SEQ, 16), SEQ)
        for g in range(3):
            lanes = slice(g * QUAD, (g + 1) * QUAD)
            product = dc2[queries, lanes].astype(F32) * c2[queries, lanes]
            product = jnp.concatenate([product * mask.astype(F32) for mask in masks], 0)
            sums = lax.dot_general(
                jnp.ones((8, QUAD), F32), product, (((1,), (1,)), ((), ())),
                preferred_element_type=F32, precision=lax.Precision.HIGHEST)
            sall[ki, pl.ds(16 + 3 * local + g, 1), :] = sums[0:1]
        return 0

    own_copy = load(dc2, dall.at[ki], csem)
    own_copy.start()
    group_barrier(di, ki, x, c)
    to_over = remote(dc2, dall.at[ki], ssem.at[1], rsem.at[ki], (di, over))
    to_core = remote(dc2, dall.at[ki], ssem.at[0], rsem.at[ki], (di, core))
    to_over.start()
    to_core.start()
    lax.fori_loop(0, own_caps, dots, 0)
    small = [remote(sall.at[ki], sall.at[ki], ssem.at[2 + j], rsem.at[4 + ki], (di, other))
             for j, other in enumerate((core, over, diag))]
    for copy in small:
        copy.start()
    own_copy.wait()
    relay = remote(dall.at[over], dall.at[over], ssem.at[5], rsem.at[over], (di, core))

    def attend(i, _):
        step, local = i // own_caps, i % own_caps
        owner = 2 * ((x + step // 2) % 2) + (c + step % 2) % 2

        @pl.when(i == own_caps)
        def _():
            load(dall.at[core], dall.at[core], rsem.at[core]).wait()
            load(sall.at[core], sall.at[core], rsem.at[4 + core]).wait()

        @pl.when(i == 2 * own_caps - 1)
        def _():
            load(dall.at[over], dall.at[over], rsem.at[over]).wait()
            relay.start()

        @pl.when(i == 2 * own_caps)
        def _():
            load(sall.at[over], sall.at[over], rsem.at[4 + over]).wait()

        @pl.when(i == 3 * own_caps)
        def _():
            load(dall.at[diag], dall.at[diag], rsem.at[diag]).wait()
            load(sall.at[diag], sall.at[diag], rsem.at[4 + diag]).wait()

        cap = owner * own_caps + local
        rows = pl.ds(pl.multiple_of(cap * tokens, 16), tokens)
        queries = pl.ds(pl.multiple_of(local * SEQ, 16), SEQ)
        for g in range(3):
            lanes = slice(g * QUAD, (g + 1) * QUAD)
            factor = jnp.exp(stats[owner, pl.ds(3 * local + g, 1), :] - sall[owner, pl.ds(3 * local + g, 1), :])
            dots_row = sall[owner, pl.ds(16 + 3 * local + g, 1), :]
            probs = e[pl.ds(pl.multiple_of((cap * 3 + g) * tokens, 16), tokens), :].astype(F32) * factor
            upstream = stacked(dall[owner, queries, lanes], masks)
            queried = stacked(qall[owner, queries, lanes], masks)
            grad = nt(vals[rows, lanes], upstream)
            grad = (probs * (grad - dots_row)).astype(BF)
            dv[rows, lanes] = nn(probs.astype(BF), upstream).astype(BF)
            dk[rows, lanes] = (nn(grad, queried) * SCALE).astype(BF)
            qbuf[owner, queries, lanes] = (own_blocks(tn(grad, keys[rows, lanes])) * SCALE).astype(BF)

        @pl.when(jnp.logical_and(local == own_caps - 1, owner != ki))
        def _():
            remote(qbuf.at[owner], rq.at[ki], ssem.at[6 + owner], rsem.at[8 + ki], (di, owner)).start()

        return 0

    lax.fori_loop(0, caps, attend, 0)

    def weight(j, _):
        cols = pl.ds(pl.multiple_of(j * 256, 256), 256)
        flipped = image[:, cols].T
        wk[cols, :] = nn(flipped, dk[...]).astype(BF)
        wv[cols, :] = nn(flipped, dv[...]).astype(BF)
        return 0

    lax.fori_loop(0, D // 256, weight, 0)
    rq[ki] = qbuf[ki]
    for other in (core, over, diag):
        load(rq.at[other], rq.at[other], rsem.at[8 + other]).wait()
    dq2[...] = (rq[0].astype(F32) + rq[1].astype(F32) + rq[2].astype(F32) + rq[3].astype(F32)).astype(BF)
    to_core.wait_send()
    to_over.wait_send()
    relay.wait_send()
    for copy in small:
        copy.wait_send()
    for other in (core, over, diag):
        load(qbuf.at[other], qbuf.at[other], ssem.at[6 + other]).wait()


def cross_backward(dc2, c2, lse, stats, qall, keys, vals, e, image, cid):
    rows = dc2.shape[0]
    ins = [dc2, c2, lse, stats, qall, keys, vals, e, image]
    return call(
        cross_backward_kernel, "cross_backward",
        [arr((rows, D)), arr(keys.shape), arr(keys.shape), arr((D, D)), arr((D, D))],
        ins, [VM] * len(ins),
        [pltpu.VMEM((4, rows, D), BF), pltpu.VMEM((4, 32, QUAD), F32), pltpu.VMEM((4, rows, D), BF),
         pltpu.VMEM((4, rows, D), BF), DMA, DMA((10,)), DMA((12,))],
        4 * keys.shape[0] * D * D, cid=cid)


def mlp_kernel(c2, x2, grad, gains, packed, down, out, dx3, dc2, dup, ddown, dco, ng, wu, wd, wc, dh, acc, ht, sem):
    wcopy = load(packed.at[:, pl.ds(7 * D, D)], wc, sem.at[8])
    wcopy.start()
    ups = [load(packed.at[:, pl.ds((8 + j) * D, D)], wu.at[j], sem.at[j]) for j in range(4)]
    downs = [load(down.at[pl.ds(j * D, D), :], wd.at[j], sem.at[4 + j]) for j in range(4)]
    for j in range(4):
        ups[j].start()
        downs[j].start()
    low = c2[...].astype(BF)
    wcopy.wait()
    third = x2[...] + nn(low, wc[...])
    unit, scaled = unit_of(third)
    gain = gains[2:3]
    h3 = (unit * gain).astype(BF)
    ht[...] = h3.T
    g = grad[...]
    acc[...] = third
    for j in range(4):
        ups[j].wait()
        downs[j].wait()
        u = nn(h3, wu[j])
        square = u * u
        tanh_part = jnp.tanh(GELU_C * (u + GELU_A * square * u))
        active = (0.5 * u * (1.0 + tanh_part)).astype(BF)
        slope = 0.5 * (1.0 + tanh_part) + 0.5 * u * (1.0 - tanh_part * tanh_part) * GELU_C * (1.0 + 3.0 * GELU_A * square)
        acc[...] += nn(active, wd[j])
        du = (nt(g, wd[j]) * slope).astype(BF)
        part = nt(du, wu[j])
        dh[...] = part if j == 0 else dh[...] + part
        ddown[pl.ds(j * D, D), :] = tn(active, g).astype(BF)
        dup[:, pl.ds(j * D, D)] = nn(ht[...], du).astype(BF)
    out[...] = acc[...].astype(BF)
    upstream = dh[...]
    ng[...] = jnp.broadcast_to(jnp.sum(upstream * unit, 0, keepdims=True), ng.shape)
    total = g.astype(F32) + norm_backward(upstream, unit, scaled, gain)
    dx3[...] = total
    branch = total.astype(BF)
    dc2[...] = nt(branch, wc[...]).astype(BF)
    dco[...] = tn(low, branch).astype(BF)


def mlp(c2, x2, grad, gains, packed, down):
    rows = c2.shape[0]
    return call(
        mlp_kernel, "feed_forward",
        [arr((rows, D)), arr((rows, D), F32), arr((rows, D)), arr((D, FF)), arr((FF, D)), arr((D, D)), arr((8, D), F32)],
        [c2, x2, grad, gains, packed, down], [VM] * 4 + [ANY] * 2,
        [pltpu.VMEM((4, D, D), BF), pltpu.VMEM((4, D, D), BF), pltpu.VMEM((D, D), BF), pltpu.VMEM((rows, D), F32),
         pltpu.VMEM((rows, D), F32), pltpu.VMEM((D, rows), BF), DMA((9,))], 12 * rows * D * FF)


def image_grad_kernel(dk, dv, packed, out, w, sem):
    @pl.when(pl.program_id(0) == 0)
    def _():
        copies = [load(packed.at[:, pl.ds((5 + j) * D, D)], w.at[j], sem.at[j]) for j in range(2)]
        for copy in copies:
            copy.start()
        for copy in copies:
            copy.wait()

    out[...] = nt(dk[...], w[0]) + nt(dv[...], w[1])


def image_gradient(dk, dv, packed):
    rows = dk.shape[0]
    block = rows // 6
    spec = pl.BlockSpec((block, D), lambda i: (i, 0))
    return pl.pallas_call(
        image_grad_kernel,
        out_shape=arr((rows, D), F32),
        grid=(rows // block,),
        in_specs=[spec, spec, ANY],
        out_specs=spec,
        scratch_shapes=[pltpu.VMEM((2, D, D), BF), DMA((2,))],
        compiler_params=pltpu.CompilerParams(vmem_limit_bytes=20 << 20),
        cost_estimate=pl.CostEstimate(flops=4 * rows * D * D, transcendentals=0, bytes_accessed=8 * rows * D),
        name="image_gradient",
    )(dk, dv, packed)


def text_backward_kernel(dq2, dx3, text, x2, h1, h2, c1, q1, k1, v1, p1, gains, ng3, packed,
                         text_grad, wq, wk, wv, wo, wcq, ngs, w, dq, dk, dv, rows_t, sem):
    weights = [load(packed.at[:, pl.ds(j * D, D)], w.at[j], sem.at[j]) for j in range(5)]
    for j in (4, 3, 0, 1, 2):
        weights[j].start()
    unit, scaled = unit_of(x2[...])
    weights[4].wait()
    upstream = nt(dq2[...], w[4])
    ngs_two = jnp.sum(upstream * unit, 0, keepdims=True)
    grad_two = dx3[...] + norm_backward(upstream, unit, scaled, gains[1:2])
    wcq[...] = tn(h2[...], dq2[...]).astype(BF)
    branch = grad_two.astype(BF)
    weights[3].wait()
    dc1 = nt(branch, w[3]).astype(BF)
    wo[...] = tn(c1[...], branch).astype(BF)
    masks = head_masks(128)
    for pair in range(HEADS // 2):
        lanes = slice(pair * 128, (pair + 1) * 128)
        sums = [None] * 3
        for j, mask in enumerate(masks):
            low = p1[2 * pair + j]
            probs = low.astype(F32)
            above = dc1[:, lanes] * mask
            grad = nt(above, v1[:, lanes])
            grad = (probs * (grad - jnp.sum(probs * grad, -1, keepdims=True))).astype(BF)
            parts = [nn(grad, k1[:, lanes] * mask), tn(grad, q1[:, lanes] * mask), tn(low, above)]
            sums = parts if j == 0 else [a + b for a, b in zip(sums, parts)]
        dq[:, lanes] = (sums[0] * SCALE).astype(BF)
        dk[:, lanes] = (sums[1] * SCALE).astype(BF)
        dv[:, lanes] = sums[2].astype(BF)
    upstream = None
    flipped = h1[...].T
    for j, (ref, out) in enumerate(((dq, wq), (dk, wk), (dv, wv))):
        weights[j].wait()
        part = nt(ref[...], w[j])
        upstream = part if j == 0 else upstream + part
        out[...] = nn(flipped, ref[...]).astype(BF)
    unit, scaled = unit_of(text[...].astype(F32))
    text_grad[...] = grad_two + norm_backward(upstream, unit, scaled, gains[0:1])
    rows_t[...] = jnp.zeros_like(rows_t)
    rows_t[0:1] = jnp.sum(upstream * unit, 0, keepdims=True)
    rows_t[1:2] = ngs_two
    rows_t[2:3] = ng3[0:1]
    ngs[...] = rows_t[...].T.astype(BF)


def text_backward(dq2, dx3, text, x2, h1, h2, c1, q1, k1, v1, p1, gains, ng3, packed):
    rows = text.shape[0]
    ins = [dq2, dx3, text, x2, h1, h2, c1, q1, k1, v1, p1, gains, ng3, packed]
    return call(
        text_backward_kernel, "text_backward",
        [arr((rows, D), F32)] + [arr((D, D))] * 5 + [arr((D, 128))],
        ins, [VM] * 13 + [ANY],
        [pltpu.VMEM((5, D, D), BF)] + [pltpu.VMEM((rows, D), BF)] * 3 + [pltpu.VMEM((128, D), F32), DMA((5,))],
        20 * rows * D * D)


def per_device(
    text_tokens, image_tokens, image_lengths, patch_mask, self_query, self_key, self_value, self_out, cross_query,
    cross_key, cross_value, cross_out, mlp_up, mlp_down, norm_self, norm_cross, norm_mlp, out_grad,
):
    ndp, nkv = lax.axis_size("dp"), lax.axis_size("kv")
    caps, tokens = image_tokens.shape[0], image_tokens.shape[1]
    gain_block = jnp.pad(jnp.stack([norm_self, norm_cross, norm_mlp], 1), ((0, 0), (0, 125)))
    parts = [self_query, self_key, self_value, self_out, cross_query, cross_key, cross_value, cross_out, mlp_up, gain_block]
    packed, down = all_gather(parts, mlp_down, ndp, nkv, 1)
    packed = packed.reshape(D, -1)
    down = down.reshape(FF, D)
    position = lax.broadcasted_iota(jnp.int32, (caps, tokens), 1) + lax.axis_index("kv") * tokens
    usable = jnp.logical_and(position < image_lengths[:, None], patch_mask == 1)
    bias = jnp.broadcast_to(jnp.where(usable, 0.0, 1.0).astype(F32)[:, :, None], (caps, tokens, 128))
    image = image_tokens.reshape(caps * tokens, D)
    h1, q1, k1, v1, p1, c1, x2, h2, q2, gains = text_forward(text_tokens, packed)
    c2, lse, keys, vals, e, stats, qall = cross_forward(q2, image, bias, packed, 2)
    layer_out, dx3, dc2, d_up, d_down, d_co, ng3 = mlp(c2, x2, out_grad, gains, packed, down)
    dq2, dk2, dv2, d_ck, d_cv = cross_backward(dc2, c2, lse, stats, qall, keys, vals, e, image, 3)
    image_grad = image_gradient(dk2, dv2, packed).reshape(caps, tokens, D)
    text_grad, d_q, d_k, d_v, d_o, d_cq, ngs = text_backward(
        dq2, dx3, text_tokens, x2, h1, h2, c1, q1, k1, v1, p1, gains, ng3, packed)
    parts = reduce_scatter([d_q, d_k, d_v, d_o, d_cq, d_ck, d_cv, d_co, d_up, ngs], d_down, ndp, nkv, 4)
    return (layer_out, text_grad, image_grad, *parts[:9], parts[10], parts[9][:, 0], parts[9][:, 1], parts[9][:, 2])


def solution(mesh):
    in_specs = (
        P(("dp", "kv"), None),
        P("dp", "kv", None),
        P("dp"),
        P("dp", "kv"),
        P(("dp", "kv"), None),
        P(("dp", "kv"), None),
        P(("dp", "kv"), None),
        P(("dp", "kv"), None),
        P(("dp", "kv"), None),
        P(("dp", "kv"), None),
        P(("dp", "kv"), None),
        P(("dp", "kv"), None),
        P(("dp", "kv"), None),
        P(("dp", "kv"), None),
        P(("dp", "kv")),
        P(("dp", "kv")),
        P(("dp", "kv")),
        P(("dp", "kv"), None),
    )
    out_specs = (
        P(("dp", "kv"), None),
        P(("dp", "kv"), None),
        P("dp", "kv", None),
        P(("dp", "kv"), None),
        P(("dp", "kv"), None),
        P(("dp", "kv"), None),
        P(("dp", "kv"), None),
        P(("dp", "kv"), None),
        P(("dp", "kv"), None),
        P(("dp", "kv"), None),
        P(("dp", "kv"), None),
        P(("dp", "kv"), None),
        P(("dp", "kv"), None),
        P(("dp", "kv")),
        P(("dp", "kv")),
        P(("dp", "kv")),
    )
    return jax.shard_map(
        per_device, mesh=mesh, in_specs=in_specs, out_specs=out_specs, check_vma=False
    )
```

```python
import functools
import types

import jax
import jax.numpy as jnp
from jax import lax
from jax.experimental import pallas as pl
from jax.experimental.pallas import tpu as pltpu
from jax.sharding import PartitionSpec as P

MESH = pl.DeviceIdType.MESH
def place(NDP, KV):
    di, ki = lax.axis_index("dp"), lax.axis_index("kv")
    Y = 2
    z, y, x, c = di // Y, di % Y, ki // 2, ki % 2
    y2, x2 = y + c*(1-2*y), x + (1-c)*(1-2*x)
    y3, x3 = y + (1-c)*(1-2*y), x + c*(1-2*x)
    return types.SimpleNamespace(
        di=di, ki=ki, z=z, y=y, x=x, c=c, Y=Y, Z=NDP//Y, KV=KV, y2=y2, x2=x2, y3=y3, x3=x3,
        up=(di + Y, ki), dn=(di - Y, ki), p2=(z*Y+y2, x2*2+c), p3=(z*Y+y3, x3*2+c), pd=(di, ki + 1 - 2*c),
        diag=(di, 2*(1-x) + 1 - c))

def enter(at, group=False):
    bar = pltpu.get_barrier_semaphore()
    @pl.when(at.z < at.Z-1)
    def _(): pl.semaphore_signal(bar, 1, device_id=at.up, device_id_type=MESH)
    @pl.when(at.z > 0)
    def _(): pl.semaphore_signal(bar, 1, device_id=at.dn, device_id_type=MESH)
    peers = (at.p2, at.p3, at.pd) + ((at.diag,) if group else ())
    for p in peers: pl.semaphore_signal(bar, 1, device_id=p, device_id_type=MESH)
    pl.semaphore_wait(bar, len(peers) + jnp.where(at.z < at.Z-1, 1, 0) + jnp.where(at.z > 0, 1, 0))

class Gather:
    def __init__(self, at, ins, outs, sems):
        self.at, self.ins, self.outs = at, ins, outs
        self.recv, self.sz, self.s2, self.s3, self.sd, self.sl = sems
        self.n = len(ins)
        self.own = self.slot(at.z, at.y, at.x)

    @staticmethod
    def sems(n, ND):
        Z = ND // 8
        D = pltpu.SemaphoreType.DMA
        return [D((n, ND)), D((n, 2, Z)), D((n, Z)), D((n, 2*Z)), D((n, ND//2)), D((n,))]

    def slot(self, zz, yy, xx):
        return (zz*self.at.Y+yy)*self.at.KV + xx*2 + self.at.c

    def send(self, s, sems, dev, own=False):
        for i in range(self.n):
            pltpu.make_async_remote_copy(
                src_ref=self.ins[i] if own else self.outs[i].at[s], dst_ref=self.outs[i].at[s], send_sem=sems(i),
                recv_sem=self.recv.at[i, s], device_id=dev, device_id_type=MESH).start()

    def arrive(self, s):
        for i in range(self.n):
            pltpu.make_async_copy(self.outs[i].at[s], self.outs[i].at[s], self.recv.at[i, s]).wait()

    def spread(self, zz, own=False):
        s = self.slot(zz, self.at.y, self.at.x)
        self.send(s, lambda i: self.s2.at[i, zz], self.at.p2, own)
        self.send(s, lambda i: self.s3.at[i, zz], self.at.p3, own)
        self.send(s, lambda i: self.sd.at[i, s//2], self.at.pd, own)

    def start(self):
        at, own = self.at, self.own
        @pl.when(at.z < at.Z-1)
        def _(): self.send(own, lambda i: self.sz.at[i, 0, at.z], at.up, True)
        @pl.when(at.z > 0)
        def _(): self.send(own, lambda i: self.sz.at[i, 1, at.z], at.dn, True)
        self.spread(at.z, True)
        for i in range(self.n):
            pltpu.make_async_copy(self.ins[i], self.outs[i].at[own], self.sl.at[i]).start()

    def second(self, zz):
        at = self.at
        s = self.slot(zz, at.y2, at.x2)
        self.arrive(s)
        self.send(s, lambda i: self.s3.at[i, at.Z+zz], at.p3)
        self.send(s, lambda i: self.sd.at[i, s//2], at.pd)

    def near(self, t):
        at = self.at
        @pl.when(at.z >= t)
        def _():
            s = self.slot(at.z-t, at.y, at.x); self.arrive(s)
            @pl.when(at.z < at.Z-1)
            def _(): self.send(s, lambda i: self.sz.at[i, 0, at.z-t], at.up)
            self.spread(at.z-t)
        @pl.when(at.z + t < at.Z)
        def _():
            s = self.slot(at.z+t, at.y, at.x); self.arrive(s)
            @pl.when(at.z > 0)
            def _(): self.send(s, lambda i: self.sz.at[i, 1, at.z+t], at.dn)
            self.spread(at.z+t)
        @pl.when(at.z >= t-1)
        def _(): self.second(at.z-t+1)
        @pl.when(jnp.logical_and(t > 1, at.z+t-1 < at.Z))
        def _(): self.second(at.z+t-1)

    def third(self, zz):
        at = self.at
        for yy, xx in ((at.y3, at.x3), (1-at.y, 1-at.x)):
            s = self.slot(zz, yy, xx)
            self.arrive(s)
            self.send(s, lambda i: self.sd.at[i, s//2], at.pd)

    def far(self, t):
        at = self.at
        @pl.when(at.z >= t)
        def _(): self.third(at.z-t)
        @pl.when(jnp.logical_and(t > 0, at.z+t < at.Z))
        def _(): self.third(at.z+t)

    def tick(self, k):
        if k < self.at.Z: self.near(jnp.int32(k+1))
        elif k < 2*self.at.Z: self.far(jnp.int32(k-self.at.Z))

    def finish(self, k=0):
        at, Z, n = self.at, self.at.Z, self.n
        lax.fori_loop(min(k, Z)+1, Z+1, lambda t, _: (self.near(t), 0)[1], 0)
        lax.fori_loop(max(k-Z, 0), Z, lambda t, _: (self.far(t), 0)[1], 0)
        def fin(h, _):
            self.arrive(2*h + 1 - at.c)
            for i in range(n):
                o = self.outs[i].at[0]
                pltpu.make_async_copy(o, o, self.sd.at[i, h]).wait()
            return 0
        lax.fori_loop(0, at.KV*Z, fin, 0)
        def finz(zz, _):
            for i in range(n):
                o = self.outs[i].at[0]
                pltpu.make_async_copy(o, o, self.s2.at[i, zz]).wait()
                pltpu.make_async_copy(o, o, self.s3.at[i, zz]).wait()
                pltpu.make_async_copy(o, o, self.s3.at[i, Z+zz]).wait()
                @pl.when(jnp.logical_and(at.z < Z-1, zz <= at.z))
                def _(): pltpu.make_async_copy(o, o, self.sz.at[i, 0, zz]).wait()
                @pl.when(jnp.logical_and(at.z > 0, zz >= at.z))
                def _(): pltpu.make_async_copy(o, o, self.sz.at[i, 1, zz]).wait()
            return 0
        lax.fori_loop(0, Z, finz, 0)
        for i in range(n):
            pltpu.make_async_copy(self.ins[i], self.outs[i].at[self.own], self.sl.at[i]).wait()

def fill_block(parts, block, sem):
    copies, offset = [], 0
    for j, part in enumerate(parts):
        copies.append(pltpu.make_async_copy(part, block.at[:, pl.ds(offset, part.shape[1])], sem.at[j]))
        offset += part.shape[1]
    for copy in copies: copy.start()
    return copies

def ag_kernel(NDP, KV, count, *refs):
    parts, out, pack, fill = refs[:count], refs[count], refs[count+1], refs[count+2]
    copies = fill_block(parts, pack, fill)
    at = place(NDP, KV)
    enter(at)
    for copy in copies: copy.wait()
    gather = Gather(at, [pack], [out], refs[count+3:])
    gather.start()
    gather.finish()

def all_gather(parts, NDP, KV, cid):
    ND = NDP*KV
    rows, width = parts[0].shape[0], sum(p.shape[1] for p in parts)
    return pl.pallas_call(
        functools.partial(ag_kernel, NDP, KV, len(parts)),
        out_shape=jax.ShapeDtypeStruct((ND, rows, width), jnp.bfloat16),
        in_specs=[pl.BlockSpec(memory_space=pl.ANY)]*len(parts),
        out_specs=pl.BlockSpec(memory_space=pl.ANY),
        scratch_shapes=[pltpu.VMEM((rows, width), jnp.bfloat16), pltpu.SemaphoreType.DMA((len(parts),))] + Gather.sems(1, ND),
        compiler_params=pltpu.CompilerParams(collective_id=cid, has_side_effects=True, vmem_limit_bytes=60<<20),
        name="gather_weights",
    )(*parts)


def rs_kernel(NDP, KV, layout, *refs):
    n, count = 2, len(layout)
    Y = 2; Z = NDP // Y
    g, outs = refs[:count], refs[count:count+n]
    k = count+n
    loc, r1, r2, r3, rz = (refs[k+j*n:k+(j+1)*n] for j in range(5))
    sl, sd, qd, s2, q2, s3, q3, sz, qz = refs[k+5*n:]
    di, ki = lax.axis_index("dp"), lax.axis_index("kv")
    z, y, x, c = di // Y, di % Y, ki // 2, ki % 2
    up, dn = (di + Y, ki), (di - Y, ki)
    y2, x2 = y + c*(1-2*y), x + (1-c)*(1-2*x)
    y3, x3 = y + (1-c)*(1-2*y), x + c*(1-2*x)
    p2, p3, pd = (z*Y+y2, x2*2+c), (z*Y+y3, x3*2+c), (di, ki + 1 - 2*c)
    def half(zz, yy, xx): return (zz*Y+yy)*(KV//2) + xx
    bar = pltpu.get_barrier_semaphore()
    @pl.when(z < Z-1)
    def _(): pl.semaphore_signal(bar, 1, device_id=up, device_id_type=MESH)
    @pl.when(z > 0)
    def _(): pl.semaphore_signal(bar, 1, device_id=dn, device_id_type=MESH)
    for p in (p2, p3, pd): pl.semaphore_signal(bar, 1, device_id=p, device_id_type=MESH)
    pl.semaphore_wait(bar, 3 + jnp.where(z < Z-1, 1, 0) + jnp.where(z > 0, 1, 0))
    def rc(src, dst, ss, rsem, dev):
        return pltpu.make_async_remote_copy(src_ref=src, dst_ref=dst, send_sem=ss, recv_sem=rsem, device_id=dev, device_id_type=MESH)
    def wait(ref, sem): pltpu.make_async_copy(ref, ref, sem).wait()
    def each(f):
        def body(t0, _):
            t = Z-1-t0
            @pl.when(z >= t)
            def _(): f(z-t)
            @pl.when(jnp.logical_and(t > 0, z+t < Z))
            def _(): f(z+t)
            return 0
        lax.fori_loop(0, Z, body, 0)
    def start(zz):
        for yy, xx in ((1-y, 1-x), (y2, x2), (y3, x3), (y, x)):
            h = half(zz, yy, xx)
            for ref, (i, offset, width) in zip(g, layout):
                cols = pl.ds(offset, width)
                rc(ref.at[2*h+1-c], r1[i].at[h, :, cols], sd.at[i, h], qd.at[i, h], pd).start()
                pltpu.make_async_copy(ref.at[2*h+c], loc[i].at[h, :, cols], sl.at[i, h]).start()
    each(start)
    def add1(h):
        for i in range(n):
            wait(loc[i].at[h], sl.at[i, h]); wait(r1[i].at[h], qd.at[i, h])
            loc[i][h] = loc[i][h] + r1[i][h]
    def stage2(zz):
        for j, (yy, xx) in enumerate(((1-y, 1-x), (y3, x3))):
            h = half(zz, yy, xx)
            add1(h)
            for i in range(n):
                rc(loc[i].at[h], r2[i].at[2*zz+j], s2.at[i, 2*zz+j], q2.at[i, 2*zz+j], p3).start()
        for yy, xx in ((y2, x2), (y, x)): add1(half(zz, yy, xx))
    each(stage2)
    def stage3(zz):
        for j, (yy, xx) in enumerate(((y2, x2), (y, x))):
            h = half(zz, yy, xx)
            for i in range(n):
                wait(r2[i].at[2*zz+j], q2.at[i, 2*zz+j])
                loc[i][h] = loc[i][h] + r2[i][2*zz+j]
                if j == 0:
                    rc(loc[i].at[h], r3[i].at[zz], s3.at[i, zz], q3.at[i, zz], p2).start()
    def stage4(zz, d, dev, has):
        h = half(zz, y, x)
        for i in range(n):
            wait(r3[i].at[zz], q3.at[i, zz])
            @pl.when(has)
            def _():
                wait(rz[i].at[d, zz], qz.at[i, d, zz])
                loc[i][h] = loc[i][h] + r3[i][zz] + rz[i][d, zz]
            @pl.when(jnp.logical_not(has))
            def _(): loc[i][h] = loc[i][h] + r3[i][zz]
            rc(loc[i].at[h], rz[i].at[d, zz], sz.at[i, d, zz], qz.at[i, d, zz], dev).start()
    def body(t0, _):
        t = Z-1-t0
        @pl.when(jnp.logical_and(t >= 0, z >= t))
        def _(): stage3(z-t)
        @pl.when(jnp.logical_and(t > 0, z+t < Z))
        def _(): stage3(z+t)
        u = t + 1
        @pl.when(z + u < Z)
        def _(): stage4(z+u, 0, up, z > 0)
        @pl.when(z >= u)
        def _(): stage4(z-u, 1, dn, z < Z-1)
        return 0
    lax.fori_loop(0, Z, body, 0)
    h = half(z, y, x)
    for i in range(n): wait(r3[i].at[z], q3.at[i, z])
    @pl.when(z > 0)
    def _():
        for i in range(n): wait(rz[i].at[0, z], qz.at[i, 0, z])
    @pl.when(z < Z-1)
    def _():
        for i in range(n): wait(rz[i].at[1, z], qz.at[i, 1, z])
    for i, out in enumerate(outs):
        out[...] = loc[i][h].astype(jnp.float32) + r3[i][z].astype(jnp.float32)
        @pl.when(z > 0)
        def _(): out[...] += rz[i][0, z].astype(jnp.float32)
        @pl.when(z < Z-1)
        def _(): out[...] += rz[i][1, z].astype(jnp.float32)
    def fin(h, _):
        for i in range(n): wait(r1[i].at[h], sd.at[i, h])
        return 0
    lax.fori_loop(0, NDP*KV//2, fin, 0)
    def fin2(zz, _):
        for i in range(n):
            wait(r3[i].at[zz], s3.at[i, zz])
            wait(r2[i].at[2*zz], s2.at[i, 2*zz]); wait(r2[i].at[2*zz+1], s2.at[i, 2*zz+1])
            @pl.when(zz > z)
            def _(): wait(rz[i].at[0, zz], sz.at[i, 0, zz])
            @pl.when(zz < z)
            def _(): wait(rz[i].at[1, zz], sz.at[i, 1, zz])
        return 0
    lax.fori_loop(0, Z, fin2, 0)

def reduce_scatter(grads, down, NDP, KV, cid):
    ND = NDP*KV; Z = NDP//2
    split = [g.reshape(ND, g.shape[0]//ND, g.shape[1]) for g in (*grads, down)]
    layout, offset = [], 0
    for g in split[:-1]:
        layout.append((0, offset, g.shape[2]))
        offset += g.shape[2]
    layout.append((1, 0, down.shape[1]))
    D = pltpu.SemaphoreType.DMA
    shapes = [(split[0].shape[1], offset), split[-1].shape[1:]]
    def bufs(*lead): return [pltpu.VMEM(lead + s, jnp.bfloat16) for s in shapes]
    n = 2
    return layout, pl.pallas_call(
        functools.partial(rs_kernel, NDP, KV, layout),
        out_shape=[jax.ShapeDtypeStruct(s, jnp.float32) for s in shapes],
        in_specs=[pl.BlockSpec(memory_space=pl.ANY)]*len(split),
        out_specs=[pl.BlockSpec(memory_space=pltpu.VMEM)]*n,
        scratch_shapes=bufs(ND//2)+bufs(ND//2)+bufs(2*Z)+bufs(Z)+bufs(2, Z)
            +[D((n, ND//2))]*3+[D((n, 2*Z))]*2+[D((n, Z))]*2+[D((n, 2, Z))]*2,
        compiler_params=pltpu.CompilerParams(collective_id=cid, has_side_effects=True, vmem_limit_bytes=60<<20),
        name="scatter_gradients",
    )(*split)


D = 768
FF = 3072
HEADS = 12
HD = 64
SEQ = 64
QUAD = 4 * HD
EPS = 1e-05
NEG = -1e30
GELU_C = 0.7978845608028654
GELU_A = 0.044715
SCALE = 0.125
BF = jnp.bfloat16
F32 = jnp.float32
VM = pl.BlockSpec(memory_space=pltpu.VMEM)
ANY = pl.BlockSpec(memory_space=pl.ANY)
DMA = pltpu.SemaphoreType.DMA


def nn(a, b):
    return lax.dot_general(a, b, (((1,), (0,)), ((), ())), preferred_element_type=F32)


def nt(a, b):
    return lax.dot_general(a, b, (((1,), (1,)), ((), ())), preferred_element_type=F32)


def tn(a, b):
    return lax.dot_general(a, b, (((0,), (0,)), ((), ())), preferred_element_type=F32)


def unit_of(values):
    centre = values - jnp.mean(values, -1, keepdims=True)
    scaled = lax.rsqrt(jnp.mean(centre * centre, -1, keepdims=True) + EPS)
    return centre * scaled, scaled


def norm_backward(upstream, unit, scaled, gain):
    through = upstream * gain
    return scaled * (
        through - jnp.mean(through, -1, keepdims=True) - unit * jnp.mean(through * unit, -1, keepdims=True)
    )


def head_masks(width):
    lane = lax.broadcasted_iota(jnp.int32, (1, width), 1) // HD
    return [(lane == head).astype(F32).astype(BF) for head in range(width // HD)]


def stacked(values, masks):
    return jnp.concatenate([values * mask for mask in masks], 0)


def own_blocks(values):
    lane = lax.broadcasted_iota(jnp.int32, (HD, QUAD), 1) // HD
    total = values[:HD]
    for head in range(1, 4):
        total = jnp.where(lane == head, values[head * HD : (head + 1) * HD], total)
    return total


def load(source, target, sem):
    return pltpu.make_async_copy(source, target, sem)


def call(kernel, name, outs, ins, specs, scratch, flops, out_specs=None, cid=None, limit=56 << 20):
    params = dict(vmem_limit_bytes=limit)
    if cid is not None:
        params.update(collective_id=cid, has_side_effects=True)
    size = lambda a: a.size * a.dtype.itemsize
    return pl.pallas_call(
        kernel,
        out_shape=outs,
        in_specs=specs,
        out_specs=out_specs or [VM] * len(outs),
        scratch_shapes=scratch,
        compiler_params=pltpu.CompilerParams(**params),
        cost_estimate=pl.CostEstimate(flops=int(flops), transcendentals=0, bytes_accessed=sum(map(size, ins)) + sum(map(size, outs))),
        name=name,
    )(*ins)


def arr(shape, dtype=BF):
    return jax.ShapeDtypeStruct(shape, dtype)


def text_forward_kernel(text, packed, h1, q1, k1, v1, p1, c1, x2, h2, q2, gains, w, gw, sem):
    weights = [load(packed.at[:, pl.ds(j * D, D)], w.at[j], sem.at[j]) for j in range(5)]
    gcopy = load(packed.at[:, pl.ds(7 * D, 128)], gw, sem.at[5])
    gcopy.start()
    for copy in weights:
        copy.start()
    x = text[...].astype(F32)
    unit, _ = unit_of(x)
    gcopy.wait()
    gains[...] = gw[...].astype(F32).T[:8]
    h1[...] = (unit * gains[0:1]).astype(BF)
    for j, ref in enumerate((q1, k1, v1)):
        weights[j].wait()
        ref[...] = nn(h1[...], w[j]).astype(BF)
    rows = text.shape[0]
    first = lax.broadcasted_iota(jnp.int32, (rows, rows), 0)
    second = lax.broadcasted_iota(jnp.int32, (rows, rows), 1)
    allowed = jnp.logical_and(first >= second, first // SEQ == second // SEQ)
    masks = head_masks(128)
    for pair in range(HEADS // 2):
        lanes = slice(pair * 128, (pair + 1) * 128)
        total = None
        for j, mask in enumerate(masks):
            scores = nt(q1[:, lanes] * mask, k1[:, lanes]) * SCALE
            scores = jnp.where(allowed, scores, NEG)
            powers = jnp.exp(scores - jnp.max(scores, -1, keepdims=True))
            probs = (powers / jnp.sum(powers, -1, keepdims=True)).astype(BF)
            p1[2 * pair + j] = probs
            part = nn(probs, v1[:, lanes] * mask)
            total = part if total is None else total + part
        c1[:, lanes] = total.astype(BF)
    weights[3].wait()
    second_res = x + nn(c1[...], w[3])
    x2[...] = second_res
    unit, _ = unit_of(second_res)
    h2[...] = (unit * gains[1:2]).astype(BF)
    weights[4].wait()
    q2[...] = nn(h2[...], w[4]).astype(BF)


def text_forward(text, packed):
    rows = text.shape[0]
    low = arr((rows, D))
    return call(
        text_forward_kernel, "text_forward",
        [low, low, low, low, arr((HEADS, rows, rows)), low, arr((rows, D), F32), low, low, arr((8, D), F32)],
        [text, packed], [VM, ANY],
        [pltpu.VMEM((5, D, D), BF), pltpu.VMEM((D, 128), BF), DMA((6,))], 10 * rows * D * D)


def group_place():
    di, ki = lax.axis_index("dp"), lax.axis_index("kv")
    x, c = ki // 2, ki % 2
    return di, ki, x, c


def group_barrier(di, ki, x, c):
    bar = pltpu.get_barrier_semaphore()
    for other in (2 * x + 1 - c, 2 * (1 - x) + c, 2 * (1 - x) + 1 - c):
        pl.semaphore_signal(bar, 1, device_id=(di, other), device_id_type=MESH)
    pl.semaphore_wait(bar, 3)


def remote(src, dst, send, recv, device):
    return pltpu.make_async_remote_copy(
        src_ref=src, dst_ref=dst, send_sem=send, recv_sem=recv, device_id=device, device_id_type=MESH)


def cross_forward_kernel(NDP, KV, q2, image, lengths, patches, packed, out_part, up_part, down_part,
                         c2, lse, keys, vals, e, stats, qall, second, down, w, obuf, ro, rst, usable, block, down_block,
                         wsem, ssem, rsem, fsem, *gsems):
    at = place(NDP, KV)
    di, ki, x, c = at.di, at.ki, at.x, at.c
    caps, tokens = patches.shape
    own_caps = caps // 4
    fills = fill_block([out_part, up_part], block, fsem)
    fills.append(load(down_part, down_block, fsem.at[2]))
    fills[-1].start()
    core, over, diag = 2 * x + 1 - c, 2 * (1 - x) + c, 2 * (1 - x) + 1 - c
    weights = [load(packed.at[:, pl.ds((5 + j) * D, D)], w.at[j], wsem.at[j]) for j in range(2)]
    for copy in weights:
        copy.start()
    own_copy = load(q2, qall.at[ki], wsem.at[2])
    own_copy.start()
    enter(at, True)
    to_core = remote(q2, qall.at[ki], ssem.at[0], rsem.at[ki], (di, core))
    to_over = remote(q2, qall.at[ki], ssem.at[1], rsem.at[ki], (di, over))
    to_over.start()
    to_core.start()
    for copy in fills:
        copy.wait()
    gather = Gather(at, [block, down_block], [second, down], gsems)
    gather.start()
    row = lax.broadcasted_iota(jnp.int32, usable.shape, 0)
    limit = jnp.zeros(usable.shape, jnp.int32)
    for cap in range(caps):
        limit = jnp.where(row == cap, lengths[cap], limit)
    position = lax.broadcasted_iota(jnp.int32, usable.shape, 1) + ki * tokens
    usable[...] = jnp.zeros(usable.shape, BF)
    usable[0:caps, :] = jnp.where(jnp.logical_and(position < limit, True)[0:caps], (patches[...] == 1).astype(F32), 0.0).astype(BF)
    weights[0].wait()

    def project(j, ref, i):
        rows = pl.ds(pl.multiple_of(i * tokens, 16), tokens)
        ref[rows, :] = nn(image[rows, :], w[j]).astype(BF)

    lax.fori_loop(0, caps, lambda i, _: (project(0, keys, i), 0)[1], 0)
    load(qall.at[over], qall.at[over], rsem.at[over]).wait()
    relay = remote(qall.at[over], qall.at[over], ssem.at[2], rsem.at[over], (di, core))
    relay.start()
    gather.tick(0)
    weights[1].wait()
    lax.fori_loop(0, caps, lambda i, _: (project(1, vals, i), 0)[1], 0)
    gather.tick(1)
    load(qall.at[core], qall.at[core], rsem.at[core]).wait()
    load(qall.at[diag], qall.at[diag], rsem.at[diag]).wait()
    own_copy.wait()
    masks = head_masks(QUAD)

    def owner_of(step):
        return 2 * ((x + 1 + step // 2) % 2) + (c + 1 + step % 2) % 2

    def attend(i, _):
        owner, local = owner_of(i // own_caps), i % own_caps
        cap = owner * own_caps + local
        rows = pl.ds(pl.multiple_of(cap * tokens, 16), tokens)
        queries = pl.ds(pl.multiple_of(local * SEQ, 16), SEQ)
        for j in range(4):
            @pl.when(i == (2 + 3 * j) * caps // 12)
            def _():
                gather.tick(2 + j)
        chosen = (lax.broadcasted_iota(jnp.int32, (usable.shape[0], QUAD), 0) == cap).astype(F32).astype(BF)
        shift = tn(usable[...], chosen)
        for g in range(3):
            lanes = slice(g * QUAD, (g + 1) * QUAD)
            scores = nt(keys[rows, lanes], stacked(qall[owner, queries, lanes], masks)) * SCALE
            scores = jnp.where(shift > 0.5, scores, NEG)
            top = jnp.max(scores, 0, keepdims=True)
            powers = jnp.where(shift > 0.5, jnp.exp(scores - top), 0.0)
            low = powers.astype(BF)
            e[pl.ds(pl.multiple_of((cap * 3 + g) * tokens, 16), tokens), :] = low
            stats[owner, pl.ds(3 * local + g, 1), :] = top
            stats[owner, pl.ds(16 + 3 * local + g, 1), :] = jnp.sum(powers, 0, keepdims=True)
            obuf[owner, queries, lanes] = own_blocks(tn(low, vals[rows, lanes])).astype(BF)

        @pl.when(jnp.logical_and(local == own_caps - 1, owner != ki))
        def _():
            remote(obuf.at[owner], ro.at[ki], ssem.at[3 + owner], rsem.at[4 + ki], (di, owner)).start()
            remote(stats.at[owner], rst.at[ki], ssem.at[7 + owner], rsem.at[8 + ki], (di, owner)).start()

        return 0

    lax.fori_loop(0, caps, attend, 0)
    ro[ki] = obuf[ki]
    rst[ki] = stats[ki]
    for other in (core, over, diag):
        load(ro.at[other], ro.at[other], rsem.at[4 + other]).wait()
        load(rst.at[other], rst.at[other], rsem.at[8 + other]).wait()
    lane = lax.broadcasted_iota(jnp.int32, (HD, QUAD), 1) // HD

    def combine(local, _):
        queries = pl.ds(pl.multiple_of(local * SEQ, 16), SEQ)
        for g in range(3):
            row = pl.ds(3 * local + g, 1)
            row_sum = pl.ds(16 + 3 * local + g, 1)
            tops = [rst[k, row, :] for k in range(4)]
            top = jnp.maximum(jnp.maximum(tops[0], tops[1]), jnp.maximum(tops[2], tops[3]))
            parts = [jnp.exp(t - top) for t in tops]
            total = sum(part * rst[k, row_sum, :] for k, part in enumerate(parts))
            lse[row, :] = top + jnp.log(total)
            table = jnp.concatenate([part / total for part in parts] * 2, 0).T
            mixed = 0.0
            for k in range(4):
                column = table[:, k : k + 1]
                weight = column[:HD] * jnp.ones((HD, QUAD), F32)
                for head in range(1, 4):
                    weight = jnp.where(lane == head, column[head * HD : (head + 1) * HD], weight)
                mixed = mixed + weight * ro[k, queries, g * QUAD : (g + 1) * QUAD].astype(F32)
            c2[queries, g * QUAD : (g + 1) * QUAD] = mixed
        return 0

    lax.fori_loop(0, own_caps, combine, 0)
    to_core.wait_send()
    to_over.wait_send()
    relay.wait_send()
    for other in (core, over, diag):
        load(obuf.at[other], obuf.at[other], ssem.at[3 + other]).wait()
        load(stats.at[other], stats.at[other], ssem.at[7 + other]).wait()
    gather.finish(6)


def cross_forward(q2, image, lengths, patches, packed, out_part, up_part, down_part, NDP, KV, cid):
    rows, (caps, tokens), ND = q2.shape[0], patches.shape, NDP * KV
    width = out_part.shape[1] + up_part.shape[1]
    return call(
        functools.partial(cross_forward_kernel, NDP, KV), "cross_forward",
        [arr((rows, D), F32), arr((16, QUAD), F32), arr((caps * tokens, D)), arr((caps * tokens, D)),
         arr((caps * 3 * tokens, QUAD)), arr((4, 32, QUAD), F32), arr((4, rows, D)),
         arr((ND, out_part.shape[0], width)), arr((ND,) + down_part.shape)],
        [q2, image, lengths, patches, packed, out_part, up_part, down_part],
        [VM, VM, pl.BlockSpec(memory_space=pltpu.SMEM), VM, ANY, ANY, ANY, ANY],
        [pltpu.VMEM((2, D, D), BF), pltpu.VMEM((4, rows, D), BF), pltpu.VMEM((4, rows, D), BF),
         pltpu.VMEM((4, 32, QUAD), F32), pltpu.VMEM((-(-caps // 16) * 16, tokens), BF),
         pltpu.VMEM((out_part.shape[0], width), BF), pltpu.VMEM(down_part.shape, BF),
         DMA((3,)), DMA((11,)), DMA((12,)), DMA((3,))] + Gather.sems(2, ND),
        4 * caps * tokens * D * D, out_specs=[VM] * 7 + [ANY] * 2, cid=cid)


def cross_backward_kernel(dc2, c2, lse, stats, qall, keys, vals, e, image, dq2, dk, dv, wk, wv,
                          dall, sall, qbuf, rq, csem, ssem, rsem):
    di, ki, x, c = group_place()
    rows_all = keys.shape[0]
    caps = 4 * (dc2.shape[0] // SEQ)
    own_caps = caps // 4
    tokens = rows_all // caps
    core, over, diag = 2 * x + 1 - c, 2 * (1 - x) + c, 2 * (1 - x) + 1 - c
    masks = head_masks(QUAD)
    sall[ki, 0:16, :] = lse[...]

    def dots(local, _):
        queries = pl.ds(pl.multiple_of(local * SEQ, 16), SEQ)
        for g in range(3):
            lanes = slice(g * QUAD, (g + 1) * QUAD)
            product = dc2[queries, lanes].astype(F32) * c2[queries, lanes]
            product = jnp.concatenate([product * mask.astype(F32) for mask in masks], 0)
            sums = lax.dot_general(
                jnp.ones((8, QUAD), F32), product, (((1,), (1,)), ((), ())),
                preferred_element_type=F32, precision=lax.Precision.HIGHEST)
            sall[ki, pl.ds(16 + 3 * local + g, 1), :] = sums[0:1]
        return 0

    own_copy = load(dc2, dall.at[ki], csem)
    own_copy.start()
    group_barrier(di, ki, x, c)
    to_over = remote(dc2, dall.at[ki], ssem.at[1], rsem.at[ki], (di, over))
    to_core = remote(dc2, dall.at[ki], ssem.at[0], rsem.at[ki], (di, core))
    to_over.start()
    to_core.start()
    lax.fori_loop(0, own_caps, dots, 0)
    small = [remote(sall.at[ki], sall.at[ki], ssem.at[2 + j], rsem.at[4 + ki], (di, other))
             for j, other in enumerate((core, over, diag))]
    for copy in small:
        copy.start()
    own_copy.wait()
    relay = remote(dall.at[over], dall.at[over], ssem.at[5], rsem.at[over], (di, core))

    def attend(i, _):
        step, local = i // own_caps, i % own_caps
        owner = 2 * ((x + step // 2) % 2) + (c + step % 2) % 2

        @pl.when(i == own_caps)
        def _():
            load(dall.at[core], dall.at[core], rsem.at[core]).wait()
            load(sall.at[core], sall.at[core], rsem.at[4 + core]).wait()

        @pl.when(i == 2 * own_caps - 1)
        def _():
            load(dall.at[over], dall.at[over], rsem.at[over]).wait()
            relay.start()

        @pl.when(i == 2 * own_caps)
        def _():
            load(sall.at[over], sall.at[over], rsem.at[4 + over]).wait()

        @pl.when(i == 3 * own_caps)
        def _():
            load(dall.at[diag], dall.at[diag], rsem.at[diag]).wait()
            load(sall.at[diag], sall.at[diag], rsem.at[4 + diag]).wait()

        cap = owner * own_caps + local
        rows = pl.ds(pl.multiple_of(cap * tokens, 16), tokens)
        queries = pl.ds(pl.multiple_of(local * SEQ, 16), SEQ)
        for g in range(3):
            lanes = slice(g * QUAD, (g + 1) * QUAD)
            factor = jnp.exp(stats[owner, pl.ds(3 * local + g, 1), :] - sall[owner, pl.ds(3 * local + g, 1), :])
            dots_row = sall[owner, pl.ds(16 + 3 * local + g, 1), :]
            probs = e[pl.ds(pl.multiple_of((cap * 3 + g) * tokens, 16), tokens), :].astype(F32) * factor
            upstream = stacked(dall[owner, queries, lanes], masks)
            queried = stacked(qall[owner, queries, lanes], masks)
            grad = nt(vals[rows, lanes], upstream)
            grad = (probs * (grad - dots_row)).astype(BF)
            dv[rows, lanes] = nn(probs.astype(BF), upstream).astype(BF)
            dk[rows, lanes] = (nn(grad, queried) * SCALE).astype(BF)
            qbuf[owner, queries, lanes] = (own_blocks(tn(grad, keys[rows, lanes])) * SCALE).astype(BF)

        @pl.when(jnp.logical_and(local == own_caps - 1, owner != ki))
        def _():
            remote(qbuf.at[owner], rq.at[ki], ssem.at[6 + owner], rsem.at[8 + ki], (di, owner)).start()

        return 0

    lax.fori_loop(0, caps, attend, 0)

    def weight(j, _):
        cols = pl.ds(pl.multiple_of(j * 256, 256), 256)
        flipped = image[:, cols].T
        wk[cols, :] = nn(flipped, dk[...]).astype(BF)
        wv[cols, :] = nn(flipped, dv[...]).astype(BF)
        return 0

    lax.fori_loop(0, D // 256, weight, 0)
    rq[ki] = qbuf[ki]
    for other in (core, over, diag):
        load(rq.at[other], rq.at[other], rsem.at[8 + other]).wait()
    dq2[...] = (rq[0].astype(F32) + rq[1].astype(F32) + rq[2].astype(F32) + rq[3].astype(F32)).astype(BF)
    to_core.wait_send()
    to_over.wait_send()
    relay.wait_send()
    for copy in small:
        copy.wait_send()
    for other in (core, over, diag):
        load(qbuf.at[other], qbuf.at[other], ssem.at[6 + other]).wait()


def cross_backward(dc2, c2, lse, stats, qall, keys, vals, e, image, cid):
    rows = dc2.shape[0]
    ins = [dc2, c2, lse, stats, qall, keys, vals, e, image]
    return call(
        cross_backward_kernel, "cross_backward",
        [arr((rows, D)), arr(keys.shape), arr(keys.shape), arr((D, D)), arr((D, D))],
        ins, [VM] * len(ins),
        [pltpu.VMEM((4, rows, D), BF), pltpu.VMEM((4, 32, QUAD), F32), pltpu.VMEM((4, rows, D), BF),
         pltpu.VMEM((4, rows, D), BF), DMA, DMA((10,)), DMA((12,))],
        4 * keys.shape[0] * D * D, cid=cid)


def mlp_kernel(c2, x2, grad, gains, packed, down, out, dx3, dc2, dup, ddown, dco, ng, wu, wd, wc, dh, acc, ht, sem):
    wcopy = load(packed.at[:, pl.ds(0, D)], wc, sem.at[8])
    wcopy.start()
    ups = [load(packed.at[:, pl.ds((1 + j) * D, D)], wu.at[j], sem.at[j]) for j in range(4)]
    downs = [load(down.at[pl.ds(j * D, D), :], wd.at[j], sem.at[4 + j]) for j in range(4)]
    for j in range(4):
        ups[j].start()
        downs[j].start()
    low = c2[...].astype(BF)
    wcopy.wait()
    third = x2[...] + nn(low, wc[...])
    unit, scaled = unit_of(third)
    gain = gains[2:3]
    h3 = (unit * gain).astype(BF)
    ht[...] = h3.T
    g = grad[...]
    acc[...] = third
    for j in range(4):
        ups[j].wait()
        downs[j].wait()
        u = nn(h3, wu[j])
        square = u * u
        tanh_part = jnp.tanh(GELU_C * (u + GELU_A * square * u))
        active = (0.5 * u * (1.0 + tanh_part)).astype(BF)
        slope = 0.5 * (1.0 + tanh_part) + 0.5 * u * (1.0 - tanh_part * tanh_part) * GELU_C * (1.0 + 3.0 * GELU_A * square)
        acc[...] += nn(active, wd[j])
        du = (nt(g, wd[j]) * slope).astype(BF)
        part = nt(du, wu[j])
        dh[...] = part if j == 0 else dh[...] + part
        ddown[pl.ds(j * D, D), :] = tn(active, g).astype(BF)
        dup[:, pl.ds(j * D, D)] = nn(ht[...], du).astype(BF)
    out[...] = acc[...].astype(BF)
    upstream = dh[...]
    ng[...] = jnp.broadcast_to(jnp.sum(upstream * unit, 0, keepdims=True), ng.shape)
    total = g.astype(F32) + norm_backward(upstream, unit, scaled, gain)
    dx3[...] = total
    branch = total.astype(BF)
    dc2[...] = nt(branch, wc[...]).astype(BF)
    dco[...] = tn(low, branch).astype(BF)


def mlp(c2, x2, grad, gains, packed, down):
    rows = c2.shape[0]
    return call(
        mlp_kernel, "feed_forward",
        [arr((rows, D)), arr((rows, D), F32), arr((rows, D)), arr((D, FF)), arr((FF, D)), arr((D, D)), arr((8, D), F32)],
        [c2, x2, grad, gains, packed, down], [VM] * 4 + [ANY] * 2,
        [pltpu.VMEM((4, D, D), BF), pltpu.VMEM((4, D, D), BF), pltpu.VMEM((D, D), BF), pltpu.VMEM((rows, D), F32),
         pltpu.VMEM((rows, D), F32), pltpu.VMEM((D, rows), BF), DMA((9,))], 12 * rows * D * FF)


def image_grad_kernel(layout, dk, dv, packed, first, second, out, *refs):
    count = len(layout)
    outs, (norms, w, sem, osem) = refs[: count - 1], refs[count - 1 :]
    sources = (first, second)
    copies = []
    for j, ref in enumerate(outs):
        i, offset, width = layout[j if j < count - 2 else count - 1]
        copies.append(load(sources[i].at[:, pl.ds(offset, width)], ref, osem.at[j]))

    @pl.when(pl.program_id(0) == 0)
    def _():
        weights = [load(packed.at[:, pl.ds((5 + j) * D, D)], w.at[j], sem.at[j]) for j in range(2)]
        for copy in weights + copies:
            copy.start()
        _, offset, width = layout[count - 2]
        block = first[:, offset : offset + width]
        block = jnp.concatenate([block, jnp.zeros((128 - block.shape[0], width), F32)], 0)
        norms[...] = block.T[:8]
        for copy in weights:
            copy.wait()

    out[...] = nt(dk[...], w[0]) + nt(dv[...], w[1])

    @pl.when(pl.program_id(0) == pl.num_programs(0) - 1)
    def _():
        for copy in copies:
            copy.wait()


def image_gradient(dk, dv, packed, layout, first, second):
    rows = dk.shape[0]
    block = rows // 6
    count = len(layout)
    spec = pl.BlockSpec((block, D), lambda i: (i, 0))
    whole = lambda a: pl.BlockSpec(a.shape, lambda i: (0, 0))
    shapes = [arr(((first, second)[i].shape[0], width), F32) for i, _, width in layout]
    norms = arr((8, 128), F32)
    return pl.pallas_call(
        functools.partial(image_grad_kernel, layout),
        out_shape=[arr((rows, D), F32)] + shapes[: count - 2] + shapes[count - 1 :] + [norms],
        grid=(rows // block,),
        in_specs=[spec, spec, ANY, whole(first), whole(second)],
        out_specs=[spec] + [ANY] * (count - 1) + [whole(norms)],
        scratch_shapes=[pltpu.VMEM((2, D, D), BF), DMA((2,)), DMA((count - 1,))],
        compiler_params=pltpu.CompilerParams(vmem_limit_bytes=56 << 20),
        cost_estimate=pl.CostEstimate(flops=4 * rows * D * D, transcendentals=0, bytes_accessed=8 * rows * D),
        name="image_gradient",
    )(dk, dv, packed, first, second)


def text_backward_kernel(dq2, dx3, text, x2, h1, h2, c1, q1, k1, v1, p1, gains, ng3, packed,
                         text_grad, wq, wk, wv, wo, wcq, ngs, w, dq, dk, dv, rows_t, sem):
    weights = [load(packed.at[:, pl.ds(j * D, D)], w.at[j], sem.at[j]) for j in range(5)]
    for j in (4, 3, 0, 1, 2):
        weights[j].start()
    unit, scaled = unit_of(x2[...])
    weights[4].wait()
    upstream = nt(dq2[...], w[4])
    ngs_two = jnp.sum(upstream * unit, 0, keepdims=True)
    grad_two = dx3[...] + norm_backward(upstream, unit, scaled, gains[1:2])
    wcq[...] = tn(h2[...], dq2[...]).astype(BF)
    branch = grad_two.astype(BF)
    weights[3].wait()
    dc1 = nt(branch, w[3]).astype(BF)
    wo[...] = tn(c1[...], branch).astype(BF)
    masks = head_masks(128)
    for pair in range(HEADS // 2):
        lanes = slice(pair * 128, (pair + 1) * 128)
        sums = [None] * 3
        for j, mask in enumerate(masks):
            low = p1[2 * pair + j]
            probs = low.astype(F32)
            above = dc1[:, lanes] * mask
            grad = nt(above, v1[:, lanes])
            grad = (probs * (grad - jnp.sum(probs * grad, -1, keepdims=True))).astype(BF)
            parts = [nn(grad, k1[:, lanes] * mask), tn(grad, q1[:, lanes] * mask), tn(low, above)]
            sums = parts if j == 0 else [a + b for a, b in zip(sums, parts)]
        dq[:, lanes] = (sums[0] * SCALE).astype(BF)
        dk[:, lanes] = (sums[1] * SCALE).astype(BF)
        dv[:, lanes] = sums[2].astype(BF)
    upstream = None
    flipped = h1[...].T
    for j, (ref, out) in enumerate(((dq, wq), (dk, wk), (dv, wv))):
        weights[j].wait()
        part = nt(ref[...], w[j])
        upstream = part if j == 0 else upstream + part
        out[...] = nn(flipped, ref[...]).astype(BF)
    unit, scaled = unit_of(text[...].astype(F32))
    text_grad[...] = grad_two + norm_backward(upstream, unit, scaled, gains[0:1])
    rows_t[...] = jnp.zeros_like(rows_t)
    rows_t[0:1] = jnp.sum(upstream * unit, 0, keepdims=True)
    rows_t[1:2] = ngs_two
    rows_t[2:3] = ng3[0:1]
    ngs[...] = rows_t[...].T.astype(BF)


def text_backward(dq2, dx3, text, x2, h1, h2, c1, q1, k1, v1, p1, gains, ng3, packed):
    rows = text.shape[0]
    ins = [dq2, dx3, text, x2, h1, h2, c1, q1, k1, v1, p1, gains, ng3, packed]
    return call(
        text_backward_kernel, "text_backward",
        [arr((rows, D), F32)] + [arr((D, D))] * 5 + [arr((D, 128))],
        ins, [VM] * 13 + [ANY],
        [pltpu.VMEM((5, D, D), BF)] + [pltpu.VMEM((rows, D), BF)] * 3 + [pltpu.VMEM((128, D), F32), DMA((5,))],
        20 * rows * D * D)


def per_device(
    text_tokens, image_tokens, image_lengths, patch_mask, self_query, self_key, self_value, self_out, cross_query,
    cross_key, cross_value, cross_out, mlp_up, mlp_down, norm_self, norm_cross, norm_mlp, out_grad,
):
    ndp, nkv = lax.axis_size("dp"), lax.axis_size("kv")
    caps, tokens = image_tokens.shape[0], image_tokens.shape[1]
    gain_block = jnp.pad(jnp.stack([norm_self, norm_cross, norm_mlp], 1), ((0, 0), (0, 125)))
    parts = [self_query, self_key, self_value, self_out, cross_query, cross_key, cross_value, gain_block]
    packed = all_gather(parts, ndp, nkv, 1).reshape(D, -1)
    image = image_tokens.reshape(caps * tokens, D)
    h1, q1, k1, v1, p1, c1, x2, h2, q2, gains = text_forward(text_tokens, packed)
    c2, lse, keys, vals, e, stats, qall, second, down = cross_forward(
        q2, image, image_lengths, patch_mask, packed, cross_out, mlp_up, mlp_down, ndp, nkv, 2)
    second = second.reshape(D, -1)
    down = down.reshape(FF, D)
    layer_out, dx3, dc2, d_up, d_down, d_co, ng3 = mlp(c2, x2, out_grad, gains, second, down)
    dq2, dk2, dv2, d_ck, d_cv = cross_backward(dc2, c2, lse, stats, qall, keys, vals, e, image, 3)
    text_grad, d_q, d_k, d_v, d_o, d_cq, ngs = text_backward(
        dq2, dx3, text_tokens, x2, h1, h2, c1, q1, k1, v1, p1, gains, ng3, packed)
    layout, (first, other) = reduce_scatter([d_q, d_k, d_v, d_o, d_cq, d_ck, d_cv, d_co, d_up, ngs], d_down, ndp, nkv, 4)
    image_grad, *parts, norms = image_gradient(dk2, dv2, packed, layout, first, other)
    rows = norm_self.shape[0]
    return (layer_out, text_grad, image_grad.reshape(caps, tokens, D), *parts, norms[0, :rows], norms[1, :rows], norms[2, :rows])


def solution(mesh):
    in_specs = (
        P(("dp", "kv"), None),
        P("dp", "kv", None),
        P("dp"),
        P("dp", "kv"),
        P(("dp", "kv"), None),
        P(("dp", "kv"), None),
        P(("dp", "kv"), None),
        P(("dp", "kv"), None),
        P(("dp", "kv"), None),
        P(("dp", "kv"), None),
        P(("dp", "kv"), None),
        P(("dp", "kv"), None),
        P(("dp", "kv"), None),
        P(("dp", "kv"), None),
        P(("dp", "kv")),
        P(("dp", "kv")),
        P(("dp", "kv")),
        P(("dp", "kv"), None),
    )
    out_specs = (
        P(("dp", "kv"), None),
        P(("dp", "kv"), None),
        P("dp", "kv", None),
        P(("dp", "kv"), None),
        P(("dp", "kv"), None),
        P(("dp", "kv"), None),
        P(("dp", "kv"), None),
        P(("dp", "kv"), None),
        P(("dp", "kv"), None),
        P(("dp", "kv"), None),
        P(("dp", "kv"), None),
        P(("dp", "kv"), None),
        P(("dp", "kv"), None),
        P(("dp", "kv")),
        P(("dp", "kv")),
        P(("dp", "kv")),
    )
    return jax.shard_map(
        per_device, mesh=mesh, in_specs=in_specs, out_specs=out_specs, check_vma=False
    )
```

```python
import functools
import types

import jax
import jax.numpy as jnp
from jax import lax
from jax.experimental import pallas as pl
from jax.experimental.pallas import tpu as pltpu
from jax.sharding import PartitionSpec as P

MESH = pl.DeviceIdType.MESH
def place(NDP, KV):
    di, ki = lax.axis_index("dp"), lax.axis_index("kv")
    Y = 2
    z, y, x, c = di // Y, di % Y, ki // 2, ki % 2
    y2, x2 = y + c*(1-2*y), x + (1-c)*(1-2*x)
    y3, x3 = y + (1-c)*(1-2*y), x + c*(1-2*x)
    return types.SimpleNamespace(
        di=di, ki=ki, z=z, y=y, x=x, c=c, Y=Y, Z=NDP//Y, KV=KV,
        split=((y2, x2), (y3, x3)), fixed=((y, 1-x), (1-y, x)), up=(di + Y, ki), dn=(di - Y, ki),
        px=(di, 2*(1-x) + c), py=(z*Y+1-y, ki), pd=(di, ki + 1 - 2*c), diag=(di, 2*(1-x) + 1 - c))

def enter(at, group=False):
    bar = pltpu.get_barrier_semaphore()
    @pl.when(at.z < at.Z-1)
    def _(): pl.semaphore_signal(bar, 1, device_id=at.up, device_id_type=MESH)
    @pl.when(at.z > 0)
    def _(): pl.semaphore_signal(bar, 1, device_id=at.dn, device_id_type=MESH)
    peers = (at.px, at.py, at.pd) + ((at.diag,) if group else ())
    for p in peers: pl.semaphore_signal(bar, 1, device_id=p, device_id_type=MESH)
    pl.semaphore_wait(bar, len(peers) + jnp.where(at.z < at.Z-1, 1, 0) + jnp.where(at.z > 0, 1, 0))

class Gather:
    def __init__(self, at, ins, outs, sems, route):
        self.at, self.ins, self.outs = at, ins, outs
        self.recv, self.sz, self.s2, self.s3, self.sd, self.sl = sems
        self.n = len(ins)
        self.own = self.slot(at.z, at.y, at.x)
        (self.y2, self.x2), (self.y3, self.x3) = route
        self.p2, self.p3 = ((at.z*at.Y+yy, 2*xx+at.c) for yy, xx in route)

    @staticmethod
    def sems(n, ND):
        Z = ND // 8
        D = pltpu.SemaphoreType.DMA
        return [D((n, ND)), D((n, 2, Z)), D((n, Z)), D((n, 2*Z)), D((n, ND//2)), D((n,))]

    def slot(self, zz, yy, xx):
        return (zz*self.at.Y+yy)*self.at.KV + xx*2 + self.at.c

    def send(self, s, sems, dev, own=False):
        for i in range(self.n):
            pltpu.make_async_remote_copy(
                src_ref=self.ins[i] if own else self.outs[i].at[s], dst_ref=self.outs[i].at[s], send_sem=sems(i),
                recv_sem=self.recv.at[i, s], device_id=dev, device_id_type=MESH).start()

    def arrive(self, s):
        for i in range(self.n):
            pltpu.make_async_copy(self.outs[i].at[s], self.outs[i].at[s], self.recv.at[i, s]).wait()

    def spread(self, zz, own=False):
        s = self.slot(zz, self.at.y, self.at.x)
        self.send(s, lambda i: self.s2.at[i, zz], self.p2, own)
        self.send(s, lambda i: self.s3.at[i, zz], self.p3, own)
        self.send(s, lambda i: self.sd.at[i, s//2], self.at.pd, own)

    def start(self):
        at, own = self.at, self.own
        @pl.when(at.z < at.Z-1)
        def _(): self.send(own, lambda i: self.sz.at[i, 0, at.z], at.up, True)
        @pl.when(at.z > 0)
        def _(): self.send(own, lambda i: self.sz.at[i, 1, at.z], at.dn, True)
        self.spread(at.z, True)
        for i in range(self.n):
            pltpu.make_async_copy(self.ins[i], self.outs[i].at[own], self.sl.at[i]).start()

    def second(self, zz):
        at = self.at
        s = self.slot(zz, self.y2, self.x2)
        self.arrive(s)
        self.send(s, lambda i: self.s3.at[i, at.Z+zz], self.p3)
        self.send(s, lambda i: self.sd.at[i, s//2], at.pd)

    def near(self, t):
        at = self.at
        @pl.when(at.z >= t)
        def _():
            s = self.slot(at.z-t, at.y, at.x); self.arrive(s)
            @pl.when(at.z < at.Z-1)
            def _(): self.send(s, lambda i: self.sz.at[i, 0, at.z-t], at.up)
            self.spread(at.z-t)
        @pl.when(at.z + t < at.Z)
        def _():
            s = self.slot(at.z+t, at.y, at.x); self.arrive(s)
            @pl.when(at.z > 0)
            def _(): self.send(s, lambda i: self.sz.at[i, 1, at.z+t], at.dn)
            self.spread(at.z+t)
        @pl.when(at.z >= t-1)
        def _(): self.second(at.z-t+1)
        @pl.when(jnp.logical_and(t > 1, at.z+t-1 < at.Z))
        def _(): self.second(at.z+t-1)

    def third(self, zz):
        at = self.at
        for yy, xx in ((self.y3, self.x3), (1-at.y, 1-at.x)):
            s = self.slot(zz, yy, xx)
            self.arrive(s)
            self.send(s, lambda i: self.sd.at[i, s//2], at.pd)

    def far(self, t):
        at = self.at
        @pl.when(at.z >= t)
        def _(): self.third(at.z-t)
        @pl.when(jnp.logical_and(t > 0, at.z+t < at.Z))
        def _(): self.third(at.z+t)

    def tick(self, k):
        if k < self.at.Z: self.near(jnp.int32(k+1))
        elif k < 2*self.at.Z: self.far(jnp.int32(k-self.at.Z))

    def finish(self, k=0):
        at, Z, n = self.at, self.at.Z, self.n
        lax.fori_loop(min(k, Z)+1, Z+1, lambda t, _: (self.near(t), 0)[1], 0)
        lax.fori_loop(max(k-Z, 0), Z, lambda t, _: (self.far(t), 0)[1], 0)
        def fin(h, _):
            self.arrive(2*h + 1 - at.c)
            for i in range(n):
                o = self.outs[i].at[0]
                pltpu.make_async_copy(o, o, self.sd.at[i, h]).wait()
            return 0
        lax.fori_loop(0, at.KV*Z, fin, 0)
        def finz(zz, _):
            for i in range(n):
                o = self.outs[i].at[0]
                pltpu.make_async_copy(o, o, self.s2.at[i, zz]).wait()
                pltpu.make_async_copy(o, o, self.s3.at[i, zz]).wait()
                pltpu.make_async_copy(o, o, self.s3.at[i, Z+zz]).wait()
                @pl.when(jnp.logical_and(at.z < Z-1, zz <= at.z))
                def _(): pltpu.make_async_copy(o, o, self.sz.at[i, 0, zz]).wait()
                @pl.when(jnp.logical_and(at.z > 0, zz >= at.z))
                def _(): pltpu.make_async_copy(o, o, self.sz.at[i, 1, zz]).wait()
            return 0
        lax.fori_loop(0, Z, finz, 0)
        for i in range(n):
            pltpu.make_async_copy(self.ins[i], self.outs[i].at[self.own], self.sl.at[i]).wait()

class PlaneGather(Gather):
    @staticmethod
    def sems(n, ND):
        D = pltpu.SemaphoreType.DMA
        return [D((n, ND)), D((n, 2, ND)), D((n, 1)), D((n, 2)), D((n, ND//2)), D((n,))]

    def onward(self, s, up, down, own=False):
        at = self.at
        if up:
            @pl.when(at.z < at.Z-1)
            def _(): self.send(s, lambda i: self.sz.at[i, 0, s], at.up, own)
        if down:
            @pl.when(at.z > 0)
            def _(): self.send(s, lambda i: self.sz.at[i, 1, s], at.dn, own)
        self.send(s, lambda i: self.sd.at[i, s//2], at.pd, own)

    def start(self):
        own = self.own
        self.send(own, lambda i: self.s2.at[i, 0], self.p2, True)
        self.send(own, lambda i: self.s3.at[i, 0], self.p3, True)
        self.onward(own, True, True, True)
        for i in range(self.n):
            pltpu.make_async_copy(self.ins[i], self.outs[i].at[own], self.sl.at[i]).start()

    def lines(self):
        at = self.at
        return ((at.y, at.x), (self.y2, self.x2), (self.y3, self.x3), (1-at.y, 1-at.x))

    def plane(self):
        at = self.at
        for j, (yy, xx) in enumerate(self.lines()[1:]):
            s = self.slot(at.z, yy, xx)
            self.arrive(s)
            if j == 0: self.send(s, lambda i: self.s3.at[i, 1], self.p3)
            self.onward(s, True, True)

    def level(self, t):
        at = self.at
        @pl.when(at.z >= t)
        def _():
            for yy, xx in self.lines():
                s = self.slot(at.z-t, yy, xx)
                self.arrive(s)
                self.onward(s, True, False)
        @pl.when(at.z + t < at.Z)
        def _():
            for yy, xx in self.lines():
                s = self.slot(at.z+t, yy, xx)
                self.arrive(s)
                self.onward(s, False, True)

    def tick(self, k):
        if k == 0: self.plane()
        elif k < self.at.Z: self.level(jnp.int32(k))

    def finish(self, k=0):
        at, Z, n = self.at, self.at.Z, self.n
        if k == 0: self.plane()
        lax.fori_loop(max(k, 1), Z, lambda t, _: (self.level(t), 0)[1], 0)
        def wait(i, sem):
            o = self.outs[i].at[0]
            pltpu.make_async_copy(o, o, sem).wait()
        def fin(h, _):
            self.arrive(2*h + 1 - at.c)
            s = 2*h + at.c
            level = s // (at.Y * at.KV)
            for i in range(n):
                wait(i, self.sd.at[i, h])
                @pl.when(jnp.logical_and(at.z < Z-1, level <= at.z))
                def _(): wait(i, self.sz.at[i, 0, s])
                @pl.when(jnp.logical_and(at.z > 0, level >= at.z))
                def _(): wait(i, self.sz.at[i, 1, s])
            return 0
        lax.fori_loop(0, at.KV*Z, fin, 0)
        for i in range(n):
            for sem in (self.s2.at[i, 0], self.s3.at[i, 0], self.s3.at[i, 1]): wait(i, sem)
            pltpu.make_async_copy(self.ins[i], self.outs[i].at[self.own], self.sl.at[i]).wait()

def fill_block(parts, block, sem):
    copies, offset = [], 0
    for j, part in enumerate(parts):
        copies.append(pltpu.make_async_copy(part, block.at[:, pl.ds(offset, part.shape[1])], sem.at[j]))
        offset += part.shape[1]
    for copy in copies: copy.start()
    return copies

def ag_kernel(NDP, KV, count, *refs):
    parts, outs, packs, fill = refs[:count], refs[count:count+2], refs[count+2:count+4], refs[count+4]
    copies = fill_block(parts[:-2], packs[0], fill)
    copies += fill_block(parts[-2:], packs[1], fill.at[pl.ds(count-2, 2)])
    at = place(NDP, KV)
    enter(at)
    for copy in copies: copy.wait()
    k = count+5
    plane = PlaneGather(at, [packs[1]], [outs[1]], refs[k+6:], at.split)
    gather = Gather(at, [packs[0]], [outs[0]], refs[k:k+6], at.split)
    plane.start()
    gather.start()
    plane.tick(0)
    for k in range(1, min(at.Z, 4)):
        gather.tick(k-1)
        plane.tick(k)
    gather.finish(min(at.Z, 4)-1)
    plane.finish(min(at.Z, 4))

def all_gather(parts, NDP, KV, cid):
    ND = NDP*KV
    rows = parts[0].shape[0]
    widths = [sum(p.shape[1] for p in some) for some in (parts[:-2], parts[-2:])]
    return pl.pallas_call(
        functools.partial(ag_kernel, NDP, KV, len(parts)),
        out_shape=[jax.ShapeDtypeStruct((ND, rows, width), jnp.bfloat16) for width in widths],
        in_specs=[pl.BlockSpec(memory_space=pl.ANY)]*len(parts),
        out_specs=[pl.BlockSpec(memory_space=pl.ANY)]*2,
        scratch_shapes=[pltpu.VMEM((rows, width), jnp.bfloat16) for width in widths] + [pltpu.SemaphoreType.DMA((len(parts),))]
            + Gather.sems(1, ND) + PlaneGather.sems(1, ND),
        compiler_params=pltpu.CompilerParams(collective_id=cid, has_side_effects=True, vmem_limit_bytes=60<<20),
        name="gather_weights",
    )(*parts)


class Scatter:
    count = 9

    def __init__(self, at, sources, bufs, sems, route):
        self.at, self.sources = at, sources
        self.n = n = len(bufs) // 5
        self.loc, self.r1, self.r2, self.r3, self.rz = (bufs[j*n:(j+1)*n] for j in range(5))
        self.sl, self.sd, self.qd, self.s2, self.q2, self.s3, self.q3, self.sz, self.qz = sems
        (self.y2, self.x2), (self.y3, self.x3) = route
        self.p2, self.p3 = ((at.z*at.Y+yy, 2*xx+at.c) for yy, xx in route)
        self.lines = ((at.y, at.x), (self.y2, self.x2), (self.y3, self.x3), (1-at.y, 1-at.x))

    @staticmethod
    def bufs(shapes, ND):
        Z = ND // 8
        return [pltpu.VMEM(lead + tuple(s), jnp.bfloat16)
                for lead in ((ND//2,), (ND//2,), (2*Z,), (Z,), (2, Z)) for s in shapes]

    @staticmethod
    def sems(n, ND):
        Z = ND // 8
        D = pltpu.SemaphoreType.DMA
        return [D((n, ND//2))]*3 + [D((n, 2*Z))]*2 + [D((n, Z))]*2 + [D((n, 2, Z))]*2

    def half(self, zz, yy, xx): return (zz*self.at.Y+yy)*(self.at.KV//2) + xx

    def send(self, src, dst, ss, rsem, dev):
        pltpu.make_async_remote_copy(
            src_ref=src, dst_ref=dst, send_sem=ss, recv_sem=rsem, device_id=dev, device_id_type=MESH).start()

    def wait(self, ref, sem): pltpu.make_async_copy(ref, ref, sem).wait()

    def both(self, t, f):
        at = self.at
        @pl.when(at.z >= t)
        def _(): f(at.z-t)
        @pl.when(jnp.logical_and(t > 0, at.z+t < at.Z))
        def _(): f(at.z+t)

    def every(self, f):
        Z = self.at.Z
        lax.fori_loop(0, Z, lambda k, _: (self.both(Z-1-k, f), 0)[1], 0)

    def start(self):
        c = self.at.c
        def one(zz):
            for yy, xx in self.lines[::-1]:
                h = self.half(zz, yy, xx)
                for ref, i, off, dst, width in self.sources:
                    to, cols = pl.ds(dst, width), pl.ds(off, width)
                    self.send(ref.at[2*h+1-c, :, cols], self.r1[i].at[h, :, to], self.sd.at[i, h], self.qd.at[i, h], self.at.pd)
                    pltpu.make_async_copy(ref.at[2*h+c, :, cols], self.loc[i].at[h, :, to], self.sl.at[i, h]).start()
        self.every(one)

    def pair(self, h):
        for i in range(self.n):
            self.wait(self.loc[i].at[h], self.sl.at[i, h]); self.wait(self.r1[i].at[h], self.qd.at[i, h])
            self.loc[i][h] = self.loc[i][h] + self.r1[i][h]

    def first(self):
        def one(zz):
            for j, (yy, xx) in enumerate((self.lines[3], self.lines[2])):
                h = self.half(zz, yy, xx)
                self.pair(h)
                for i in range(self.n):
                    self.send(self.loc[i].at[h], self.r2[i].at[2*zz+j], self.s2.at[i, 2*zz+j], self.q2.at[i, 2*zz+j], self.p3)
            for yy, xx in self.lines[:2]: self.pair(self.half(zz, yy, xx))
        self.every(one)

    def second(self, t):
        at, Z = self.at, self.at.Z
        def one(zz):
            for j, (yy, xx) in enumerate((self.lines[1], self.lines[0])):
                h = self.half(zz, yy, xx)
                for i in range(self.n):
                    self.wait(self.r2[i].at[2*zz+j], self.q2.at[i, 2*zz+j])
                    self.loc[i][h] = self.loc[i][h] + self.r2[i][2*zz+j]
                    if j == 0:
                        self.send(self.loc[i].at[h], self.r3[i].at[zz], self.s3.at[i, zz], self.q3.at[i, zz], self.p2)
        self.both(t, one)
        def along(zz, d, dev, has):
            h = self.half(zz, at.y, at.x)
            for i in range(self.n):
                loc, rz = self.loc[i], self.rz[i]
                self.wait(self.r3[i].at[zz], self.q3.at[i, zz])
                @pl.when(has)
                def _():
                    self.wait(rz.at[d, zz], self.qz.at[i, d, zz])
                    loc[h] = loc[h] + self.r3[i][zz] + rz[d, zz]
                @pl.when(jnp.logical_not(has))
                def _(): loc[h] = loc[h] + self.r3[i][zz]
                self.send(loc.at[h], rz.at[d, zz], self.sz.at[i, d, zz], self.qz.at[i, d, zz], dev)
        u = t + 1
        @pl.when(at.z + u < Z)
        def _(): along(at.z+u, 0, at.up, at.z > 0)
        @pl.when(at.z >= u)
        def _(): along(at.z-u, 1, at.dn, at.z < Z-1)

    def tick(self, k):
        if k == 0: self.first()
        elif k <= self.at.Z: self.second(jnp.int32(self.at.Z-k))

    def rest(self, k):
        Z = self.at.Z
        if k == 0: self.first()
        lax.fori_loop(max(k, 1), Z+1, lambda j, _: (self.second(Z-j), 0)[1], 0)

    def finish(self, k, outs):
        at, Z, z = self.at, self.at.Z, self.at.z
        self.rest(k)
        h = self.half(z, at.y, at.x)
        for i, out in enumerate(outs):
            self.wait(self.r3[i].at[z], self.q3.at[i, z])
            out[...] = self.loc[i][h].astype(jnp.float32) + self.r3[i][z].astype(jnp.float32)
            for d, has in ((0, z > 0), (1, z < Z-1)):
                @pl.when(has)
                def _():
                    self.wait(self.rz[i].at[d, z], self.qz.at[i, d, z])
                    out[...] += self.rz[i][d, z].astype(jnp.float32)
        def fin(h, _):
            for i in range(self.n): self.wait(self.r1[i].at[h], self.sd.at[i, h])
            return 0
        lax.fori_loop(0, at.KV*Z, fin, 0)
        def fin2(zz, _):
            for i in range(self.n):
                self.wait(self.r3[i].at[zz], self.s3.at[i, zz])
                for j in range(2): self.wait(self.r2[i].at[2*zz+j], self.s2.at[i, 2*zz+j])
                @pl.when(zz > z)
                def _(): self.wait(self.rz[i].at[0, zz], self.sz.at[i, 0, zz])
                @pl.when(zz < z)
                def _(): self.wait(self.rz[i].at[1, zz], self.sz.at[i, 1, zz])
            return 0
        lax.fori_loop(0, Z, fin2, 0)

class PlaneScatter(Scatter):
    @staticmethod
    def bufs(shapes, ND):
        Z = ND // 8
        return [pltpu.VMEM(lead + tuple(s), jnp.bfloat16)
                for lead in ((ND//2,), (ND//2,), (2,), (1,), (2, 4*Z)) for s in shapes]

    @staticmethod
    def sems(n, ND):
        Z = ND // 8
        D = pltpu.SemaphoreType.DMA
        return [D((n, ND//2))]*3 + [D((n, 2))]*2 + [D((n, 1))]*2 + [D((n, 2, 4*Z))]*2

    def chain(self, t):
        at, Z = self.at, self.at.Z
        def along(zz, d, dev, has):
            for l, (yy, xx) in enumerate(self.lines):
                h = self.half(zz, yy, xx)
                k = 4*zz + l
                self.pair(h)
                for i in range(self.n):
                    loc, rz = self.loc[i], self.rz[i]
                    @pl.when(has)
                    def _():
                        self.wait(rz.at[d, k], self.qz.at[i, d, k])
                        loc[h] = loc[h] + rz[d, k]
                    self.send(loc.at[h], rz.at[d, k], self.sz.at[i, d, k], self.qz.at[i, d, k], dev)
        @pl.when(at.z + t < Z)
        def _(): along(at.z+t, 0, at.up, at.z > 0)
        @pl.when(at.z >= t)
        def _(): along(at.z-t, 1, at.dn, at.z < Z-1)

    def level(self):
        at, z = self.at, self.at.z
        for l, (yy, xx) in reversed(list(enumerate(self.lines))):
            h = self.half(z, yy, xx)
            k = 4*z + l
            self.pair(h)
            for i in range(self.n):
                loc, rz = self.loc[i], self.rz[i]
                for d, has in ((0, z > 0), (1, z < at.Z-1)):
                    @pl.when(has)
                    def _():
                        self.wait(rz.at[d, k], self.qz.at[i, d, k])
                        loc[h] = loc[h] + rz[d, k]
                if l >= 2:
                    self.send(loc.at[h], self.r2[i].at[3-l], self.s2.at[i, 3-l], self.q2.at[i, 3-l], self.p3)

    def plane(self):
        for j, (yy, xx) in enumerate((self.lines[1], self.lines[0])):
            h = self.half(self.at.z, yy, xx)
            for i in range(self.n):
                self.wait(self.r2[i].at[j], self.q2.at[i, j])
                self.loc[i][h] = self.loc[i][h] + self.r2[i][j]
                if j == 0: self.send(self.loc[i].at[h], self.r3[i].at[0], self.s3.at[i, 0], self.q3.at[i, 0], self.p2)

    def tick(self, k):
        Z = self.at.Z
        if k < Z-1: self.chain(jnp.int32(Z-1-k))
        elif k == Z-1: self.level()
        elif k == Z: self.plane()

    def finish(self, k, outs):
        at, Z, z = self.at, self.at.Z, self.at.z
        lax.fori_loop(min(k, Z-1), Z-1, lambda j, _: (self.chain(Z-1-j), 0)[1], 0)
        if k <= Z-1: self.level()
        if k <= Z: self.plane()
        h = self.half(z, at.y, at.x)
        for i, out in enumerate(outs):
            self.wait(self.r3[i].at[0], self.q3.at[i, 0])
            out[...] = self.loc[i][h].astype(jnp.float32) + self.r3[i][0].astype(jnp.float32)
        def fin(h, _):
            zz = h // (at.Y * at.KV // 2)
            for i in range(self.n):
                self.wait(self.r1[i].at[h], self.sd.at[i, h])
                for d, cond in ((0, zz > z), (1, zz < z)):
                    @pl.when(cond)
                    def _(): self.wait(self.rz[i].at[d, h], self.sz.at[i, d, h])
            return 0
        lax.fori_loop(0, at.KV*Z, fin, 0)
        for i in range(self.n):
            self.wait(self.r3[i].at[0], self.s3.at[i, 0])
            for j in range(2): self.wait(self.r2[i].at[j], self.s2.at[i, j])

def rs_kernel(NDP, KV, count, *refs):
    parts, outs, k = refs[:count], refs[count:count+2], count+2
    at = place(NDP, KV)
    enter(at)
    def sources(some):
        found, offset = [], 0
        for ref in some:
            found.append((ref, 0, 0, offset, ref.shape[2]))
            offset += ref.shape[2]
        return found
    plane = PlaneScatter(at, sources(parts[-2:]), refs[k:k+5], refs[k+5:k+14], at.split)
    scatter = Scatter(at, sources(parts[:-2]), refs[k+14:k+19], refs[k+19:], at.split)
    plane.start()
    scatter.start()
    last = min(at.Z, 4)
    for j in range(last):
        plane.tick(j)
        scatter.tick(j)
    plane.finish(last, outs[1:])
    scatter.finish(last, outs[:1])

def blocks(g, ND): return g.reshape(ND, g.shape[0]//ND, g.shape[1])

def reduce_scatter(grads, NDP, KV, cid):
    ND = NDP*KV
    parts = [blocks(g, ND) for g in grads]
    rows = parts[0].shape[1]
    shapes = [(rows, sum(g.shape[2] for g in some)) for some in (parts[:-2], parts[-2:])]
    return pl.pallas_call(
        functools.partial(rs_kernel, NDP, KV, len(parts)),
        out_shape=[jax.ShapeDtypeStruct(s, jnp.float32) for s in shapes],
        in_specs=[pl.BlockSpec(memory_space=pl.ANY)]*len(parts),
        out_specs=[pl.BlockSpec(memory_space=pltpu.VMEM)]*2,
        scratch_shapes=PlaneScatter.bufs(shapes[1:], ND) + PlaneScatter.sems(1, ND) + Scatter.bufs(shapes[:1], ND) + Scatter.sems(1, ND),
        compiler_params=pltpu.CompilerParams(collective_id=cid, has_side_effects=True, vmem_limit_bytes=60<<20),
        name="scatter_gradients",
    )(*parts)


D = 768
FF = 3072
HEADS = 12
HD = 64
SEQ = 64
QUAD = 4 * HD
EPS = 1e-05
NEG = -1e30
GELU_C = 0.7978845608028654
GELU_A = 0.044715
SCALE = 0.125
BF = jnp.bfloat16
F32 = jnp.float32
VM = pl.BlockSpec(memory_space=pltpu.VMEM)
ANY = pl.BlockSpec(memory_space=pl.ANY)
DMA = pltpu.SemaphoreType.DMA


def nn(a, b):
    return lax.dot_general(a, b, (((1,), (0,)), ((), ())), preferred_element_type=F32)


def nt(a, b):
    return lax.dot_general(a, b, (((1,), (1,)), ((), ())), preferred_element_type=F32)


def tn(a, b):
    return lax.dot_general(a, b, (((0,), (0,)), ((), ())), preferred_element_type=F32)


def unit_of(values):
    centre = values - jnp.mean(values, -1, keepdims=True)
    scaled = lax.rsqrt(jnp.mean(centre * centre, -1, keepdims=True) + EPS)
    return centre * scaled, scaled


def norm_backward(upstream, unit, scaled, gain):
    through = upstream * gain
    return scaled * (
        through - jnp.mean(through, -1, keepdims=True) - unit * jnp.mean(through * unit, -1, keepdims=True)
    )


def head_masks(width):
    lane = lax.broadcasted_iota(jnp.int32, (1, width), 1) // HD
    return [(lane == head).astype(F32).astype(BF) for head in range(width // HD)]


def stacked(values, masks):
    return jnp.concatenate([values * mask for mask in masks], 0)


def own_blocks(values):
    lane = lax.broadcasted_iota(jnp.int32, (HD, QUAD), 1) // HD
    total = values[:HD]
    for head in range(1, 4):
        total = jnp.where(lane == head, values[head * HD : (head + 1) * HD], total)
    return total


def load(source, target, sem):
    return pltpu.make_async_copy(source, target, sem)


def call(kernel, name, outs, ins, specs, scratch, flops, out_specs=None, cid=None, limit=56 << 20):
    params = dict(vmem_limit_bytes=limit)
    if cid is not None:
        params.update(collective_id=cid, has_side_effects=True)
    size = lambda a: a.size * a.dtype.itemsize
    return pl.pallas_call(
        kernel,
        out_shape=outs,
        in_specs=specs,
        out_specs=out_specs or [VM] * len(outs),
        scratch_shapes=scratch,
        compiler_params=pltpu.CompilerParams(**params),
        cost_estimate=pl.CostEstimate(flops=int(flops), transcendentals=0, bytes_accessed=sum(map(size, ins)) + sum(map(size, outs))),
        name=name,
    )(*ins)


def arr(shape, dtype=BF):
    return jax.ShapeDtypeStruct(shape, dtype)


def text_forward_kernel(text, packed, tail, h1, q1, k1, v1, p1, c1, x2, h2, q2, gains, w, gw, sem):
    weights = [load(packed.at[:, pl.ds(j * D, D)], w.at[j], sem.at[j]) for j in range(5)]
    gcopy = load(tail.at[:, pl.ds(D, 128)], gw, sem.at[5])
    gcopy.start()
    for copy in weights:
        copy.start()
    x = text[...].astype(F32)
    unit, _ = unit_of(x)
    gcopy.wait()
    gains[...] = gw[...].astype(F32).T[:8]
    h1[...] = (unit * gains[0:1]).astype(BF)
    for j, ref in enumerate((q1, k1, v1)):
        weights[j].wait()
        ref[...] = nn(h1[...], w[j]).astype(BF)
    rows = text.shape[0]
    first = lax.broadcasted_iota(jnp.int32, (rows, rows), 0)
    second = lax.broadcasted_iota(jnp.int32, (rows, rows), 1)
    allowed = jnp.logical_and(first >= second, first // SEQ == second // SEQ)
    masks = head_masks(128)
    for pair in range(HEADS // 2):
        lanes = slice(pair * 128, (pair + 1) * 128)
        total = None
        for j, mask in enumerate(masks):
            scores = nt(q1[:, lanes] * mask, k1[:, lanes]) * SCALE
            scores = jnp.where(allowed, scores, NEG)
            powers = jnp.exp(scores - jnp.max(scores, -1, keepdims=True))
            probs = (powers / jnp.sum(powers, -1, keepdims=True)).astype(BF)
            p1[2 * pair + j] = probs
            part = nn(probs, v1[:, lanes] * mask)
            total = part if total is None else total + part
        c1[:, lanes] = total.astype(BF)
    weights[3].wait()
    second_res = x + nn(c1[...], w[3])
    x2[...] = second_res
    unit, _ = unit_of(second_res)
    h2[...] = (unit * gains[1:2]).astype(BF)
    weights[4].wait()
    q2[...] = nn(h2[...], w[4]).astype(BF)


def text_forward(text, packed, tail):
    rows = text.shape[0]
    low = arr((rows, D))
    return call(
        text_forward_kernel, "text_forward",
        [low, low, low, low, arr((HEADS, rows, rows)), low, arr((rows, D), F32), low, low, arr((8, D), F32)],
        [text, packed, tail], [VM, ANY, ANY],
        [pltpu.VMEM((5, D, D), BF), pltpu.VMEM((D, 128), BF), DMA((6,))], 10 * rows * D * D)


TICKS = (3, 6, 8, 10)


def remote(src, dst, send, recv, device):
    return pltpu.make_async_remote_copy(
        src_ref=src, dst_ref=dst, send_sem=send, recv_sem=recv, device_id=device, device_id_type=MESH)


def cross_forward_kernel(NDP, KV, q2, image, lengths, patches, packed, tail, out_part, up_part, down_part,
                         c2, lse, keys, vals, e, stats, qall, second, third, down, w, obuf, ro, rst, usable, block, wide, down_block,
                         wsem, ssem, rsem, fsem, *gsems):
    at = place(NDP, KV)
    di, ki, x, c = at.di, at.ki, at.x, at.c
    caps, tokens = patches.shape
    own_caps = caps // 4
    fills = fill_block([out_part, up_part.at[:, pl.ds(0, D)]], block, fsem)
    fills += [load(down_part, down_block, fsem.at[2]), load(up_part.at[:, pl.ds(D, FF - D)], wide, fsem.at[3])]
    for copy in fills[2:]:
        copy.start()
    core, over, diag = 2 * x + 1 - c, 2 * (1 - x) + c, 2 * (1 - x) + 1 - c
    weights = [load(packed.at[:, pl.ds(5 * D, D)], w.at[0], wsem.at[0]), load(tail.at[:, pl.ds(0, D)], w.at[1], wsem.at[1])]
    for copy in weights:
        copy.start()
    own_copy = load(q2, qall.at[ki], wsem.at[2])
    own_copy.start()
    enter(at, True)
    to_core = remote(q2, qall.at[ki], ssem.at[0], rsem.at[ki], (di, core))
    to_over = remote(q2, qall.at[ki], ssem.at[1], rsem.at[ki], (di, over))
    for copy in fills:
        copy.wait()
    plane = PlaneGather(at, [wide], [third], gsems[6:], at.fixed)
    gather = Gather(at, [block, down_block], [second, down], gsems[:6], at.fixed)
    plane.start()
    gather.start()
    to_over.start()
    to_core.start()
    row = lax.broadcasted_iota(jnp.int32, usable.shape, 0)
    limit = jnp.zeros(usable.shape, jnp.int32)
    for cap in range(caps):
        limit = jnp.where(row == cap, lengths[cap], limit)
    position = lax.broadcasted_iota(jnp.int32, usable.shape, 1) + ki * tokens
    usable[...] = jnp.zeros(usable.shape, BF)
    usable[0:caps, :] = jnp.where(jnp.logical_and(position < limit, True)[0:caps], (patches[...] == 1).astype(F32), 0.0).astype(BF)
    weights[0].wait()

    def project(j, ref, i):
        rows = pl.ds(pl.multiple_of(i * tokens, 16), tokens)
        ref[rows, :] = nn(image[rows, :], w[j]).astype(BF)

    lax.fori_loop(0, caps, lambda i, _: (project(0, keys, i), 0)[1], 0)
    load(qall.at[over], qall.at[over], rsem.at[over]).wait()
    relay = remote(qall.at[over], qall.at[over], ssem.at[2], rsem.at[over], (di, core))
    relay.start()
    plane.tick(0)
    gather.tick(0)
    weights[1].wait()
    lax.fori_loop(0, caps, lambda i, _: (project(1, vals, i), 0)[1], 0)
    plane.tick(1)
    gather.tick(1)
    load(qall.at[core], qall.at[core], rsem.at[core]).wait()
    load(qall.at[diag], qall.at[diag], rsem.at[diag]).wait()
    own_copy.wait()
    masks = head_masks(QUAD)

    def owner_of(step):
        return 2 * ((x + 1 + step // 2) % 2) + (c + 1 + step % 2) % 2

    def attend(i, _):
        owner, local = owner_of(i // own_caps), i % own_caps
        cap = owner * own_caps + local
        rows = pl.ds(pl.multiple_of(cap * tokens, 16), tokens)
        queries = pl.ds(pl.multiple_of(local * SEQ, 16), SEQ)
        for j, when in enumerate(TICKS):
            @pl.when(i == when * caps // 12)
            def _():
                plane.tick(2 + j)
                gather.tick(2 + j)
        chosen = (lax.broadcasted_iota(jnp.int32, (usable.shape[0], QUAD), 0) == cap).astype(F32).astype(BF)
        shift = tn(usable[...], chosen)
        for g in range(3):
            lanes = slice(g * QUAD, (g + 1) * QUAD)
            scores = nt(keys[rows, lanes], stacked(qall[owner, queries, lanes], masks)) * SCALE
            scores = jnp.where(shift > 0.5, scores, NEG)
            top = jnp.max(scores, 0, keepdims=True)
            powers = jnp.where(shift > 0.5, jnp.exp(scores - top), 0.0)
            low = powers.astype(BF)
            e[pl.ds(pl.multiple_of((cap * 3 + g) * tokens, 16), tokens), :] = low
            stats[owner, pl.ds(3 * local + g, 1), :] = top
            stats[owner, pl.ds(16 + 3 * local + g, 1), :] = jnp.sum(powers, 0, keepdims=True)
            obuf[owner, queries, lanes] = own_blocks(tn(low, vals[rows, lanes])).astype(BF)

        @pl.when(jnp.logical_and(local == own_caps - 1, owner != ki))
        def _():
            remote(obuf.at[owner], ro.at[ki], ssem.at[3 + owner], rsem.at[4 + ki], (di, owner)).start()
            remote(stats.at[owner], rst.at[ki], ssem.at[7 + owner], rsem.at[8 + ki], (di, owner)).start()

        return 0

    lax.fori_loop(0, caps, attend, 0)
    ro[ki] = obuf[ki]
    rst[ki] = stats[ki]
    for other in (core, over, diag):
        load(ro.at[other], ro.at[other], rsem.at[4 + other]).wait()
        load(rst.at[other], rst.at[other], rsem.at[8 + other]).wait()
    lane = lax.broadcasted_iota(jnp.int32, (HD, QUAD), 1) // HD

    def combine(local, _):
        queries = pl.ds(pl.multiple_of(local * SEQ, 16), SEQ)
        for g in range(3):
            row = pl.ds(3 * local + g, 1)
            row_sum = pl.ds(16 + 3 * local + g, 1)
            tops = [rst[k, row, :] for k in range(4)]
            top = jnp.maximum(jnp.maximum(tops[0], tops[1]), jnp.maximum(tops[2], tops[3]))
            parts = [jnp.exp(t - top) for t in tops]
            total = sum(part * rst[k, row_sum, :] for k, part in enumerate(parts))
            lse[row, :] = top + jnp.log(total)
            table = jnp.concatenate([part / total for part in parts] * 2, 0).T
            mixed = 0.0
            for k in range(4):
                column = table[:, k : k + 1]
                weight = column[:HD] * jnp.ones((HD, QUAD), F32)
                for head in range(1, 4):
                    weight = jnp.where(lane == head, column[head * HD : (head + 1) * HD], weight)
                mixed = mixed + weight * ro[k, queries, g * QUAD : (g + 1) * QUAD].astype(F32)
            c2[queries, g * QUAD : (g + 1) * QUAD] = mixed
        return 0

    lax.fori_loop(0, own_caps, combine, 0)
    to_core.wait_send()
    to_over.wait_send()
    relay.wait_send()
    for other in (core, over, diag):
        load(obuf.at[other], obuf.at[other], ssem.at[3 + other]).wait()
        load(stats.at[other], stats.at[other], ssem.at[7 + other]).wait()
    plane.finish(2 + len(TICKS))
    gather.finish(2 + len(TICKS))


def cross_forward(q2, image, lengths, patches, packed, tail, out_part, up_part, down_part, NDP, KV, cid):
    rows, (caps, tokens), ND = q2.shape[0], patches.shape, NDP * KV
    lows = out_part.shape[0]
    return call(
        functools.partial(cross_forward_kernel, NDP, KV), "cross_forward",
        [arr((rows, D), F32), arr((16, QUAD), F32), arr((caps * tokens, D)), arr((caps * tokens, D)),
         arr((caps * 3 * tokens, QUAD)), arr((4, 32, QUAD), F32), arr((4, rows, D)),
         arr((ND, lows, 2 * D)), arr((ND, lows, FF - D)), arr((ND,) + down_part.shape)],
        [q2, image, lengths, patches, packed, tail, out_part, up_part, down_part],
        [VM, VM, pl.BlockSpec(memory_space=pltpu.SMEM), VM, ANY, ANY, ANY, ANY, ANY],
        [pltpu.VMEM((2, D, D), BF), pltpu.VMEM((4, rows, D), BF), pltpu.VMEM((4, rows, D), BF),
         pltpu.VMEM((4, 32, QUAD), F32), pltpu.VMEM((-(-caps // 16) * 16, tokens), BF),
         pltpu.VMEM((lows, 2 * D), BF), pltpu.VMEM((lows, FF - D), BF), pltpu.VMEM(down_part.shape, BF),
         DMA((3,)), DMA((11,)), DMA((12,)), DMA((4,))] + Gather.sems(2, ND) + PlaneGather.sems(1, ND),
        4 * caps * tokens * D * D, out_specs=[VM] * 7 + [ANY] * 3, cid=cid)


BACK_TICKS = (4, 9)


def cross_backward_kernel(NDP, KV, dc2, c2, lse, stats, qall, keys, vals, e, image, packed, tail, dco, dup, ddown,
                          dq2, wk, wv, igrad, sum_a, sum_b, sum_c, dk, dv, w, ibuf,
                          dall, sall, qbuf, rq, csem, wsem, isem, ssem, rsem, *more):
    at = place(NDP, KV)
    di, ki, x, c = at.di, at.ki, at.x, at.c
    weights = [load(packed.at[:, pl.ds(5 * D, D)], w.at[0], wsem.at[0]), load(tail.at[:, pl.ds(0, D)], w.at[1], wsem.at[1])]
    for copy in weights:
        copy.start()
    rows_all = keys.shape[0]
    caps = 4 * (dc2.shape[0] // SEQ)
    own_caps = caps // 4
    tokens = rows_all // caps
    core, over, diag = 2 * x + 1 - c, 2 * (1 - x) + c, 2 * (1 - x) + 1 - c
    masks = head_masks(QUAD)
    sall[ki, 0:16, :] = lse[...]

    def dots(local, _):
        queries = pl.ds(pl.multiple_of(local * SEQ, 16), SEQ)
        for g in range(3):
            lanes = slice(g * QUAD, (g + 1) * QUAD)
            product = dc2[queries, lanes].astype(F32) * c2[queries, lanes]
            product = jnp.concatenate([product * mask.astype(F32) for mask in masks], 0)
            sums = lax.dot_general(
                jnp.ones((8, QUAD), F32), product, (((1,), (1,)), ((), ())),
                preferred_element_type=F32, precision=lax.Precision.HIGHEST)
            sall[ki, pl.ds(16 + 3 * local + g, 1), :] = sums[0:1]
        return 0

    own_copy = load(dc2, dall.at[ki], csem)
    own_copy.start()
    enter(at, True)
    plane = PlaneScatter(at, [(dup, 0, D, 0, FF - D)], more[0:5], more[5:14], at.fixed)
    scatter = Scatter(at, [(dco, 0, 0, 0, D), (dup, 0, 0, D, D), (ddown, 1, 0, 0, D)], more[14:24], more[24:], at.fixed)
    to_over = remote(dc2, dall.at[ki], ssem.at[1], rsem.at[ki], (di, over))
    to_core = remote(dc2, dall.at[ki], ssem.at[0], rsem.at[ki], (di, core))
    to_over.start()
    to_core.start()
    plane.start()
    scatter.start()
    lax.fori_loop(0, own_caps, dots, 0)
    small = [remote(sall.at[ki], sall.at[ki], ssem.at[2 + j], rsem.at[4 + ki], (di, other))
             for j, other in enumerate((core, over, diag))]
    for copy in small:
        copy.start()
    own_copy.wait()
    plane.tick(0)
    scatter.tick(0)
    relay = remote(dall.at[over], dall.at[over], ssem.at[5], rsem.at[over], (di, core))

    def attend(i, _):
        step, local = i // own_caps, i % own_caps
        owner = 2 * ((x + step // 2) % 2) + (c + step % 2) % 2

        @pl.when(i == own_caps)
        def _():
            load(dall.at[core], dall.at[core], rsem.at[core]).wait()
            load(sall.at[core], sall.at[core], rsem.at[4 + core]).wait()

        @pl.when(i == 2 * own_caps - 1)
        def _():
            load(dall.at[over], dall.at[over], rsem.at[over]).wait()
            relay.start()

        @pl.when(i == 2 * own_caps)
        def _():
            load(sall.at[over], sall.at[over], rsem.at[4 + over]).wait()

        @pl.when(i == 3 * own_caps)
        def _():
            load(dall.at[diag], dall.at[diag], rsem.at[diag]).wait()
            load(sall.at[diag], sall.at[diag], rsem.at[4 + diag]).wait()

        for j, when in enumerate(BACK_TICKS):
            @pl.when(i == when * caps // 12)
            def _():
                plane.tick(1 + j)
                scatter.tick(1 + j)

        cap = owner * own_caps + local
        rows = pl.ds(pl.multiple_of(cap * tokens, 16), tokens)
        queries = pl.ds(pl.multiple_of(local * SEQ, 16), SEQ)
        for g in range(3):
            lanes = slice(g * QUAD, (g + 1) * QUAD)
            factor = jnp.exp(stats[owner, pl.ds(3 * local + g, 1), :] - sall[owner, pl.ds(3 * local + g, 1), :])
            dots_row = sall[owner, pl.ds(16 + 3 * local + g, 1), :]
            probs = e[pl.ds(pl.multiple_of((cap * 3 + g) * tokens, 16), tokens), :].astype(F32) * factor
            upstream = stacked(dall[owner, queries, lanes], masks)
            queried = stacked(qall[owner, queries, lanes], masks)
            grad = nt(vals[rows, lanes], upstream)
            grad = (probs * (grad - dots_row)).astype(BF)
            dv[rows, lanes] = nn(probs.astype(BF), upstream).astype(BF)
            dk[rows, lanes] = (nn(grad, queried) * SCALE).astype(BF)
            qbuf[owner, queries, lanes] = (own_blocks(tn(grad, keys[rows, lanes])) * SCALE).astype(BF)

        @pl.when(jnp.logical_and(local == own_caps - 1, owner != ki))
        def _():
            remote(qbuf.at[owner], rq.at[ki], ssem.at[6 + owner], rsem.at[8 + ki], (di, owner)).start()

        return 0

    lax.fori_loop(0, caps, attend, 0)

    def weight(j, _):
        cols = pl.ds(pl.multiple_of(j * 256, 256), 256)
        flipped = image[:, cols].T
        wk[cols, :] = nn(flipped, dk[...]).astype(BF)
        wv[cols, :] = nn(flipped, dv[...]).astype(BF)
        return 0

    lax.fori_loop(0, D // 256, weight, 0)
    ticks = 1 + len(BACK_TICKS)
    plane.tick(ticks)
    scatter.tick(ticks)
    for copy in weights:
        copy.wait()

    def flush(i):
        return load(ibuf.at[i % 2], igrad.at[pl.ds(pl.multiple_of(i * tokens, 16), tokens), :], isem.at[i % 2])

    def image_rows(i, _):
        @pl.when(i >= 2)
        def _():
            flush(i - 2).wait()

        rows = pl.ds(pl.multiple_of(i * tokens, 16), tokens)
        ibuf[i % 2] = nt(dk[rows, :], w[0]) + nt(dv[rows, :], w[1])
        flush(i).start()
        return 0

    lax.fori_loop(0, caps, image_rows, 0)
    plane.tick(ticks + 1)
    scatter.tick(ticks + 1)
    rq[ki] = qbuf[ki]
    for other in (core, over, diag):
        load(rq.at[other], rq.at[other], rsem.at[8 + other]).wait()
    dq2[...] = (rq[0].astype(F32) + rq[1].astype(F32) + rq[2].astype(F32) + rq[3].astype(F32)).astype(BF)
    to_core.wait_send()
    to_over.wait_send()
    relay.wait_send()
    for copy in small:
        copy.wait_send()
    for other in (core, over, diag):
        load(qbuf.at[other], qbuf.at[other], ssem.at[6 + other]).wait()
    flush(caps - 2).wait()
    flush(caps - 1).wait()
    plane.finish(ticks + 2, [sum_c])
    scatter.finish(ticks + 2, [sum_a, sum_b])


def cross_backward(dc2, c2, lse, stats, qall, keys, vals, e, image, packed, tail, dco, dup, ddown, NDP, KV, cid):
    rows, ND = dc2.shape[0], NDP * KV
    caps = 4 * (rows // SEQ)
    dco, dup, ddown = blocks(dco, ND), blocks(dup, ND), blocks(ddown, ND)
    ins = [dc2, c2, lse, stats, qall, keys, vals, e, image, packed, tail, dco, dup, ddown]
    low = dco.shape[1]
    shapes = [(low, 2 * D), ddown.shape[1:], (low, FF - D)]
    return call(
        functools.partial(cross_backward_kernel, NDP, KV), "cross_backward",
        [arr((rows, D)), arr((D, D)), arr((D, D)), arr(keys.shape, F32)] + [arr(s, F32) for s in shapes],
        ins, [VM] * 9 + [ANY] * 5,
        [pltpu.VMEM(keys.shape, BF), pltpu.VMEM(keys.shape, BF), pltpu.VMEM((2, D, D), BF),
         pltpu.VMEM((2, keys.shape[0] // caps, D), F32),
         pltpu.VMEM((4, rows, D), BF), pltpu.VMEM((4, 32, QUAD), F32), pltpu.VMEM((4, rows, D), BF),
         pltpu.VMEM((4, rows, D), BF), DMA, DMA((2,)), DMA((2,)), DMA((10,)), DMA((12,))]
        + PlaneScatter.bufs(shapes[2:], ND) + PlaneScatter.sems(1, ND) + Scatter.bufs(shapes[:2], ND) + Scatter.sems(2, ND),
        4 * keys.shape[0] * D * D, out_specs=[VM] * 3 + [ANY] + [VM] * 3, cid=cid, limit=62 << 20)


def mlp_kernel(c2, x2, grad, gains, packed, wide, down, out, dx3, dc2, dup, ddown, dco, ng, wu, wd, wc, dh, acc, ht, sem):
    wcopy = load(packed.at[:, pl.ds(0, D)], wc, sem.at[8])
    wcopy.start()
    ups = [load(packed.at[:, pl.ds(D, D)] if j == 0 else wide.at[:, pl.ds((j - 1) * D, D)], wu.at[j], sem.at[j]) for j in range(4)]
    downs = [load(down.at[pl.ds(j * D, D), :], wd.at[j], sem.at[4 + j]) for j in range(4)]
    for j in range(4):
        ups[j].start()
        downs[j].start()
    low = c2[...].astype(BF)
    wcopy.wait()
    third = x2[...] + nn(low, wc[...])
    unit, scaled = unit_of(third)
    gain = gains[2:3]
    h3 = (unit * gain).astype(BF)
    ht[...] = h3.T
    g = grad[...]
    acc[...] = third
    for j in range(4):
        ups[j].wait()
        downs[j].wait()
        u = nn(h3, wu[j])
        square = u * u
        tanh_part = jnp.tanh(GELU_C * (u + GELU_A * square * u))
        active = (0.5 * u * (1.0 + tanh_part)).astype(BF)
        slope = 0.5 * (1.0 + tanh_part) + 0.5 * u * (1.0 - tanh_part * tanh_part) * GELU_C * (1.0 + 3.0 * GELU_A * square)
        acc[...] += nn(active, wd[j])
        du = (nt(g, wd[j]) * slope).astype(BF)
        part = nt(du, wu[j])
        dh[...] = part if j == 0 else dh[...] + part
        ddown[pl.ds(j * D, D), :] = tn(active, g).astype(BF)
        dup[:, pl.ds(j * D, D)] = nn(ht[...], du).astype(BF)
    out[...] = acc[...].astype(BF)
    upstream = dh[...]
    ng[...] = jnp.broadcast_to(jnp.sum(upstream * unit, 0, keepdims=True), ng.shape)
    total = g.astype(F32) + norm_backward(upstream, unit, scaled, gain)
    dx3[...] = total
    branch = total.astype(BF)
    dc2[...] = nt(branch, wc[...]).astype(BF)
    dco[...] = tn(low, branch).astype(BF)


def mlp(c2, x2, grad, gains, packed, wide, down):
    rows = c2.shape[0]
    return call(
        mlp_kernel, "feed_forward",
        [arr((rows, D)), arr((rows, D), F32), arr((rows, D)), arr((D, FF)), arr((FF, D)), arr((D, D)), arr((8, D), F32)],
        [c2, x2, grad, gains, packed, wide, down], [VM] * 4 + [ANY] * 3,
        [pltpu.VMEM((4, D, D), BF), pltpu.VMEM((4, D, D), BF), pltpu.VMEM((D, D), BF), pltpu.VMEM((rows, D), F32),
         pltpu.VMEM((rows, D), F32), pltpu.VMEM((D, rows), BF), DMA((9,))], 12 * rows * D * FF)


def deliver_kernel(moves, gain, *refs):
    sources, outs, sem = refs[: -len(moves[0]) - 2], refs[-len(moves[0]) - 2 : -2], refs[-1]
    norms = refs[-2]
    copies = []
    for (i, offset, width, j, to) in moves[1]:
        copies.append(load(sources[i].at[:, pl.ds(offset, width)], outs[j].at[:, pl.ds(to, width)], sem.at[len(copies)]))
    for copy in copies:
        copy.start()
    i, offset = gain
    block = sources[i][:, offset : offset + 128]
    block = jnp.concatenate([block, jnp.zeros((128 - block.shape[0], 128), F32)], 0)
    norms[...] = block.T[:8]
    for copy in copies:
        copy.wait()


def deliver(sources, widths, copies, gain):
    outs = [arr((rows, width), F32) for rows, width in widths]
    return call(
        functools.partial(deliver_kernel, (widths, copies), gain), "deliver_gradients",
        outs + [arr((8, 128), F32)], sources, [VM] * len(sources),
        [DMA((len(copies),))], 1, out_specs=[ANY] * len(outs) + [VM], limit=60 << 20)


def text_backward_kernel(dq2, dx3, text, x2, h1, h2, c1, q1, k1, v1, p1, gains, ng3, packed, igrad,
                         text_grad, wq, wk, wv, wo, wcq, ngs, image_out, w, dq, dk, dv, rows_t, moved, sem, msem):
    size = igrad.shape[0] // 6
    pieces = [pl.ds(j * size, size) for j in range(6)]
    inward = [load(igrad.at[rows, :], moved.at[rows, :], msem.at[j]) for j, rows in enumerate(pieces)]
    outward = [load(moved.at[rows, :], image_out.at[rows, :], msem.at[j]) for j, rows in enumerate(pieces)]
    weights = [load(packed.at[:, pl.ds(j * D, D)], w.at[j], sem.at[j]) for j in range(5)]
    for j in (4, 3, 0, 1, 2):
        weights[j].start()
    for copy in inward:
        copy.start()
    unit, scaled = unit_of(x2[...])
    weights[4].wait()
    upstream = nt(dq2[...], w[4])
    ngs_two = jnp.sum(upstream * unit, 0, keepdims=True)
    grad_two = dx3[...] + norm_backward(upstream, unit, scaled, gains[1:2])
    wcq[...] = tn(h2[...], dq2[...]).astype(BF)
    branch = grad_two.astype(BF)
    weights[3].wait()
    dc1 = nt(branch, w[3]).astype(BF)
    wo[...] = tn(c1[...], branch).astype(BF)
    for there, back in zip(inward, outward):
        there.wait()
        back.start()
    masks = head_masks(128)
    for pair in range(HEADS // 2):
        lanes = slice(pair * 128, (pair + 1) * 128)
        sums = [None] * 3
        for j, mask in enumerate(masks):
            low = p1[2 * pair + j]
            probs = low.astype(F32)
            above = dc1[:, lanes] * mask
            grad = nt(above, v1[:, lanes])
            grad = (probs * (grad - jnp.sum(probs * grad, -1, keepdims=True))).astype(BF)
            parts = [nn(grad, k1[:, lanes] * mask), tn(grad, q1[:, lanes] * mask), tn(low, above)]
            sums = parts if j == 0 else [a + b for a, b in zip(sums, parts)]
        dq[:, lanes] = (sums[0] * SCALE).astype(BF)
        dk[:, lanes] = (sums[1] * SCALE).astype(BF)
        dv[:, lanes] = sums[2].astype(BF)
    upstream = None
    flipped = h1[...].T
    for j, (ref, out) in enumerate(((dq, wq), (dk, wk), (dv, wv))):
        weights[j].wait()
        part = nt(ref[...], w[j])
        upstream = part if j == 0 else upstream + part
        out[...] = nn(flipped, ref[...]).astype(BF)
    unit, scaled = unit_of(text[...].astype(F32))
    text_grad[...] = grad_two + norm_backward(upstream, unit, scaled, gains[0:1])
    rows_t[...] = jnp.zeros_like(rows_t)
    rows_t[0:1] = jnp.sum(upstream * unit, 0, keepdims=True)
    rows_t[1:2] = ngs_two
    rows_t[2:3] = ng3[0:1]
    ngs[...] = rows_t[...].T.astype(BF)
    for copy in outward:
        copy.wait()


def text_backward(dq2, dx3, text, x2, h1, h2, c1, q1, k1, v1, p1, gains, ng3, packed, igrad):
    rows = text.shape[0]
    ins = [dq2, dx3, text, x2, h1, h2, c1, q1, k1, v1, p1, gains, ng3, packed, igrad]
    return call(
        text_backward_kernel, "text_backward",
        [arr((rows, D), F32)] + [arr((D, D))] * 5 + [arr((D, 128)), arr(igrad.shape, F32)],
        ins, [VM] * 13 + [ANY] * 2,
        [pltpu.VMEM((5, D, D), BF)] + [pltpu.VMEM((rows, D), BF)] * 3 + [pltpu.VMEM((128, D), F32), pltpu.VMEM(igrad.shape, F32), DMA((5,)), DMA((6,))],
        20 * rows * D * D, out_specs=[VM] * 7 + [ANY], limit=60 << 20)


def per_device(
    text_tokens, image_tokens, image_lengths, patch_mask, self_query, self_key, self_value, self_out, cross_query,
    cross_key, cross_value, cross_out, mlp_up, mlp_down, norm_self, norm_cross, norm_mlp, out_grad,
):
    ndp, nkv = lax.axis_size("dp"), lax.axis_size("kv")
    caps, tokens = image_tokens.shape[0], image_tokens.shape[1]
    gain_block = jnp.pad(jnp.stack([norm_self, norm_cross, norm_mlp], 1), ((0, 0), (0, 125)))
    parts = [self_query, self_key, self_value, self_out, cross_query, cross_key, cross_value, gain_block]
    packed, tail = (a.reshape(D, -1) for a in all_gather(parts, ndp, nkv, 1))
    image = image_tokens.reshape(caps * tokens, D)
    h1, q1, k1, v1, p1, c1, x2, h2, q2, gains = text_forward(text_tokens, packed, tail)
    c2, lse, keys, vals, e, stats, qall, second, third, down = cross_forward(
        q2, image, image_lengths, patch_mask, packed, tail, cross_out, mlp_up, mlp_down, ndp, nkv, 2)
    second, third = second.reshape(D, -1), third.reshape(D, -1)
    down = down.reshape(FF, D)
    layer_out, dx3, dc2, d_up, d_down, d_co, ng3 = mlp(c2, x2, out_grad, gains, second, third, down)
    dq2, d_ck, d_cv, igrad, sum_a, sum_b, sum_c = cross_backward(
        dc2, c2, lse, stats, qall, keys, vals, e, image, packed, tail, d_co, d_up, d_down, ndp, nkv, 3)
    text_grad, d_q, d_k, d_v, d_o, d_cq, ngs, image_grad = text_backward(
        dq2, dx3, text_tokens, x2, h1, h2, c1, q1, k1, v1, p1, gains, ng3, packed, igrad)
    sum_d, sum_e = reduce_scatter([d_q, d_k, d_v, d_o, d_cq, d_ck, d_cv, ngs], ndp, nkv, 4)
    rows = norm_self.shape[0]
    moves = [(3, j * D, D, j, 0) for j in range(6)] + [(4, 0, D, 6, 0), (0, 0, D, 7, 0), (0, D, D, 8, 0), (2, 0, FF - D, 8, D), (1, 0, D, 9, 0)]
    *parts, norms = deliver(
        [sum_a, sum_b, sum_c, sum_d, sum_e], [(rows, D)] * 8 + [(rows, FF), mlp_down.shape], moves, (4, D))
    return (layer_out, text_grad, image_grad.reshape(caps, tokens, D), *parts, norms[0, :rows], norms[1, :rows], norms[2, :rows])


def solution(mesh):
    in_specs = (
        P(("dp", "kv"), None),
        P("dp", "kv", None),
        P("dp"),
        P("dp", "kv"),
        P(("dp", "kv"), None),
        P(("dp", "kv"), None),
        P(("dp", "kv"), None),
        P(("dp", "kv"), None),
        P(("dp", "kv"), None),
        P(("dp", "kv"), None),
        P(("dp", "kv"), None),
        P(("dp", "kv"), None),
        P(("dp", "kv"), None),
        P(("dp", "kv"), None),
        P(("dp", "kv")),
        P(("dp", "kv")),
        P(("dp", "kv")),
        P(("dp", "kv"), None),
    )
    out_specs = (
        P(("dp", "kv"), None),
        P(("dp", "kv"), None),
        P("dp", "kv", None),
        P(("dp", "kv"), None),
        P(("dp", "kv"), None),
        P(("dp", "kv"), None),
        P(("dp", "kv"), None),
        P(("dp", "kv"), None),
        P(("dp", "kv"), None),
        P(("dp", "kv"), None),
        P(("dp", "kv"), None),
        P(("dp", "kv"), None),
        P(("dp", "kv"), None),
        P(("dp", "kv")),
        P(("dp", "kv")),
        P(("dp", "kv")),
    )
    return jax.shard_map(
        per_device, mesh=mesh, in_specs=in_specs, out_specs=out_specs, check_vma=False
    )
```

```python
import functools
import types

import jax
import jax.numpy as jnp
from jax import lax
from jax.experimental import pallas as pl
from jax.experimental.pallas import tpu as pltpu
from jax.sharding import PartitionSpec as P

MESH = pl.DeviceIdType.MESH
def place(NDP, KV):
    di, ki = lax.axis_index("dp"), lax.axis_index("kv")
    Y = 2
    z, y, x, c = di // Y, di % Y, ki // 2, ki % 2
    y2, x2 = y + c*(1-2*y), x + (1-c)*(1-2*x)
    y3, x3 = y + (1-c)*(1-2*y), x + c*(1-2*x)
    return types.SimpleNamespace(
        di=di, ki=ki, z=z, y=y, x=x, c=c, Y=Y, Z=NDP//Y, KV=KV,
        split=((y2, x2), (y3, x3)), fixed=((y, 1-x), (1-y, x)), up=(di + Y, ki), dn=(di - Y, ki),
        px=(di, 2*(1-x) + c), py=(z*Y+1-y, ki), pd=(di, ki + 1 - 2*c), diag=(di, 2*(1-x) + 1 - c))

def enter(at, group=False):
    bar = pltpu.get_barrier_semaphore()
    @pl.when(at.z < at.Z-1)
    def _(): pl.semaphore_signal(bar, 1, device_id=at.up, device_id_type=MESH)
    @pl.when(at.z > 0)
    def _(): pl.semaphore_signal(bar, 1, device_id=at.dn, device_id_type=MESH)
    peers = (at.px, at.py, at.pd) + ((at.diag,) if group else ())
    for p in peers: pl.semaphore_signal(bar, 1, device_id=p, device_id_type=MESH)
    pl.semaphore_wait(bar, len(peers) + jnp.where(at.z < at.Z-1, 1, 0) + jnp.where(at.z > 0, 1, 0))

class Gather:
    def __init__(self, at, ins, outs, sems, route):
        self.at, self.ins, self.outs = at, ins, outs
        self.recv, self.sz, self.s2, self.s3, self.sd, self.sl = sems
        self.n = len(ins)
        self.own = self.slot(at.z, at.y, at.x)
        (self.y2, self.x2), (self.y3, self.x3) = route
        self.p2, self.p3 = ((at.z*at.Y+yy, 2*xx+at.c) for yy, xx in route)

    @staticmethod
    def sems(n, ND):
        Z = ND // 8
        D = pltpu.SemaphoreType.DMA
        return [D((n, ND)), D((n, 2, Z)), D((n, Z)), D((n, 2*Z)), D((n, ND//2)), D((n,))]

    def at_slot(self, i, s):
        out, rows = self.outs[i], self.ins[i].shape[0]
        if len(out.shape) == 3: return out.at[s]
        return out.at[pl.ds(pl.multiple_of(s * rows, 8), rows), :]

    def slot(self, zz, yy, xx):
        return (zz*self.at.Y+yy)*self.at.KV + xx*2 + self.at.c

    def send(self, s, sems, dev, own=False):
        for i in range(self.n):
            pltpu.make_async_remote_copy(
                src_ref=self.ins[i] if own else self.at_slot(i, s), dst_ref=self.at_slot(i, s), send_sem=sems(i),
                recv_sem=self.recv.at[i, s], device_id=dev, device_id_type=MESH).start()

    def arrive(self, s):
        for i in range(self.n):
            pltpu.make_async_copy(self.at_slot(i, s), self.at_slot(i, s), self.recv.at[i, s]).wait()

    def spread(self, zz, own=False):
        s = self.slot(zz, self.at.y, self.at.x)
        self.send(s, lambda i: self.s2.at[i, zz], self.p2, own)
        self.send(s, lambda i: self.s3.at[i, zz], self.p3, own)
        self.send(s, lambda i: self.sd.at[i, s//2], self.at.pd, own)

    def start(self):
        at, own = self.at, self.own
        @pl.when(at.z < at.Z-1)
        def _(): self.send(own, lambda i: self.sz.at[i, 0, at.z], at.up, True)
        @pl.when(at.z > 0)
        def _(): self.send(own, lambda i: self.sz.at[i, 1, at.z], at.dn, True)
        self.spread(at.z, True)
        for i in range(self.n):
            pltpu.make_async_copy(self.ins[i], self.at_slot(i, own), self.sl.at[i]).start()

    def second(self, zz):
        at = self.at
        s = self.slot(zz, self.y2, self.x2)
        self.arrive(s)
        self.send(s, lambda i: self.s3.at[i, at.Z+zz], self.p3)
        self.send(s, lambda i: self.sd.at[i, s//2], at.pd)

    def near(self, t):
        at = self.at
        @pl.when(at.z >= t)
        def _():
            s = self.slot(at.z-t, at.y, at.x); self.arrive(s)
            @pl.when(at.z < at.Z-1)
            def _(): self.send(s, lambda i: self.sz.at[i, 0, at.z-t], at.up)
            self.spread(at.z-t)
        @pl.when(at.z + t < at.Z)
        def _():
            s = self.slot(at.z+t, at.y, at.x); self.arrive(s)
            @pl.when(at.z > 0)
            def _(): self.send(s, lambda i: self.sz.at[i, 1, at.z+t], at.dn)
            self.spread(at.z+t)
        @pl.when(at.z >= t-1)
        def _(): self.second(at.z-t+1)
        @pl.when(jnp.logical_and(t > 1, at.z+t-1 < at.Z))
        def _(): self.second(at.z+t-1)

    def third(self, zz):
        at = self.at
        for yy, xx in ((self.y3, self.x3), (1-at.y, 1-at.x)):
            s = self.slot(zz, yy, xx)
            self.arrive(s)
            self.send(s, lambda i: self.sd.at[i, s//2], at.pd)

    def far(self, t):
        at = self.at
        @pl.when(at.z >= t)
        def _(): self.third(at.z-t)
        @pl.when(jnp.logical_and(t > 0, at.z+t < at.Z))
        def _(): self.third(at.z+t)

    def tick(self, k):
        if k < self.at.Z: self.near(jnp.int32(k+1))
        elif k < 2*self.at.Z: self.far(jnp.int32(k-self.at.Z))

    def finish(self, k=0):
        at, Z, n = self.at, self.at.Z, self.n
        lax.fori_loop(min(k, Z)+1, Z+1, lambda t, _: (self.near(t), 0)[1], 0)
        lax.fori_loop(max(k-Z, 0), Z, lambda t, _: (self.far(t), 0)[1], 0)
        def fin(h, _):
            self.arrive(2*h + 1 - at.c)
            for i in range(n):
                o = self.at_slot(i, 0)
                pltpu.make_async_copy(o, o, self.sd.at[i, h]).wait()
            return 0
        lax.fori_loop(0, at.KV*Z, fin, 0)
        def finz(zz, _):
            for i in range(n):
                o = self.at_slot(i, 0)
                pltpu.make_async_copy(o, o, self.s2.at[i, zz]).wait()
                pltpu.make_async_copy(o, o, self.s3.at[i, zz]).wait()
                pltpu.make_async_copy(o, o, self.s3.at[i, Z+zz]).wait()
                @pl.when(jnp.logical_and(at.z < Z-1, zz <= at.z))
                def _(): pltpu.make_async_copy(o, o, self.sz.at[i, 0, zz]).wait()
                @pl.when(jnp.logical_and(at.z > 0, zz >= at.z))
                def _(): pltpu.make_async_copy(o, o, self.sz.at[i, 1, zz]).wait()
            return 0
        lax.fori_loop(0, Z, finz, 0)
        for i in range(n):
            pltpu.make_async_copy(self.ins[i], self.at_slot(i, self.own), self.sl.at[i]).wait()

class PlaneGather(Gather):
    @staticmethod
    def sems(n, ND):
        D = pltpu.SemaphoreType.DMA
        return [D((n, ND)), D((n, 2, ND)), D((n, 1)), D((n, 2)), D((n, ND//2)), D((n,))]

    def onward(self, s, up, down, own=False):
        at = self.at
        if up:
            @pl.when(at.z < at.Z-1)
            def _(): self.send(s, lambda i: self.sz.at[i, 0, s], at.up, own)
        if down:
            @pl.when(at.z > 0)
            def _(): self.send(s, lambda i: self.sz.at[i, 1, s], at.dn, own)
        self.send(s, lambda i: self.sd.at[i, s//2], at.pd, own)

    def start(self):
        own = self.own
        self.send(own, lambda i: self.s2.at[i, 0], self.p2, True)
        self.send(own, lambda i: self.s3.at[i, 0], self.p3, True)
        self.onward(own, True, True, True)
        for i in range(self.n):
            pltpu.make_async_copy(self.ins[i], self.at_slot(i, own), self.sl.at[i]).start()

    def lines(self):
        at = self.at
        return ((at.y, at.x), (self.y2, self.x2), (self.y3, self.x3), (1-at.y, 1-at.x))

    def plane(self):
        at = self.at
        for j, (yy, xx) in enumerate(self.lines()[1:]):
            s = self.slot(at.z, yy, xx)
            self.arrive(s)
            if j == 0: self.send(s, lambda i: self.s3.at[i, 1], self.p3)
            self.onward(s, True, True)

    def level(self, t):
        at = self.at
        @pl.when(at.z >= t)
        def _():
            for yy, xx in self.lines():
                s = self.slot(at.z-t, yy, xx)
                self.arrive(s)
                self.onward(s, True, False)
        @pl.when(at.z + t < at.Z)
        def _():
            for yy, xx in self.lines():
                s = self.slot(at.z+t, yy, xx)
                self.arrive(s)
                self.onward(s, False, True)

    def tick(self, k):
        if k == 0: self.plane()
        elif k < self.at.Z: self.level(jnp.int32(k))

    def finish(self, k=0):
        at, Z, n = self.at, self.at.Z, self.n
        if k == 0: self.plane()
        lax.fori_loop(max(k, 1), Z, lambda t, _: (self.level(t), 0)[1], 0)
        def wait(i, sem):
            o = self.at_slot(i, 0)
            pltpu.make_async_copy(o, o, sem).wait()
        def fin(h, _):
            self.arrive(2*h + 1 - at.c)
            s = 2*h + at.c
            level = s // (at.Y * at.KV)
            for i in range(n):
                wait(i, self.sd.at[i, h])
                @pl.when(jnp.logical_and(at.z < Z-1, level <= at.z))
                def _(): wait(i, self.sz.at[i, 0, s])
                @pl.when(jnp.logical_and(at.z > 0, level >= at.z))
                def _(): wait(i, self.sz.at[i, 1, s])
            return 0
        lax.fori_loop(0, at.KV*Z, fin, 0)
        for i in range(n):
            for sem in (self.s2.at[i, 0], self.s3.at[i, 0], self.s3.at[i, 1]): wait(i, sem)
            pltpu.make_async_copy(self.ins[i], self.at_slot(i, self.own), self.sl.at[i]).wait()

def fill_block(parts, block, sem):
    copies, offset = [], 0
    for j, part in enumerate(parts):
        copies.append(pltpu.make_async_copy(part, block.at[:, pl.ds(offset, part.shape[1])], sem.at[j]))
        offset += part.shape[1]
    for copy in copies: copy.start()
    return copies

def ag_kernel(NDP, KV, count, *refs):
    parts, outs, packs, fill = refs[:count], refs[count:count+2], refs[count+2:count+4], refs[count+4]
    copies = fill_block(parts[:-2], packs[0], fill)
    copies += fill_block(parts[-2:], packs[1], fill.at[pl.ds(count-2, 2)])
    at = place(NDP, KV)
    enter(at)
    for copy in copies: copy.wait()
    k = count+5
    plane = PlaneGather(at, [packs[1]], [outs[1]], refs[k+6:], at.split)
    gather = Gather(at, [packs[0]], [outs[0]], refs[k:k+6], at.split)
    plane.start()
    gather.start()
    plane.tick(0)
    for k in range(1, min(at.Z, 4)):
        gather.tick(k-1)
        plane.tick(k)
    gather.finish(min(at.Z, 4)-1)
    plane.finish(min(at.Z, 4))

def all_gather(parts, NDP, KV, cid):
    ND = NDP*KV
    rows = parts[0].shape[0]
    widths = [sum(p.shape[1] for p in some) for some in (parts[:-2], parts[-2:])]
    return pl.pallas_call(
        functools.partial(ag_kernel, NDP, KV, len(parts)),
        out_shape=[jax.ShapeDtypeStruct((ND, rows, width), jnp.bfloat16) for width in widths],
        in_specs=[pl.BlockSpec(memory_space=pl.ANY)]*len(parts),
        out_specs=[pl.BlockSpec(memory_space=pl.ANY)]*2,
        scratch_shapes=[pltpu.VMEM((rows, width), jnp.bfloat16) for width in widths] + [pltpu.SemaphoreType.DMA((len(parts),))]
            + Gather.sems(1, ND) + PlaneGather.sems(1, ND),
        compiler_params=pltpu.CompilerParams(collective_id=cid, has_side_effects=True, vmem_limit_bytes=60<<20),
        name="gather_weights",
    )(*parts)


class Scatter:
    count = 9

    def __init__(self, at, sources, bufs, sems, route):
        self.at, self.sources = at, sources
        self.n = n = len(bufs) // 5
        self.loc, self.r1, self.r2, self.r3, self.rz = (bufs[j*n:(j+1)*n] for j in range(5))
        self.sl, self.sd, self.qd, self.s2, self.q2, self.s3, self.q3, self.sz, self.qz = sems
        (self.y2, self.x2), (self.y3, self.x3) = route
        self.p2, self.p3 = ((at.z*at.Y+yy, 2*xx+at.c) for yy, xx in route)
        self.lines = ((at.y, at.x), (self.y2, self.x2), (self.y3, self.x3), (1-at.y, 1-at.x))

    @staticmethod
    def bufs(shapes, ND):
        Z = ND // 8
        return [pltpu.VMEM(lead + tuple(s), jnp.bfloat16)
                for lead in ((ND//2,), (ND//2,), (2*Z,), (Z,), (2, Z)) for s in shapes]

    @staticmethod
    def sems(n, ND):
        Z = ND // 8
        D = pltpu.SemaphoreType.DMA
        return [D((n, ND//2))]*3 + [D((n, 2*Z))]*2 + [D((n, Z))]*2 + [D((n, 2, Z))]*2

    def half(self, zz, yy, xx): return (zz*self.at.Y+yy)*(self.at.KV//2) + xx

    def send(self, src, dst, ss, rsem, dev):
        pltpu.make_async_remote_copy(
            src_ref=src, dst_ref=dst, send_sem=ss, recv_sem=rsem, device_id=dev, device_id_type=MESH).start()

    def wait(self, ref, sem): pltpu.make_async_copy(ref, ref, sem).wait()

    def both(self, t, f):
        at = self.at
        @pl.when(at.z >= t)
        def _(): f(at.z-t)
        @pl.when(jnp.logical_and(t > 0, at.z+t < at.Z))
        def _(): f(at.z+t)

    def every(self, f):
        Z = self.at.Z
        lax.fori_loop(0, Z, lambda k, _: (self.both(Z-1-k, f), 0)[1], 0)

    def start(self):
        c = self.at.c
        def one(zz):
            for yy, xx in self.lines[::-1]:
                h = self.half(zz, yy, xx)
                for ref, i, off, dst, width in self.sources:
                    to, cols = pl.ds(dst, width), pl.ds(off, width)
                    self.send(ref.at[2*h+1-c, :, cols], self.r1[i].at[h, :, to], self.sd.at[i, h], self.qd.at[i, h], self.at.pd)
                    pltpu.make_async_copy(ref.at[2*h+c, :, cols], self.loc[i].at[h, :, to], self.sl.at[i, h]).start()
        self.every(one)

    def pair(self, h):
        for i in range(self.n):
            self.wait(self.loc[i].at[h], self.sl.at[i, h]); self.wait(self.r1[i].at[h], self.qd.at[i, h])
            self.loc[i][h] = self.loc[i][h] + self.r1[i][h]

    def first(self):
        def one(zz):
            for j, (yy, xx) in enumerate((self.lines[3], self.lines[2])):
                h = self.half(zz, yy, xx)
                self.pair(h)
                for i in range(self.n):
                    self.send(self.loc[i].at[h], self.r2[i].at[2*zz+j], self.s2.at[i, 2*zz+j], self.q2.at[i, 2*zz+j], self.p3)
            for yy, xx in self.lines[:2]: self.pair(self.half(zz, yy, xx))
        self.every(one)

    def second(self, t):
        at, Z = self.at, self.at.Z
        def one(zz):
            for j, (yy, xx) in enumerate((self.lines[1], self.lines[0])):
                h = self.half(zz, yy, xx)
                for i in range(self.n):
                    self.wait(self.r2[i].at[2*zz+j], self.q2.at[i, 2*zz+j])
                    self.loc[i][h] = self.loc[i][h] + self.r2[i][2*zz+j]
                    if j == 0:
                        self.send(self.loc[i].at[h], self.r3[i].at[zz], self.s3.at[i, zz], self.q3.at[i, zz], self.p2)
        self.both(t, one)
        def along(zz, d, dev, has):
            h = self.half(zz, at.y, at.x)
            for i in range(self.n):
                loc, rz = self.loc[i], self.rz[i]
                self.wait(self.r3[i].at[zz], self.q3.at[i, zz])
                @pl.when(has)
                def _():
                    self.wait(rz.at[d, zz], self.qz.at[i, d, zz])
                    loc[h] = loc[h] + self.r3[i][zz] + rz[d, zz]
                @pl.when(jnp.logical_not(has))
                def _(): loc[h] = loc[h] + self.r3[i][zz]
                self.send(loc.at[h], rz.at[d, zz], self.sz.at[i, d, zz], self.qz.at[i, d, zz], dev)
        u = t + 1
        @pl.when(at.z + u < Z)
        def _(): along(at.z+u, 0, at.up, at.z > 0)
        @pl.when(at.z >= u)
        def _(): along(at.z-u, 1, at.dn, at.z < Z-1)

    def tick(self, k):
        if k == 0: self.first()
        elif k <= self.at.Z: self.second(jnp.int32(self.at.Z-k))

    def rest(self, k):
        Z = self.at.Z
        if k == 0: self.first()
        lax.fori_loop(max(k, 1), Z+1, lambda j, _: (self.second(Z-j), 0)[1], 0)

    def finish(self, k, outs):
        at, Z, z = self.at, self.at.Z, self.at.z
        self.rest(k)
        h = self.half(z, at.y, at.x)
        for i, out in enumerate(outs):
            self.wait(self.r3[i].at[z], self.q3.at[i, z])
            out[...] = self.loc[i][h].astype(jnp.float32) + self.r3[i][z].astype(jnp.float32)
            for d, has in ((0, z > 0), (1, z < Z-1)):
                @pl.when(has)
                def _():
                    self.wait(self.rz[i].at[d, z], self.qz.at[i, d, z])
                    out[...] += self.rz[i][d, z].astype(jnp.float32)
        def fin(h, _):
            for i in range(self.n): self.wait(self.r1[i].at[h], self.sd.at[i, h])
            return 0
        lax.fori_loop(0, at.KV*Z, fin, 0)
        def fin2(zz, _):
            for i in range(self.n):
                self.wait(self.r3[i].at[zz], self.s3.at[i, zz])
                for j in range(2): self.wait(self.r2[i].at[2*zz+j], self.s2.at[i, 2*zz+j])
                @pl.when(zz > z)
                def _(): self.wait(self.rz[i].at[0, zz], self.sz.at[i, 0, zz])
                @pl.when(zz < z)
                def _(): self.wait(self.rz[i].at[1, zz], self.sz.at[i, 1, zz])
            return 0
        lax.fori_loop(0, Z, fin2, 0)

class PlaneScatter(Scatter):
    @staticmethod
    def bufs(shapes, ND):
        Z = ND // 8
        return [pltpu.VMEM(lead + tuple(s), jnp.bfloat16)
                for lead in ((ND//2,), (ND//2,), (2,), (1,), (2, 4*Z)) for s in shapes]

    @staticmethod
    def sems(n, ND):
        Z = ND // 8
        D = pltpu.SemaphoreType.DMA
        return [D((n, ND//2))]*3 + [D((n, 2))]*2 + [D((n, 1))]*2 + [D((n, 2, 4*Z))]*2

    def chain(self, t):
        at, Z = self.at, self.at.Z
        def along(zz, d, dev, has):
            for l, (yy, xx) in enumerate(self.lines):
                h = self.half(zz, yy, xx)
                k = 4*zz + l
                self.pair(h)
                for i in range(self.n):
                    loc, rz = self.loc[i], self.rz[i]
                    @pl.when(has)
                    def _():
                        self.wait(rz.at[d, k], self.qz.at[i, d, k])
                        loc[h] = loc[h] + rz[d, k]
                    self.send(loc.at[h], rz.at[d, k], self.sz.at[i, d, k], self.qz.at[i, d, k], dev)
        @pl.when(at.z + t < Z)
        def _(): along(at.z+t, 0, at.up, at.z > 0)
        @pl.when(at.z >= t)
        def _(): along(at.z-t, 1, at.dn, at.z < Z-1)

    def level(self):
        at, z = self.at, self.at.z
        for l, (yy, xx) in reversed(list(enumerate(self.lines))):
            h = self.half(z, yy, xx)
            k = 4*z + l
            self.pair(h)
            for i in range(self.n):
                loc, rz = self.loc[i], self.rz[i]
                for d, has in ((0, z > 0), (1, z < at.Z-1)):
                    @pl.when(has)
                    def _():
                        self.wait(rz.at[d, k], self.qz.at[i, d, k])
                        loc[h] = loc[h] + rz[d, k]
                if l >= 2:
                    self.send(loc.at[h], self.r2[i].at[3-l], self.s2.at[i, 3-l], self.q2.at[i, 3-l], self.p3)

    def plane(self):
        for j, (yy, xx) in enumerate((self.lines[1], self.lines[0])):
            h = self.half(self.at.z, yy, xx)
            for i in range(self.n):
                self.wait(self.r2[i].at[j], self.q2.at[i, j])
                self.loc[i][h] = self.loc[i][h] + self.r2[i][j]
                if j == 0: self.send(self.loc[i].at[h], self.r3[i].at[0], self.s3.at[i, 0], self.q3.at[i, 0], self.p2)

    def tick(self, k):
        Z = self.at.Z
        if k < Z-1: self.chain(jnp.int32(Z-1-k))
        elif k == Z-1: self.level()
        elif k == Z: self.plane()

    def finish(self, k, outs):
        at, Z, z = self.at, self.at.Z, self.at.z
        lax.fori_loop(min(k, Z-1), Z-1, lambda j, _: (self.chain(Z-1-j), 0)[1], 0)
        if k <= Z-1: self.level()
        if k <= Z: self.plane()
        h = self.half(z, at.y, at.x)
        for i, out in enumerate(outs):
            self.wait(self.r3[i].at[0], self.q3.at[i, 0])
            out[...] = self.loc[i][h].astype(jnp.float32) + self.r3[i][0].astype(jnp.float32)
        def fin(h, _):
            zz = h // (at.Y * at.KV // 2)
            for i in range(self.n):
                self.wait(self.r1[i].at[h], self.sd.at[i, h])
                for d, cond in ((0, zz > z), (1, zz < z)):
                    @pl.when(cond)
                    def _(): self.wait(self.rz[i].at[d, h], self.sz.at[i, d, h])
            return 0
        lax.fori_loop(0, at.KV*Z, fin, 0)
        for i in range(self.n):
            self.wait(self.r3[i].at[0], self.s3.at[i, 0])
            for j in range(2): self.wait(self.r2[i].at[j], self.s2.at[i, j])

def rs_kernel(NDP, KV, count, *refs):
    parts, outs, k = refs[:count], refs[count:count+2], count+2
    at = place(NDP, KV)
    enter(at)
    def sources(some):
        found, offset = [], 0
        for ref in some:
            found.append((ref, 0, 0, offset, ref.shape[2]))
            offset += ref.shape[2]
        return found
    plane = PlaneScatter(at, sources(parts[-2:]), refs[k:k+5], refs[k+5:k+14], at.split)
    scatter = Scatter(at, sources(parts[:-2]), refs[k+14:k+19], refs[k+19:], at.split)
    plane.start()
    scatter.start()
    last = min(at.Z, 4)
    for j in range(last):
        plane.tick(j)
        scatter.tick(j)
    plane.finish(last, outs[1:])
    scatter.finish(last, outs[:1])

def blocks(g, ND): return g.reshape(ND, g.shape[0]//ND, g.shape[1])

def reduce_scatter(grads, NDP, KV, cid):
    ND = NDP*KV
    parts = [blocks(g, ND) for g in grads]
    rows = parts[0].shape[1]
    shapes = [(rows, sum(g.shape[2] for g in some)) for some in (parts[:-2], parts[-2:])]
    return pl.pallas_call(
        functools.partial(rs_kernel, NDP, KV, len(parts)),
        out_shape=[jax.ShapeDtypeStruct(s, jnp.float32) for s in shapes],
        in_specs=[pl.BlockSpec(memory_space=pl.ANY)]*len(parts),
        out_specs=[pl.BlockSpec(memory_space=pltpu.VMEM)]*2,
        scratch_shapes=PlaneScatter.bufs(shapes[1:], ND) + PlaneScatter.sems(1, ND) + Scatter.bufs(shapes[:1], ND) + Scatter.sems(1, ND),
        compiler_params=pltpu.CompilerParams(collective_id=cid, has_side_effects=True, vmem_limit_bytes=60<<20),
        name="scatter_gradients",
    )(*parts)


D = 768
FF = 3072
HEADS = 12
HD = 64
SEQ = 64
QUAD = 4 * HD
EPS = 1e-05
NEG = -1e30
GELU_C = 0.7978845608028654
GELU_A = 0.044715
SCALE = 0.125
BF = jnp.bfloat16
F32 = jnp.float32
VM = pl.BlockSpec(memory_space=pltpu.VMEM)
ANY = pl.BlockSpec(memory_space=pl.ANY)
DMA = pltpu.SemaphoreType.DMA


def nn(a, b):
    return lax.dot_general(a, b, (((1,), (0,)), ((), ())), preferred_element_type=F32)


def nt(a, b):
    return lax.dot_general(a, b, (((1,), (1,)), ((), ())), preferred_element_type=F32)


def tn(a, b):
    return lax.dot_general(a, b, (((0,), (0,)), ((), ())), preferred_element_type=F32)


def unit_of(values):
    centre = values - jnp.mean(values, -1, keepdims=True)
    scaled = lax.rsqrt(jnp.mean(centre * centre, -1, keepdims=True) + EPS)
    return centre * scaled, scaled


def norm_backward(upstream, unit, scaled, gain):
    through = upstream * gain
    return scaled * (
        through - jnp.mean(through, -1, keepdims=True) - unit * jnp.mean(through * unit, -1, keepdims=True)
    )


def head_masks(width):
    lane = lax.broadcasted_iota(jnp.int32, (1, width), 1) // HD
    return [(lane == head).astype(F32).astype(BF) for head in range(width // HD)]


def stacked(values, masks):
    return jnp.concatenate([values * mask for mask in masks], 0)


def own_blocks(values):
    lane = lax.broadcasted_iota(jnp.int32, (HD, QUAD), 1) // HD
    total = values[:HD]
    for head in range(1, 4):
        total = jnp.where(lane == head, values[head * HD : (head + 1) * HD], total)
    return total


def load(source, target, sem):
    return pltpu.make_async_copy(source, target, sem)


def call(kernel, name, outs, ins, specs, scratch, flops, out_specs=None, cid=None, limit=56 << 20):
    params = dict(vmem_limit_bytes=limit)
    if cid is not None:
        params.update(collective_id=cid, has_side_effects=True)
    size = lambda a: a.size * a.dtype.itemsize
    return pl.pallas_call(
        kernel,
        out_shape=outs,
        in_specs=specs,
        out_specs=out_specs or [VM] * len(outs),
        scratch_shapes=scratch,
        compiler_params=pltpu.CompilerParams(**params),
        cost_estimate=pl.CostEstimate(flops=int(flops), transcendentals=0, bytes_accessed=sum(map(size, ins)) + sum(map(size, outs))),
        name=name,
    )(*ins)


def arr(shape, dtype=BF):
    return jax.ShapeDtypeStruct(shape, dtype)


def text_forward_kernel(text, packed, tail, h1, q1, k1, v1, p1, c1, x2, h2, q2, gains, w, gw, sem, between=lambda k: None):
    weights = [load(packed.at[:, pl.ds(j * D, D)] if j < 4 else tail.at[:, pl.ds(0, D)], w.at[j], sem.at[j]) for j in range(5)]
    gcopy = load(tail.at[:, pl.ds(D, 128)], gw, sem.at[5])
    gcopy.start()
    for copy in weights:
        copy.start()
    x = text[...].astype(F32)
    unit, _ = unit_of(x)
    gcopy.wait()
    gains[...] = gw[...].astype(F32).T[:8]
    h1[...] = (unit * gains[0:1]).astype(BF)
    for j, ref in enumerate((q1, k1, v1)):
        weights[j].wait()
        ref[...] = nn(h1[...], w[j]).astype(BF)
    between(0)
    rows = text.shape[0]
    first = lax.broadcasted_iota(jnp.int32, (rows, rows), 0)
    second = lax.broadcasted_iota(jnp.int32, (rows, rows), 1)
    allowed = jnp.logical_and(first >= second, first // SEQ == second // SEQ)
    masks = head_masks(128)
    for pair in range(HEADS // 2):
        lanes = slice(pair * 128, (pair + 1) * 128)
        total = None
        for j, mask in enumerate(masks):
            scores = nt(q1[:, lanes] * mask, k1[:, lanes]) * SCALE
            scores = jnp.where(allowed, scores, NEG)
            powers = jnp.exp(scores - jnp.max(scores, -1, keepdims=True))
            probs = (powers / jnp.sum(powers, -1, keepdims=True)).astype(BF)
            p1[2 * pair + j] = probs
            part = nn(probs, v1[:, lanes] * mask)
            total = part if total is None else total + part
        c1[:, lanes] = total.astype(BF)
    between(1)
    weights[3].wait()
    second_res = x + nn(c1[...], w[3])
    x2[...] = second_res
    unit, _ = unit_of(second_res)
    h2[...] = (unit * gains[1:2]).astype(BF)
    weights[4].wait()
    q2[...] = nn(h2[...], w[4]).astype(BF)


def text_forward(text, packed, tail):
    rows = text.shape[0]
    low = arr((rows, D))
    return call(
        text_forward_kernel, "text_forward",
        [low, low, low, low, arr((HEADS, rows, rows)), low, arr((rows, D), F32), low, low, arr((8, D), F32)],
        [text, packed, tail], [VM, ANY, ANY],
        [pltpu.VMEM((5, D, D), BF), pltpu.VMEM((D, 128), BF), DMA((6,))], 10 * rows * D * D)


TICKS = (3, 6, 8, 10)


def remote(src, dst, send, recv, device):
    return pltpu.make_async_remote_copy(
        src_ref=src, dst_ref=dst, send_sem=send, recv_sem=recv, device_id=device, device_id_type=MESH)


def cross_forward_kernel(NDP, KV, q2, image, lengths, patches, both, out_part, up_part, down_part,
                         c2, lse, keys, vals, e, stats, qall, second, third, down, w, obuf, ro, rst, usable, block, wide, down_block,
                         wsem, ssem, rsem, fsem, *gsems):
    at = place(NDP, KV)
    fills = fill_second(out_part, up_part, down_part, block, wide, down_block, fsem)
    found = cross_weights(both, w, wsem)
    own_copy = load(q2, qall.at[at.ki], wsem.at[2])
    own_copy.start()
    enter(at, True)
    for copy in fills:
        copy.wait()
    plane = PlaneGather(at, [wide], [third], gsems[6:], at.fixed)
    gather = Gather(at, [block, down_block], [second, down], gsems[:6], at.fixed)
    plane.start()
    gather.start()
    cross_forward_part(at, plane, gather, 0, lambda: found, own_copy, q2, image, lengths, patches,
                       c2, lse, keys, vals, e, stats, qall, w, obuf, ro, rst, usable, ssem, rsem)


def fill_second(out_part, up_part, down_part, block, wide, down_block, fsem):
    fills = fill_block([out_part, up_part.at[:, pl.ds(0, D)]], block, fsem)
    late = [load(down_part, down_block, fsem.at[2]), load(up_part.at[:, pl.ds(D, FF - D)], wide, fsem.at[3])]
    for copy in late:
        copy.start()
    return fills + late


def cross_weights(pair, w, sem):
    weights = [load(pair.at[:, pl.ds(j * D, D)], w.at[j], sem.at[j]) for j in range(2)]
    for copy in weights:
        copy.start()
    return weights


def cross_forward_part(at, plane, gather, done, weights, own_copy, q2, image, lengths, patches,
                       c2, lse, keys, vals, e, stats, qall, w, obuf, ro, rst, usable, ssem, rsem, after=lambda: None):
    di, ki, x, c = at.di, at.ki, at.x, at.c
    caps, tokens = patches.shape
    own_caps = caps // 4
    core, over, diag = 2 * x + 1 - c, 2 * (1 - x) + c, 2 * (1 - x) + 1 - c
    to_core = remote(q2, qall.at[ki], ssem.at[0], rsem.at[ki], (di, core))
    to_over = remote(q2, qall.at[ki], ssem.at[1], rsem.at[ki], (di, over))
    to_over.start()
    to_core.start()
    weights = weights()
    row = lax.broadcasted_iota(jnp.int32, usable.shape, 0)
    limit = jnp.zeros(usable.shape, jnp.int32)
    for cap in range(caps):
        limit = jnp.where(row == cap, lengths[cap], limit)
    position = lax.broadcasted_iota(jnp.int32, usable.shape, 1) + ki * tokens
    usable[...] = jnp.zeros(usable.shape, BF)
    usable[0:caps, :] = jnp.where(jnp.logical_and(position < limit, True)[0:caps], (patches[...] == 1).astype(F32), 0.0).astype(BF)
    weights[0].wait()

    def project(j, ref, i):
        rows = pl.ds(pl.multiple_of(i * tokens, 16), tokens)
        ref[rows, :] = nn(image[rows, :], w[j]).astype(BF)

    lax.fori_loop(0, caps, lambda i, _: (project(0, keys, i), 0)[1], 0)
    load(qall.at[over], qall.at[over], rsem.at[over]).wait()
    relay = remote(qall.at[over], qall.at[over], ssem.at[2], rsem.at[over], (di, core))
    relay.start()
    plane.tick(done)
    gather.tick(done)
    weights[1].wait()
    lax.fori_loop(0, caps, lambda i, _: (project(1, vals, i), 0)[1], 0)
    plane.tick(done + 1)
    gather.tick(done + 1)
    load(qall.at[core], qall.at[core], rsem.at[core]).wait()
    load(qall.at[diag], qall.at[diag], rsem.at[diag]).wait()
    own_copy.wait()
    masks = head_masks(QUAD)

    def owner_of(step):
        return 2 * ((x + 1 + step // 2) % 2) + (c + 1 + step % 2) % 2

    def attend(i, _):
        owner, local = owner_of(i // own_caps), i % own_caps
        cap = owner * own_caps + local
        rows = pl.ds(pl.multiple_of(cap * tokens, 16), tokens)
        queries = pl.ds(pl.multiple_of(local * SEQ, 16), SEQ)
        for j, when in enumerate(TICKS):
            @pl.when(i == when * caps // 12)
            def _():
                plane.tick(done + 2 + j)
                gather.tick(done + 2 + j)
        chosen = (lax.broadcasted_iota(jnp.int32, (usable.shape[0], QUAD), 0) == cap).astype(F32).astype(BF)
        shift = tn(usable[...], chosen)
        for g in range(3):
            lanes = slice(g * QUAD, (g + 1) * QUAD)
            scores = nt(keys[rows, lanes], stacked(qall[owner, queries, lanes], masks)) * SCALE
            scores = jnp.where(shift > 0.5, scores, NEG)
            top = jnp.max(scores, 0, keepdims=True)
            powers = jnp.where(shift > 0.5, jnp.exp(scores - top), 0.0)
            low = powers.astype(BF)
            e[pl.ds(pl.multiple_of((cap * 3 + g) * tokens, 16), tokens), :] = low
            stats[owner, pl.ds(3 * local + g, 1), :] = top
            stats[owner, pl.ds(16 + 3 * local + g, 1), :] = jnp.sum(powers, 0, keepdims=True)
            obuf[owner, queries, lanes] = own_blocks(tn(low, vals[rows, lanes])).astype(BF)

        @pl.when(jnp.logical_and(local == own_caps - 1, owner != ki))
        def _():
            remote(obuf.at[owner], ro.at[ki], ssem.at[3 + owner], rsem.at[4 + ki], (di, owner)).start()
            remote(stats.at[owner], rst.at[ki], ssem.at[7 + owner], rsem.at[8 + ki], (di, owner)).start()

        return 0

    lax.fori_loop(0, caps, attend, 0)
    after()
    ro[ki] = obuf[ki]
    rst[ki] = stats[ki]
    for other in (core, over, diag):
        load(ro.at[other], ro.at[other], rsem.at[4 + other]).wait()
        load(rst.at[other], rst.at[other], rsem.at[8 + other]).wait()
    lane = lax.broadcasted_iota(jnp.int32, (HD, QUAD), 1) // HD

    def combine(local, _):
        queries = pl.ds(pl.multiple_of(local * SEQ, 16), SEQ)
        for g in range(3):
            row = pl.ds(3 * local + g, 1)
            row_sum = pl.ds(16 + 3 * local + g, 1)
            tops = [rst[k, row, :] for k in range(4)]
            top = jnp.maximum(jnp.maximum(tops[0], tops[1]), jnp.maximum(tops[2], tops[3]))
            parts = [jnp.exp(t - top) for t in tops]
            total = sum(part * rst[k, row_sum, :] for k, part in enumerate(parts))
            lse[row, :] = top + jnp.log(total)
            table = jnp.concatenate([part / total for part in parts] * 2, 0).T
            mixed = 0.0
            for k in range(4):
                column = table[:, k : k + 1]
                weight = column[:HD] * jnp.ones((HD, QUAD), F32)
                for head in range(1, 4):
                    weight = jnp.where(lane == head, column[head * HD : (head + 1) * HD], weight)
                mixed = mixed + weight * ro[k, queries, g * QUAD : (g + 1) * QUAD].astype(F32)
            c2[queries, g * QUAD : (g + 1) * QUAD] = mixed
        return 0

    lax.fori_loop(0, own_caps, combine, 0)
    to_core.wait_send()
    to_over.wait_send()
    relay.wait_send()
    for other in (core, over, diag):
        load(obuf.at[other], obuf.at[other], ssem.at[3 + other]).wait()
        load(stats.at[other], stats.at[other], ssem.at[7 + other]).wait()
    plane.finish(done + 2 + len(TICKS))
    gather.finish(done + 2 + len(TICKS))


def forward_kernel(NDP, KV, *refs):
    text, image, lengths, patches, *parts = refs[:15]
    firsts, crosses, (out_part, up_part, down_part) = parts[:6], parts[6:8], parts[8:]
    h1, q1, k1, v1, p1, c1, x2, h2, gains, c2, lse, stats, qall, *outs = refs[15:37]
    keys_out, vals_out, e_out, packed, tail, both, second, third, down = outs
    (q2, tw, gw, keys, vals, e, pixels, w, obuf, ro, rst, usable, block, wide, down_block, pack, pack_tail, pack_both,
     tsem, wsem, ssem, rsem, fsem, sem, osem) = refs[37:62]
    gsems = refs[62:]
    copies = fill_block(firsts[:-2], pack, sem) + fill_block(firsts[-2:], pack_tail, sem.at[pl.ds(4, 2)])
    copies += fill_block(crosses, pack_both, sem.at[pl.ds(6, 2)])
    fills = fill_second(out_part, up_part, down_part, block, wide, down_block, fsem)
    image_copy = load(image, pixels, osem.at[3])
    image_copy.start()
    at = place(NDP, KV)
    enter(at, True)
    for copy in copies:
        copy.wait()
    plane = PlaneGather(at, [pack_tail], [tail], gsems[0:6], at.split)
    gather = Gather(at, [pack], [packed], gsems[6:12], at.split)
    middle = Gather(at, [pack_both], [both], gsems[12:18], at.split)
    late_plane = PlaneGather(at, [wide], [third], gsems[18:24], at.fixed)
    late = Gather(at, [block, down_block], [second, down], gsems[24:30], at.fixed)
    plane.start()
    gather.start()
    plane.tick(0)
    for copy in fills:
        copy.wait()
    image_copy.wait()
    last = min(at.Z, 4)
    for k in range(1, last):
        gather.tick(k - 1)
        plane.tick(k)
        if k == 1:
            middle.start()
        else:
            middle.tick(k - 2)
    late_plane.start()
    late.start()
    gather.finish(last - 1)
    plane.finish(last)

    def between(k):
        middle.tick(last - 2 + k)
        late_plane.tick(k)
        late.tick(k)

    text_forward_kernel(text, packed, tail, h1, q1, k1, v1, p1, c1, x2, h2, q2, gains, tw, gw, tsem, between)
    own_copy = load(q2, qall.at[at.ki], wsem.at[2])
    own_copy.start()
    results = [load(keys, keys_out, osem.at[0]), load(vals, vals_out, osem.at[1]), load(e, e_out, osem.at[2])]

    def weights():
        middle.finish(last)
        return cross_weights(both, w, wsem)

    def after():
        for copy in results:
            copy.start()

    cross_forward_part(at, late_plane, late, 2, weights, own_copy, q2, pixels, lengths, patches,
                       c2, lse, keys, vals, e, stats, qall, w, obuf, ro, rst, usable, ssem, rsem, after)
    for copy in results:
        copy.wait()


def forward(text, image, lengths, patches, firsts, crosses, out_part, up_part, down_part, NDP, KV, cid):
    rows, (caps, tokens), ND = text.shape[0], patches.shape, NDP * KV
    lows = out_part.shape[0]
    low, wide_row = arr((rows, D)), arr((rows, D), F32)
    keys, scores = (caps * tokens, D), (caps * 3 * tokens, QUAD)
    ins = [text, image, lengths, patches, *firsts, *crosses, out_part, up_part, down_part]
    V = pltpu.VMEM
    return call(
        functools.partial(forward_kernel, NDP, KV), "forward",
        [low, low, low, low, arr((HEADS, rows, rows)), low, wide_row, low, arr((8, D), F32),
         wide_row, arr((16, QUAD), F32), arr((4, 32, QUAD), F32), arr((4, rows, D)),
         arr(keys), arr(keys), arr(scores), arr((D, 4 * D)), arr((D, D + 128)), arr((D, 2 * D)),
         arr((D, 2 * D)), arr((D, FF - D)), arr((FF, D))],
        ins, [VM, ANY, pl.BlockSpec(memory_space=pltpu.SMEM), VM] + [ANY] * 11,
        [V((rows, D), BF), V((5, D, D), BF), V((D, 128), BF), V(keys, BF), V(keys, BF), V(scores, BF), V(keys, BF),
         V((2, D, D), BF), V((4, rows, D), BF), V((4, rows, D), BF), V((4, 32, QUAD), F32),
         V((-(-caps // 16) * 16, tokens), BF), V((lows, 2 * D), BF), V((lows, FF - D), BF), V(down_part.shape, BF),
         V((lows, 4 * D), BF), V((lows, D + 128), BF), V((lows, 2 * D), BF),
         DMA((6,)), DMA((3,)), DMA((11,)), DMA((12,)), DMA((4,)), DMA((8,)), DMA((4,))]
        + PlaneGather.sems(1, ND) + Gather.sems(1, ND) + Gather.sems(1, ND) + PlaneGather.sems(1, ND) + Gather.sems(2, ND),
        6 * caps * tokens * D * D, out_specs=[VM] * 13 + [ANY] * 9, cid=cid, limit=62 << 20)


def cross_forward(q2, image, lengths, patches, both, out_part, up_part, down_part, NDP, KV, cid):
    rows, (caps, tokens), ND = q2.shape[0], patches.shape, NDP * KV
    lows = out_part.shape[0]
    return call(
        functools.partial(cross_forward_kernel, NDP, KV), "cross_forward",
        [arr((rows, D), F32), arr((16, QUAD), F32), arr((caps * tokens, D)), arr((caps * tokens, D)),
         arr((caps * 3 * tokens, QUAD)), arr((4, 32, QUAD), F32), arr((4, rows, D)),
         arr((ND, lows, 2 * D)), arr((ND, lows, FF - D)), arr((ND,) + down_part.shape)],
        [q2, image, lengths, patches, both, out_part, up_part, down_part],
        [VM, VM, pl.BlockSpec(memory_space=pltpu.SMEM), VM, ANY, ANY, ANY, ANY],
        [pltpu.VMEM((2, D, D), BF), pltpu.VMEM((4, rows, D), BF), pltpu.VMEM((4, rows, D), BF),
         pltpu.VMEM((4, 32, QUAD), F32), pltpu.VMEM((-(-caps // 16) * 16, tokens), BF),
         pltpu.VMEM((lows, 2 * D), BF), pltpu.VMEM((lows, FF - D), BF), pltpu.VMEM(down_part.shape, BF),
         DMA((3,)), DMA((11,)), DMA((12,)), DMA((4,))] + Gather.sems(2, ND) + PlaneGather.sems(1, ND),
        4 * caps * tokens * D * D, out_specs=[VM] * 7 + [ANY] * 3, cid=cid)


BACK_TICKS = (4, 9)


def cross_backward_kernel(NDP, KV, dc2, c2, lse, stats, qall, keys, vals, e, image, both, dco, dup, ddown,
                          dq2, wk, wv, igrad, sum_a, sum_b, sum_c, dk, dv, w, ibuf,
                          dall, sall, qbuf, rq, csem, wsem, isem, ssem, rsem, *more):
    at = place(NDP, KV)
    di, ki, x, c = at.di, at.ki, at.x, at.c
    weights = cross_weights(both, w, wsem)
    rows_all = keys.shape[0]
    caps = 4 * (dc2.shape[0] // SEQ)
    own_caps = caps // 4
    tokens = rows_all // caps
    core, over, diag = 2 * x + 1 - c, 2 * (1 - x) + c, 2 * (1 - x) + 1 - c
    masks = head_masks(QUAD)
    sall[ki, 0:16, :] = lse[...]

    def dots(local, _):
        queries = pl.ds(pl.multiple_of(local * SEQ, 16), SEQ)
        for g in range(3):
            lanes = slice(g * QUAD, (g + 1) * QUAD)
            product = dc2[queries, lanes].astype(F32) * c2[queries, lanes]
            product = jnp.concatenate([product * mask.astype(F32) for mask in masks], 0)
            sums = lax.dot_general(
                jnp.ones((8, QUAD), F32), product, (((1,), (1,)), ((), ())),
                preferred_element_type=F32, precision=lax.Precision.HIGHEST)
            sall[ki, pl.ds(16 + 3 * local + g, 1), :] = sums[0:1]
        return 0

    own_copy = load(dc2, dall.at[ki], csem)
    own_copy.start()
    enter(at, True)
    plane = PlaneScatter(at, [(dup, 0, D, 0, FF - D)], more[0:5], more[5:14], at.fixed)
    scatter = Scatter(at, [(dco, 0, 0, 0, D), (dup, 0, 0, D, D), (ddown, 1, 0, 0, D)], more[14:24], more[24:], at.fixed)
    to_over = remote(dc2, dall.at[ki], ssem.at[1], rsem.at[ki], (di, over))
    to_core = remote(dc2, dall.at[ki], ssem.at[0], rsem.at[ki], (di, core))
    to_over.start()
    to_core.start()
    plane.start()
    scatter.start()
    lax.fori_loop(0, own_caps, dots, 0)
    small = [remote(sall.at[ki], sall.at[ki], ssem.at[2 + j], rsem.at[4 + ki], (di, other))
             for j, other in enumerate((core, over, diag))]
    for copy in small:
        copy.start()
    own_copy.wait()
    plane.tick(0)
    scatter.tick(0)
    relay = remote(dall.at[over], dall.at[over], ssem.at[5], rsem.at[over], (di, core))

    def attend(i, _):
        step, local = i // own_caps, i % own_caps
        owner = 2 * ((x + step // 2) % 2) + (c + step % 2) % 2

        @pl.when(i == own_caps)
        def _():
            load(dall.at[core], dall.at[core], rsem.at[core]).wait()
            load(sall.at[core], sall.at[core], rsem.at[4 + core]).wait()

        @pl.when(i == 2 * own_caps - 1)
        def _():
            load(dall.at[over], dall.at[over], rsem.at[over]).wait()
            relay.start()

        @pl.when(i == 2 * own_caps)
        def _():
            load(sall.at[over], sall.at[over], rsem.at[4 + over]).wait()

        @pl.when(i == 3 * own_caps)
        def _():
            load(dall.at[diag], dall.at[diag], rsem.at[diag]).wait()
            load(sall.at[diag], sall.at[diag], rsem.at[4 + diag]).wait()

        for j, when in enumerate(BACK_TICKS):
            @pl.when(i == when * caps // 12)
            def _():
                plane.tick(1 + j)
                scatter.tick(1 + j)

        cap = owner * own_caps + local
        rows = pl.ds(pl.multiple_of(cap * tokens, 16), tokens)
        queries = pl.ds(pl.multiple_of(local * SEQ, 16), SEQ)
        for g in range(3):
            lanes = slice(g * QUAD, (g + 1) * QUAD)
            factor = jnp.exp(stats[owner, pl.ds(3 * local + g, 1), :] - sall[owner, pl.ds(3 * local + g, 1), :])
            dots_row = sall[owner, pl.ds(16 + 3 * local + g, 1), :]
            probs = e[pl.ds(pl.multiple_of((cap * 3 + g) * tokens, 16), tokens), :].astype(F32) * factor
            upstream = stacked(dall[owner, queries, lanes], masks)
            queried = stacked(qall[owner, queries, lanes], masks)
            grad = nt(vals[rows, lanes], upstream)
            grad = (probs * (grad - dots_row)).astype(BF)
            dv[rows, lanes] = nn(probs.astype(BF), upstream).astype(BF)
            dk[rows, lanes] = (nn(grad, queried) * SCALE).astype(BF)
            qbuf[owner, queries, lanes] = (own_blocks(tn(grad, keys[rows, lanes])) * SCALE).astype(BF)

        @pl.when(jnp.logical_and(local == own_caps - 1, owner != ki))
        def _():
            remote(qbuf.at[owner], rq.at[ki], ssem.at[6 + owner], rsem.at[8 + ki], (di, owner)).start()

        return 0

    lax.fori_loop(0, caps, attend, 0)

    def weight(j, _):
        cols = pl.ds(pl.multiple_of(j * 256, 256), 256)
        flipped = image[:, cols].T
        wk[cols, :] = nn(flipped, dk[...]).astype(BF)
        wv[cols, :] = nn(flipped, dv[...]).astype(BF)
        return 0

    lax.fori_loop(0, D // 256, weight, 0)
    ticks = 1 + len(BACK_TICKS)
    plane.tick(ticks)
    scatter.tick(ticks)
    for copy in weights:
        copy.wait()

    def flush(i):
        return load(ibuf.at[i % 2], igrad.at[pl.ds(pl.multiple_of(i * tokens, 16), tokens), :], isem.at[i % 2])

    def image_rows(i, _):
        @pl.when(i >= 2)
        def _():
            flush(i - 2).wait()

        rows = pl.ds(pl.multiple_of(i * tokens, 16), tokens)
        ibuf[i % 2] = nt(dk[rows, :], w[0]) + nt(dv[rows, :], w[1])
        flush(i).start()
        return 0

    lax.fori_loop(0, caps, image_rows, 0)
    plane.tick(ticks + 1)
    scatter.tick(ticks + 1)
    rq[ki] = qbuf[ki]
    for other in (core, over, diag):
        load(rq.at[other], rq.at[other], rsem.at[8 + other]).wait()
    dq2[...] = (rq[0].astype(F32) + rq[1].astype(F32) + rq[2].astype(F32) + rq[3].astype(F32)).astype(BF)
    to_core.wait_send()
    to_over.wait_send()
    relay.wait_send()
    for copy in small:
        copy.wait_send()
    for other in (core, over, diag):
        load(qbuf.at[other], qbuf.at[other], ssem.at[6 + other]).wait()
    flush(caps - 2).wait()
    flush(caps - 1).wait()
    plane.finish(ticks + 2, [sum_c])
    scatter.finish(ticks + 2, [sum_a, sum_b])


def cross_backward(dc2, c2, lse, stats, qall, keys, vals, e, image, both, dco, dup, ddown, NDP, KV, cid):
    rows, ND = dc2.shape[0], NDP * KV
    caps = 4 * (rows // SEQ)
    dco, dup, ddown = blocks(dco, ND), blocks(dup, ND), blocks(ddown, ND)
    ins = [dc2, c2, lse, stats, qall, keys, vals, e, image, both, dco, dup, ddown]
    low = dco.shape[1]
    shapes = [(low, 2 * D), ddown.shape[1:], (low, FF - D)]
    return call(
        functools.partial(cross_backward_kernel, NDP, KV), "cross_backward",
        [arr((rows, D)), arr((D, D)), arr((D, D)), arr(keys.shape, F32)] + [arr(s, F32) for s in shapes],
        ins, [VM] * 9 + [ANY] * 4,
        [pltpu.VMEM(keys.shape, BF), pltpu.VMEM(keys.shape, BF), pltpu.VMEM((2, D, D), BF),
         pltpu.VMEM((2, keys.shape[0] // caps, D), F32),
         pltpu.VMEM((4, rows, D), BF), pltpu.VMEM((4, 32, QUAD), F32), pltpu.VMEM((4, rows, D), BF),
         pltpu.VMEM((4, rows, D), BF), DMA, DMA((2,)), DMA((2,)), DMA((10,)), DMA((12,))]
        + PlaneScatter.bufs(shapes[2:], ND) + PlaneScatter.sems(1, ND) + Scatter.bufs(shapes[:2], ND) + Scatter.sems(2, ND),
        4 * keys.shape[0] * D * D, out_specs=[VM] * 3 + [ANY] + [VM] * 3, cid=cid, limit=62 << 20)


def mlp_kernel(c2, x2, grad, gains, packed, wide, down, out, dx3, dc2, dup, ddown, dco, ng, wu, wd, wc, dh, acc, ht, sem):
    wcopy = load(packed.at[:, pl.ds(0, D)], wc, sem.at[8])
    wcopy.start()
    ups = [load(packed.at[:, pl.ds(D, D)] if j == 0 else wide.at[:, pl.ds((j - 1) * D, D)], wu.at[j], sem.at[j]) for j in range(4)]
    downs = [load(down.at[pl.ds(j * D, D), :], wd.at[j], sem.at[4 + j]) for j in range(4)]
    for j in range(4):
        ups[j].start()
        downs[j].start()
    low = c2[...].astype(BF)
    wcopy.wait()
    third = x2[...] + nn(low, wc[...])
    unit, scaled = unit_of(third)
    gain = gains[2:3]
    h3 = (unit * gain).astype(BF)
    ht[...] = h3.T
    g = grad[...]
    acc[...] = third
    for j in range(4):
        ups[j].wait()
        downs[j].wait()
        u = nn(h3, wu[j])
        square = u * u
        tanh_part = jnp.tanh(GELU_C * (u + GELU_A * square * u))
        active = (0.5 * u * (1.0 + tanh_part)).astype(BF)
        slope = 0.5 * (1.0 + tanh_part) + 0.5 * u * (1.0 - tanh_part * tanh_part) * GELU_C * (1.0 + 3.0 * GELU_A * square)
        acc[...] += nn(active, wd[j])
        du = (nt(g, wd[j]) * slope).astype(BF)
        part = nt(du, wu[j])
        dh[...] = part if j == 0 else dh[...] + part
        ddown[pl.ds(j * D, D), :] = tn(active, g).astype(BF)
        dup[:, pl.ds(j * D, D)] = nn(ht[...], du).astype(BF)
    out[...] = acc[...].astype(BF)
    upstream = dh[...]
    ng[...] = jnp.broadcast_to(jnp.sum(upstream * unit, 0, keepdims=True), ng.shape)
    total = g.astype(F32) + norm_backward(upstream, unit, scaled, gain)
    dx3[...] = total
    branch = total.astype(BF)
    dc2[...] = nt(branch, wc[...]).astype(BF)
    dco[...] = tn(low, branch).astype(BF)


def mlp(c2, x2, grad, gains, packed, wide, down):
    rows = c2.shape[0]
    return call(
        mlp_kernel, "feed_forward",
        [arr((rows, D)), arr((rows, D), F32), arr((rows, D)), arr((D, FF)), arr((FF, D)), arr((D, D)), arr((8, D), F32)],
        [c2, x2, grad, gains, packed, wide, down], [VM] * 4 + [ANY] * 3,
        [pltpu.VMEM((4, D, D), BF), pltpu.VMEM((4, D, D), BF), pltpu.VMEM((D, D), BF), pltpu.VMEM((rows, D), F32),
         pltpu.VMEM((rows, D), F32), pltpu.VMEM((D, rows), BF), DMA((9,))], 12 * rows * D * FF)


def deliver_kernel(moves, gain, *refs):
    sources, outs, sem = refs[: -len(moves[0]) - 2], refs[-len(moves[0]) - 2 : -2], refs[-1]
    norms = refs[-2]
    copies = []
    for (i, offset, width, j, to) in moves[1]:
        copies.append(load(sources[i].at[:, pl.ds(offset, width)], outs[j].at[:, pl.ds(to, width)], sem.at[len(copies)]))
    for copy in copies:
        copy.start()
    i, offset = gain
    block = sources[i][:, offset : offset + 128]
    block = jnp.concatenate([block, jnp.zeros((128 - block.shape[0], 128), F32)], 0)
    norms[...] = block.T[:8]
    for copy in copies:
        copy.wait()


def deliver(sources, widths, copies, gain):
    outs = [arr((rows, width), F32) for rows, width in widths]
    return call(
        functools.partial(deliver_kernel, (widths, copies), gain), "deliver_gradients",
        outs + [arr((8, 128), F32)], sources, [VM] * len(sources),
        [DMA((len(copies),))], 1, out_specs=[ANY] * len(outs) + [VM], limit=60 << 20)


def text_backward_kernel(dq2, dx3, text, x2, h1, h2, c1, q1, k1, v1, p1, gains, ng3, packed, tail, igrad,
                         text_grad, wq, wk, wv, wo, wcq, ngs, image_out, w, dq, dk, dv, rows_t, moved, sem, msem):
    size = igrad.shape[0] // 6
    pieces = [pl.ds(j * size, size) for j in range(6)]
    inward = [load(igrad.at[rows, :], moved.at[rows, :], msem.at[j]) for j, rows in enumerate(pieces)]
    outward = [load(moved.at[rows, :], image_out.at[rows, :], msem.at[j]) for j, rows in enumerate(pieces)]
    weights = [load(packed.at[:, pl.ds(j * D, D)] if j < 4 else tail.at[:, pl.ds(0, D)], w.at[j], sem.at[j]) for j in range(5)]
    for j in (4, 3, 0, 1, 2):
        weights[j].start()
    for copy in inward:
        copy.start()
    unit, scaled = unit_of(x2[...])
    weights[4].wait()
    upstream = nt(dq2[...], w[4])
    ngs_two = jnp.sum(upstream * unit, 0, keepdims=True)
    grad_two = dx3[...] + norm_backward(upstream, unit, scaled, gains[1:2])
    wcq[...] = tn(h2[...], dq2[...]).astype(BF)
    branch = grad_two.astype(BF)
    weights[3].wait()
    dc1 = nt(branch, w[3]).astype(BF)
    wo[...] = tn(c1[...], branch).astype(BF)
    for there, back in zip(inward, outward):
        there.wait()
        back.start()
    masks = head_masks(128)
    for pair in range(HEADS // 2):
        lanes = slice(pair * 128, (pair + 1) * 128)
        sums = [None] * 3
        for j, mask in enumerate(masks):
            low = p1[2 * pair + j]
            probs = low.astype(F32)
            above = dc1[:, lanes] * mask
            grad = nt(above, v1[:, lanes])
            grad = (probs * (grad - jnp.sum(probs * grad, -1, keepdims=True))).astype(BF)
            parts = [nn(grad, k1[:, lanes] * mask), tn(grad, q1[:, lanes] * mask), tn(low, above)]
            sums = parts if j == 0 else [a + b for a, b in zip(sums, parts)]
        dq[:, lanes] = (sums[0] * SCALE).astype(BF)
        dk[:, lanes] = (sums[1] * SCALE).astype(BF)
        dv[:, lanes] = sums[2].astype(BF)
    upstream = None
    flipped = h1[...].T
    for j, (ref, out) in enumerate(((dq, wq), (dk, wk), (dv, wv))):
        weights[j].wait()
        part = nt(ref[...], w[j])
        upstream = part if j == 0 else upstream + part
        out[...] = nn(flipped, ref[...]).astype(BF)
    unit, scaled = unit_of(text[...].astype(F32))
    text_grad[...] = grad_two + norm_backward(upstream, unit, scaled, gains[0:1])
    rows_t[...] = jnp.zeros_like(rows_t)
    rows_t[0:1] = jnp.sum(upstream * unit, 0, keepdims=True)
    rows_t[1:2] = ngs_two
    rows_t[2:3] = ng3[0:1]
    ngs[...] = rows_t[...].T.astype(BF)
    for copy in outward:
        copy.wait()


def text_backward(dq2, dx3, text, x2, h1, h2, c1, q1, k1, v1, p1, gains, ng3, packed, tail, igrad):
    rows = text.shape[0]
    ins = [dq2, dx3, text, x2, h1, h2, c1, q1, k1, v1, p1, gains, ng3, packed, tail, igrad]
    return call(
        text_backward_kernel, "text_backward",
        [arr((rows, D), F32)] + [arr((D, D))] * 5 + [arr((D, 128)), arr(igrad.shape, F32)],
        ins, [VM] * 13 + [ANY] * 3,
        [pltpu.VMEM((5, D, D), BF)] + [pltpu.VMEM((rows, D), BF)] * 3 + [pltpu.VMEM((128, D), F32), pltpu.VMEM(igrad.shape, F32), DMA((5,)), DMA((6,))],
        20 * rows * D * D, out_specs=[VM] * 7 + [ANY], limit=60 << 20)


def apart(text, image, lengths, patches, firsts, crosses, out_part, up_part, down_part, ndp, nkv):
    packed, tail = (a.reshape(D, -1) for a in all_gather(firsts[:4] + crosses + firsts[4:], ndp, nkv, 1))
    packed, both = packed[:, : 4 * D], packed[:, 4 * D :]
    h1, q1, k1, v1, p1, c1, x2, h2, q2, gains = text_forward(text, packed, tail)
    c2, lse, keys, vals, e, stats, qall, second, third, down = cross_forward(
        q2, image, lengths, patches, both, out_part, up_part, down_part, ndp, nkv, 2)
    second, third, down = second.reshape(D, -1), third.reshape(D, -1), down.reshape(FF, D)
    return h1, q1, k1, v1, p1, c1, x2, h2, gains, c2, lse, stats, qall, keys, vals, e, packed, tail, both, second, third, down


def per_device(
    text_tokens, image_tokens, image_lengths, patch_mask, self_query, self_key, self_value, self_out, cross_query,
    cross_key, cross_value, cross_out, mlp_up, mlp_down, norm_self, norm_cross, norm_mlp, out_grad,
):
    ndp, nkv = lax.axis_size("dp"), lax.axis_size("kv")
    caps, tokens = image_tokens.shape[0], image_tokens.shape[1]
    gain_block = jnp.pad(jnp.stack([norm_self, norm_cross, norm_mlp], 1), ((0, 0), (0, 125)))
    parts = [self_query, self_key, self_value, self_out, cross_query, gain_block]
    crosses = [cross_key, cross_value]
    image = image_tokens.reshape(caps * tokens, D)
    if self_query.shape[0] % 8 == 0:
        (h1, q1, k1, v1, p1, c1, x2, h2, gains, c2, lse, stats, qall, keys, vals, e, packed, tail, both, second, third, down) = forward(
            text_tokens, image, image_lengths, patch_mask, parts, crosses, cross_out, mlp_up, mlp_down, ndp, nkv, 1)
    else:
        (h1, q1, k1, v1, p1, c1, x2, h2, gains, c2, lse, stats, qall, keys, vals, e, packed, tail, both, second, third, down) = apart(
            text_tokens, image, image_lengths, patch_mask, parts, crosses, cross_out, mlp_up, mlp_down, ndp, nkv)
    layer_out, dx3, dc2, d_up, d_down, d_co, ng3 = mlp(c2, x2, out_grad, gains, second, third, down)
    dq2, d_ck, d_cv, igrad, sum_a, sum_b, sum_c = cross_backward(
        dc2, c2, lse, stats, qall, keys, vals, e, image, both, d_co, d_up, d_down, ndp, nkv, 3)
    text_grad, d_q, d_k, d_v, d_o, d_cq, ngs, image_grad = text_backward(
        dq2, dx3, text_tokens, x2, h1, h2, c1, q1, k1, v1, p1, gains, ng3, packed, tail, igrad)
    sum_d, sum_e = reduce_scatter([d_q, d_k, d_v, d_o, d_cq, d_ck, d_cv, ngs], ndp, nkv, 4)
    rows = norm_self.shape[0]
    moves = [(3, j * D, D, j, 0) for j in range(6)] + [(4, 0, D, 6, 0), (0, 0, D, 7, 0), (0, D, D, 8, 0), (2, 0, FF - D, 8, D), (1, 0, D, 9, 0)]
    *parts, norms = deliver(
        [sum_a, sum_b, sum_c, sum_d, sum_e], [(rows, D)] * 8 + [(rows, FF), mlp_down.shape], moves, (4, D))
    return (layer_out, text_grad, image_grad.reshape(caps, tokens, D), *parts, norms[0, :rows], norms[1, :rows], norms[2, :rows])


def solution(mesh):
    in_specs = (
        P(("dp", "kv"), None),
        P("dp", "kv", None),
        P("dp"),
        P("dp", "kv"),
        P(("dp", "kv"), None),
        P(("dp", "kv"), None),
        P(("dp", "kv"), None),
        P(("dp", "kv"), None),
        P(("dp", "kv"), None),
        P(("dp", "kv"), None),
        P(("dp", "kv"), None),
        P(("dp", "kv"), None),
        P(("dp", "kv"), None),
        P(("dp", "kv"), None),
        P(("dp", "kv")),
        P(("dp", "kv")),
        P(("dp", "kv")),
        P(("dp", "kv"), None),
    )
    out_specs = (
        P(("dp", "kv"), None),
        P(("dp", "kv"), None),
        P("dp", "kv", None),
        P(("dp", "kv"), None),
        P(("dp", "kv"), None),
        P(("dp", "kv"), None),
        P(("dp", "kv"), None),
        P(("dp", "kv"), None),
        P(("dp", "kv"), None),
        P(("dp", "kv"), None),
        P(("dp", "kv"), None),
        P(("dp", "kv"), None),
        P(("dp", "kv"), None),
        P(("dp", "kv")),
        P(("dp", "kv")),
        P(("dp", "kv")),
    )
    return jax.shard_map(
        per_device, mesh=mesh, in_specs=in_specs, out_specs=out_specs, check_vma=False
    )
```

```python
import functools
import types

import jax
import jax.numpy as jnp
from jax import lax
from jax.experimental import pallas as pl
from jax.experimental.pallas import tpu as pltpu
from jax.sharding import PartitionSpec as P

MESH = pl.DeviceIdType.MESH
def place(NDP, KV):
    di, ki = lax.axis_index("dp"), lax.axis_index("kv")
    Y = 2
    z, y, x, c = di // Y, di % Y, ki // 2, ki % 2
    y2, x2 = y + c*(1-2*y), x + (1-c)*(1-2*x)
    y3, x3 = y + (1-c)*(1-2*y), x + c*(1-2*x)
    return types.SimpleNamespace(
        di=di, ki=ki, z=z, y=y, x=x, c=c, Y=Y, Z=NDP//Y, KV=KV,
        split=((y2, x2), (y3, x3)), fixed=((y, 1-x), (1-y, x)), up=(di + Y, ki), dn=(di - Y, ki),
        px=(di, 2*(1-x) + c), py=(z*Y+1-y, ki), pd=(di, ki + 1 - 2*c), diag=(di, 2*(1-x) + 1 - c))

def enter(at, group=False):
    bar = pltpu.get_barrier_semaphore()
    @pl.when(at.z < at.Z-1)
    def _(): pl.semaphore_signal(bar, 1, device_id=at.up, device_id_type=MESH)
    @pl.when(at.z > 0)
    def _(): pl.semaphore_signal(bar, 1, device_id=at.dn, device_id_type=MESH)
    peers = (at.px, at.py, at.pd) + ((at.diag,) if group else ())
    for p in peers: pl.semaphore_signal(bar, 1, device_id=p, device_id_type=MESH)
    pl.semaphore_wait(bar, len(peers) + jnp.where(at.z < at.Z-1, 1, 0) + jnp.where(at.z > 0, 1, 0))

class Gather:
    def __init__(self, at, ins, outs, sems, route):
        self.at, self.ins, self.outs = at, ins, outs
        self.recv, self.sz, self.s2, self.s3, self.sd, self.sl = sems
        self.n = len(ins)
        self.own = self.slot(at.z, at.y, at.x)
        (self.y2, self.x2), (self.y3, self.x3) = route
        self.p2, self.p3 = ((at.z*at.Y+yy, 2*xx+at.c) for yy, xx in route)

    @staticmethod
    def sems(n, ND):
        Z = ND // 8
        D = pltpu.SemaphoreType.DMA
        return [D((n, ND)), D((n, 2, Z)), D((n, Z)), D((n, 2*Z)), D((n, ND//2)), D((n,))]

    def at_slot(self, i, s):
        out, rows = self.outs[i], self.ins[i].shape[0]
        if len(out.shape) == 3: return out.at[s]
        return out.at[pl.ds(pl.multiple_of(s * rows, 8), rows), :]

    def slot(self, zz, yy, xx):
        return (zz*self.at.Y+yy)*self.at.KV + xx*2 + self.at.c

    def send(self, s, sems, dev, own=False):
        for i in range(self.n):
            pltpu.make_async_remote_copy(
                src_ref=self.ins[i] if own else self.at_slot(i, s), dst_ref=self.at_slot(i, s), send_sem=sems(i),
                recv_sem=self.recv.at[i, s], device_id=dev, device_id_type=MESH).start()

    def arrive(self, s):
        for i in range(self.n):
            pltpu.make_async_copy(self.at_slot(i, s), self.at_slot(i, s), self.recv.at[i, s]).wait()

    def spread(self, zz, own=False):
        s = self.slot(zz, self.at.y, self.at.x)
        self.send(s, lambda i: self.s2.at[i, zz], self.p2, own)
        self.send(s, lambda i: self.s3.at[i, zz], self.p3, own)
        self.send(s, lambda i: self.sd.at[i, s//2], self.at.pd, own)

    def start(self):
        at, own = self.at, self.own
        @pl.when(at.z < at.Z-1)
        def _(): self.send(own, lambda i: self.sz.at[i, 0, at.z], at.up, True)
        @pl.when(at.z > 0)
        def _(): self.send(own, lambda i: self.sz.at[i, 1, at.z], at.dn, True)
        self.spread(at.z, True)
        for i in range(self.n):
            pltpu.make_async_copy(self.ins[i], self.at_slot(i, own), self.sl.at[i]).start()

    def second(self, zz):
        at = self.at
        s = self.slot(zz, self.y2, self.x2)
        self.arrive(s)
        self.send(s, lambda i: self.s3.at[i, at.Z+zz], self.p3)
        self.send(s, lambda i: self.sd.at[i, s//2], at.pd)

    def near(self, t):
        at = self.at
        @pl.when(at.z >= t)
        def _():
            s = self.slot(at.z-t, at.y, at.x); self.arrive(s)
            @pl.when(at.z < at.Z-1)
            def _(): self.send(s, lambda i: self.sz.at[i, 0, at.z-t], at.up)
            self.spread(at.z-t)
        @pl.when(at.z + t < at.Z)
        def _():
            s = self.slot(at.z+t, at.y, at.x); self.arrive(s)
            @pl.when(at.z > 0)
            def _(): self.send(s, lambda i: self.sz.at[i, 1, at.z+t], at.dn)
            self.spread(at.z+t)
        @pl.when(at.z >= t-1)
        def _(): self.second(at.z-t+1)
        @pl.when(jnp.logical_and(t > 1, at.z+t-1 < at.Z))
        def _(): self.second(at.z+t-1)

    def third(self, zz):
        at = self.at
        for yy, xx in ((self.y3, self.x3), (1-at.y, 1-at.x)):
            s = self.slot(zz, yy, xx)
            self.arrive(s)
            self.send(s, lambda i: self.sd.at[i, s//2], at.pd)

    def far(self, t):
        at = self.at
        @pl.when(at.z >= t)
        def _(): self.third(at.z-t)
        @pl.when(jnp.logical_and(t > 0, at.z+t < at.Z))
        def _(): self.third(at.z+t)

    def tick(self, k):
        if k < self.at.Z: self.near(jnp.int32(k+1))
        elif k < 2*self.at.Z: self.far(jnp.int32(k-self.at.Z))

    def finish(self, k=0):
        at, Z, n = self.at, self.at.Z, self.n
        lax.fori_loop(min(k, Z)+1, Z+1, lambda t, _: (self.near(t), 0)[1], 0)
        lax.fori_loop(max(k-Z, 0), Z, lambda t, _: (self.far(t), 0)[1], 0)
        def fin(h, _):
            self.arrive(2*h + 1 - at.c)
            for i in range(n):
                o = self.at_slot(i, 0)
                pltpu.make_async_copy(o, o, self.sd.at[i, h]).wait()
            return 0
        lax.fori_loop(0, at.KV*Z, fin, 0)
        def finz(zz, _):
            for i in range(n):
                o = self.at_slot(i, 0)
                pltpu.make_async_copy(o, o, self.s2.at[i, zz]).wait()
                pltpu.make_async_copy(o, o, self.s3.at[i, zz]).wait()
                pltpu.make_async_copy(o, o, self.s3.at[i, Z+zz]).wait()
                @pl.when(jnp.logical_and(at.z < Z-1, zz <= at.z))
                def _(): pltpu.make_async_copy(o, o, self.sz.at[i, 0, zz]).wait()
                @pl.when(jnp.logical_and(at.z > 0, zz >= at.z))
                def _(): pltpu.make_async_copy(o, o, self.sz.at[i, 1, zz]).wait()
            return 0
        lax.fori_loop(0, Z, finz, 0)
        for i in range(n):
            pltpu.make_async_copy(self.ins[i], self.at_slot(i, self.own), self.sl.at[i]).wait()

class PlaneGather(Gather):
    @staticmethod
    def sems(n, ND):
        D = pltpu.SemaphoreType.DMA
        return [D((n, ND)), D((n, 2, ND)), D((n, 1)), D((n, 2)), D((n, ND//2)), D((n,))]

    def onward(self, s, up, down, own=False):
        at = self.at
        if up:
            @pl.when(at.z < at.Z-1)
            def _(): self.send(s, lambda i: self.sz.at[i, 0, s], at.up, own)
        if down:
            @pl.when(at.z > 0)
            def _(): self.send(s, lambda i: self.sz.at[i, 1, s], at.dn, own)
        self.send(s, lambda i: self.sd.at[i, s//2], at.pd, own)

    def start(self):
        own = self.own
        self.send(own, lambda i: self.s2.at[i, 0], self.p2, True)
        self.send(own, lambda i: self.s3.at[i, 0], self.p3, True)
        self.onward(own, True, True, True)
        for i in range(self.n):
            pltpu.make_async_copy(self.ins[i], self.at_slot(i, own), self.sl.at[i]).start()

    def lines(self):
        at = self.at
        return ((at.y, at.x), (self.y2, self.x2), (self.y3, self.x3), (1-at.y, 1-at.x))

    def plane(self):
        at = self.at
        for j, (yy, xx) in enumerate(self.lines()[1:]):
            s = self.slot(at.z, yy, xx)
            self.arrive(s)
            if j == 0: self.send(s, lambda i: self.s3.at[i, 1], self.p3)
            self.onward(s, True, True)

    def level(self, t):
        at = self.at
        @pl.when(at.z >= t)
        def _():
            for yy, xx in self.lines():
                s = self.slot(at.z-t, yy, xx)
                self.arrive(s)
                self.onward(s, True, False)
        @pl.when(at.z + t < at.Z)
        def _():
            for yy, xx in self.lines():
                s = self.slot(at.z+t, yy, xx)
                self.arrive(s)
                self.onward(s, False, True)

    def tick(self, k):
        if k == 0: self.plane()
        elif k < self.at.Z: self.level(jnp.int32(k))

    def finish(self, k=0):
        at, Z, n = self.at, self.at.Z, self.n
        if k == 0: self.plane()
        lax.fori_loop(max(k, 1), Z, lambda t, _: (self.level(t), 0)[1], 0)
        def wait(i, sem):
            o = self.at_slot(i, 0)
            pltpu.make_async_copy(o, o, sem).wait()
        def fin(h, _):
            self.arrive(2*h + 1 - at.c)
            s = 2*h + at.c
            level = s // (at.Y * at.KV)
            for i in range(n):
                wait(i, self.sd.at[i, h])
                @pl.when(jnp.logical_and(at.z < Z-1, level <= at.z))
                def _(): wait(i, self.sz.at[i, 0, s])
                @pl.when(jnp.logical_and(at.z > 0, level >= at.z))
                def _(): wait(i, self.sz.at[i, 1, s])
            return 0
        lax.fori_loop(0, at.KV*Z, fin, 0)
        for i in range(n):
            for sem in (self.s2.at[i, 0], self.s3.at[i, 0], self.s3.at[i, 1]): wait(i, sem)
            pltpu.make_async_copy(self.ins[i], self.at_slot(i, self.own), self.sl.at[i]).wait()

def fill_block(parts, block, sem):
    copies, offset = [], 0
    for j, part in enumerate(parts):
        copies.append(pltpu.make_async_copy(part, block.at[:, pl.ds(offset, part.shape[1])], sem.at[j]))
        offset += part.shape[1]
    for copy in copies: copy.start()
    return copies

def ag_kernel(NDP, KV, count, *refs):
    parts, outs, packs, fill = refs[:count], refs[count:count+2], refs[count+2:count+4], refs[count+4]
    copies = fill_block(parts[:-2], packs[0], fill)
    copies += fill_block(parts[-2:], packs[1], fill.at[pl.ds(count-2, 2)])
    at = place(NDP, KV)
    enter(at)
    for copy in copies: copy.wait()
    k = count+5
    plane = PlaneGather(at, [packs[1]], [outs[1]], refs[k+6:], at.split)
    gather = Gather(at, [packs[0]], [outs[0]], refs[k:k+6], at.split)
    plane.start()
    gather.start()
    plane.tick(0)
    for k in range(1, min(at.Z, 4)):
        gather.tick(k-1)
        plane.tick(k)
    gather.finish(min(at.Z, 4)-1)
    plane.finish(min(at.Z, 4))

def all_gather(parts, NDP, KV, cid):
    ND = NDP*KV
    rows = parts[0].shape[0]
    widths = [sum(p.shape[1] for p in some) for some in (parts[:-2], parts[-2:])]
    return pl.pallas_call(
        functools.partial(ag_kernel, NDP, KV, len(parts)),
        out_shape=[jax.ShapeDtypeStruct((ND, rows, width), jnp.bfloat16) for width in widths],
        in_specs=[pl.BlockSpec(memory_space=pl.ANY)]*len(parts),
        out_specs=[pl.BlockSpec(memory_space=pl.ANY)]*2,
        scratch_shapes=[pltpu.VMEM((rows, width), jnp.bfloat16) for width in widths] + [pltpu.SemaphoreType.DMA((len(parts),))]
            + Gather.sems(1, ND) + PlaneGather.sems(1, ND),
        compiler_params=pltpu.CompilerParams(collective_id=cid, has_side_effects=True, vmem_limit_bytes=60<<20),
        name="gather_weights",
    )(*parts)


class Scatter:
    count = 9

    def __init__(self, at, sources, bufs, sems, route):
        self.at, self.sources = at, sources
        self.n = n = len(bufs) // 5
        self.loc, self.r1, self.r2, self.r3, self.rz = (bufs[j*n:(j+1)*n] for j in range(5))
        self.sl, self.sd, self.qd, self.s2, self.q2, self.s3, self.q3, self.sz, self.qz = sems
        (self.y2, self.x2), (self.y3, self.x3) = route
        self.p2, self.p3 = ((at.z*at.Y+yy, 2*xx+at.c) for yy, xx in route)
        self.lines = ((at.y, at.x), (self.y2, self.x2), (self.y3, self.x3), (1-at.y, 1-at.x))

    @staticmethod
    def bufs(shapes, ND):
        Z = ND // 8
        return [pltpu.VMEM(lead + tuple(s), jnp.bfloat16)
                for lead in ((ND//2,), (ND//2,), (2*Z,), (Z,), (2, Z)) for s in shapes]

    @staticmethod
    def sems(n, ND):
        Z = ND // 8
        D = pltpu.SemaphoreType.DMA
        return [D((n, ND//2))]*3 + [D((n, 2*Z))]*2 + [D((n, Z))]*2 + [D((n, 2, Z))]*2

    def half(self, zz, yy, xx): return (zz*self.at.Y+yy)*(self.at.KV//2) + xx

    def send(self, src, dst, ss, rsem, dev):
        pltpu.make_async_remote_copy(
            src_ref=src, dst_ref=dst, send_sem=ss, recv_sem=rsem, device_id=dev, device_id_type=MESH).start()

    def wait(self, ref, sem): pltpu.make_async_copy(ref, ref, sem).wait()

    def both(self, t, f):
        at = self.at
        @pl.when(at.z >= t)
        def _(): f(at.z-t)
        @pl.when(jnp.logical_and(t > 0, at.z+t < at.Z))
        def _(): f(at.z+t)

    def every(self, f):
        Z = self.at.Z
        lax.fori_loop(0, Z, lambda k, _: (self.both(Z-1-k, f), 0)[1], 0)

    def start(self):
        c = self.at.c
        def one(zz):
            for yy, xx in self.lines[::-1]:
                h = self.half(zz, yy, xx)
                for ref, i, off, dst, width in self.sources:
                    to, cols = pl.ds(dst, width), pl.ds(off, width)
                    self.send(ref.at[2*h+1-c, :, cols], self.r1[i].at[h, :, to], self.sd.at[i, h], self.qd.at[i, h], self.at.pd)
                    pltpu.make_async_copy(ref.at[2*h+c, :, cols], self.loc[i].at[h, :, to], self.sl.at[i, h]).start()
        self.every(one)

    def pair(self, h):
        for i in range(self.n):
            self.wait(self.loc[i].at[h], self.sl.at[i, h]); self.wait(self.r1[i].at[h], self.qd.at[i, h])
            self.loc[i][h] = self.loc[i][h] + self.r1[i][h]

    def first(self):
        def one(zz):
            for j, (yy, xx) in enumerate((self.lines[3], self.lines[2])):
                h = self.half(zz, yy, xx)
                self.pair(h)
                for i in range(self.n):
                    self.send(self.loc[i].at[h], self.r2[i].at[2*zz+j], self.s2.at[i, 2*zz+j], self.q2.at[i, 2*zz+j], self.p3)
            for yy, xx in self.lines[:2]: self.pair(self.half(zz, yy, xx))
        self.every(one)

    def second(self, t):
        at, Z = self.at, self.at.Z
        def one(zz):
            for j, (yy, xx) in enumerate((self.lines[1], self.lines[0])):
                h = self.half(zz, yy, xx)
                for i in range(self.n):
                    self.wait(self.r2[i].at[2*zz+j], self.q2.at[i, 2*zz+j])
                    self.loc[i][h] = self.loc[i][h] + self.r2[i][2*zz+j]
                    if j == 0:
                        self.send(self.loc[i].at[h], self.r3[i].at[zz], self.s3.at[i, zz], self.q3.at[i, zz], self.p2)
        self.both(t, one)
        def along(zz, d, dev, has):
            h = self.half(zz, at.y, at.x)
            for i in range(self.n):
                loc, rz = self.loc[i], self.rz[i]
                self.wait(self.r3[i].at[zz], self.q3.at[i, zz])
                @pl.when(has)
                def _():
                    self.wait(rz.at[d, zz], self.qz.at[i, d, zz])
                    loc[h] = loc[h] + self.r3[i][zz] + rz[d, zz]
                @pl.when(jnp.logical_not(has))
                def _(): loc[h] = loc[h] + self.r3[i][zz]
                self.send(loc.at[h], rz.at[d, zz], self.sz.at[i, d, zz], self.qz.at[i, d, zz], dev)
        u = t + 1
        @pl.when(at.z + u < Z)
        def _(): along(at.z+u, 0, at.up, at.z > 0)
        @pl.when(at.z >= u)
        def _(): along(at.z-u, 1, at.dn, at.z < Z-1)

    def tick(self, k):
        if k == 0: self.first()
        elif k <= self.at.Z: self.second(jnp.int32(self.at.Z-k))

    def rest(self, k):
        Z = self.at.Z
        if k == 0: self.first()
        lax.fori_loop(max(k, 1), Z+1, lambda j, _: (self.second(Z-j), 0)[1], 0)

    def finish(self, k, outs):
        at, Z, z = self.at, self.at.Z, self.at.z
        self.rest(k)
        h = self.half(z, at.y, at.x)
        for i, out in enumerate(outs):
            self.wait(self.r3[i].at[z], self.q3.at[i, z])
            out[...] = self.loc[i][h].astype(jnp.float32) + self.r3[i][z].astype(jnp.float32)
            for d, has in ((0, z > 0), (1, z < Z-1)):
                @pl.when(has)
                def _():
                    self.wait(self.rz[i].at[d, z], self.qz.at[i, d, z])
                    out[...] += self.rz[i][d, z].astype(jnp.float32)
        def fin(h, _):
            for i in range(self.n): self.wait(self.r1[i].at[h], self.sd.at[i, h])
            return 0
        lax.fori_loop(0, at.KV*Z, fin, 0)
        def fin2(zz, _):
            for i in range(self.n):
                self.wait(self.r3[i].at[zz], self.s3.at[i, zz])
                for j in range(2): self.wait(self.r2[i].at[2*zz+j], self.s2.at[i, 2*zz+j])
                @pl.when(zz > z)
                def _(): self.wait(self.rz[i].at[0, zz], self.sz.at[i, 0, zz])
                @pl.when(zz < z)
                def _(): self.wait(self.rz[i].at[1, zz], self.sz.at[i, 1, zz])
            return 0
        lax.fori_loop(0, Z, fin2, 0)

class PlaneScatter(Scatter):
    @staticmethod
    def bufs(shapes, ND):
        Z = ND // 8
        return [pltpu.VMEM(lead + tuple(s), jnp.bfloat16)
                for lead in ((ND//2,), (ND//2,), (2,), (1,), (2, 4*Z)) for s in shapes]

    @staticmethod
    def sems(n, ND):
        Z = ND // 8
        D = pltpu.SemaphoreType.DMA
        return [D((n, ND//2))]*3 + [D((n, 2))]*2 + [D((n, 1))]*2 + [D((n, 2, 4*Z))]*2

    def chain(self, t):
        at, Z = self.at, self.at.Z
        def along(zz, d, dev, has):
            for l, (yy, xx) in enumerate(self.lines):
                h = self.half(zz, yy, xx)
                k = 4*zz + l
                self.pair(h)
                for i in range(self.n):
                    loc, rz = self.loc[i], self.rz[i]
                    @pl.when(has)
                    def _():
                        self.wait(rz.at[d, k], self.qz.at[i, d, k])
                        loc[h] = loc[h] + rz[d, k]
                    self.send(loc.at[h], rz.at[d, k], self.sz.at[i, d, k], self.qz.at[i, d, k], dev)
        @pl.when(at.z + t < Z)
        def _(): along(at.z+t, 0, at.up, at.z > 0)
        @pl.when(at.z >= t)
        def _(): along(at.z-t, 1, at.dn, at.z < Z-1)

    def level(self):
        at, z = self.at, self.at.z
        for l, (yy, xx) in reversed(list(enumerate(self.lines))):
            h = self.half(z, yy, xx)
            k = 4*z + l
            self.pair(h)
            for i in range(self.n):
                loc, rz = self.loc[i], self.rz[i]
                for d, has in ((0, z > 0), (1, z < at.Z-1)):
                    @pl.when(has)
                    def _():
                        self.wait(rz.at[d, k], self.qz.at[i, d, k])
                        loc[h] = loc[h] + rz[d, k]
                if l >= 2:
                    self.send(loc.at[h], self.r2[i].at[3-l], self.s2.at[i, 3-l], self.q2.at[i, 3-l], self.p3)

    def plane(self):
        for j, (yy, xx) in enumerate((self.lines[1], self.lines[0])):
            h = self.half(self.at.z, yy, xx)
            for i in range(self.n):
                self.wait(self.r2[i].at[j], self.q2.at[i, j])
                self.loc[i][h] = self.loc[i][h] + self.r2[i][j]
                if j == 0: self.send(self.loc[i].at[h], self.r3[i].at[0], self.s3.at[i, 0], self.q3.at[i, 0], self.p2)

    def tick(self, k):
        Z = self.at.Z
        if k < Z-1: self.chain(jnp.int32(Z-1-k))
        elif k == Z-1: self.level()
        elif k == Z: self.plane()

    def finish(self, k, outs):
        at, Z, z = self.at, self.at.Z, self.at.z
        lax.fori_loop(min(k, Z-1), Z-1, lambda j, _: (self.chain(Z-1-j), 0)[1], 0)
        if k <= Z-1: self.level()
        if k <= Z: self.plane()
        h = self.half(z, at.y, at.x)
        for i, out in enumerate(outs):
            self.wait(self.r3[i].at[0], self.q3.at[i, 0])
            out[...] = self.loc[i][h].astype(jnp.float32) + self.r3[i][0].astype(jnp.float32)
        def fin(h, _):
            zz = h // (at.Y * at.KV // 2)
            for i in range(self.n):
                self.wait(self.r1[i].at[h], self.sd.at[i, h])
                for d, cond in ((0, zz > z), (1, zz < z)):
                    @pl.when(cond)
                    def _(): self.wait(self.rz[i].at[d, h], self.sz.at[i, d, h])
            return 0
        lax.fori_loop(0, at.KV*Z, fin, 0)
        for i in range(self.n):
            self.wait(self.r3[i].at[0], self.s3.at[i, 0])
            for j in range(2): self.wait(self.r2[i].at[j], self.s2.at[i, j])

def rs_kernel(NDP, KV, count, *refs):
    parts, outs, k = refs[:count], refs[count:count+2], count+2
    at = place(NDP, KV)
    enter(at)
    def sources(some):
        found, offset = [], 0
        for ref in some:
            found.append((ref, 0, 0, offset, ref.shape[2]))
            offset += ref.shape[2]
        return found
    plane = PlaneScatter(at, sources(parts[-2:]), refs[k:k+5], refs[k+5:k+14], at.split)
    scatter = Scatter(at, sources(parts[:-2]), refs[k+14:k+19], refs[k+19:], at.split)
    plane.start()
    scatter.start()
    last = min(at.Z, 4)
    for j in range(last):
        plane.tick(j)
        scatter.tick(j)
    plane.finish(last, outs[1:])
    scatter.finish(last, outs[:1])

def blocks(g, ND): return g.reshape(ND, g.shape[0]//ND, g.shape[1])

def reduce_scatter(grads, NDP, KV, cid):
    ND = NDP*KV
    parts = [blocks(g, ND) for g in grads]
    rows = parts[0].shape[1]
    shapes = [(rows, sum(g.shape[2] for g in some)) for some in (parts[:-2], parts[-2:])]
    return pl.pallas_call(
        functools.partial(rs_kernel, NDP, KV, len(parts)),
        out_shape=[jax.ShapeDtypeStruct(s, jnp.float32) for s in shapes],
        in_specs=[pl.BlockSpec(memory_space=pl.ANY)]*len(parts),
        out_specs=[pl.BlockSpec(memory_space=pltpu.VMEM)]*2,
        scratch_shapes=PlaneScatter.bufs(shapes[1:], ND) + PlaneScatter.sems(1, ND) + Scatter.bufs(shapes[:1], ND) + Scatter.sems(1, ND),
        compiler_params=pltpu.CompilerParams(collective_id=cid, has_side_effects=True, vmem_limit_bytes=60<<20),
        name="scatter_gradients",
    )(*parts)


D = 768
FF = 3072
HEADS = 12
HD = 64
SEQ = 64
QUAD = 4 * HD
EPS = 1e-05
NEG = -1e30
GELU_C = 0.7978845608028654
GELU_A = 0.044715
SCALE = 0.125
BF = jnp.bfloat16
F32 = jnp.float32
VM = pl.BlockSpec(memory_space=pltpu.VMEM)
ANY = pl.BlockSpec(memory_space=pl.ANY)
DMA = pltpu.SemaphoreType.DMA


def nn(a, b):
    return lax.dot_general(a, b, (((1,), (0,)), ((), ())), preferred_element_type=F32)


def nt(a, b):
    return lax.dot_general(a, b, (((1,), (1,)), ((), ())), preferred_element_type=F32)


def tn(a, b):
    return lax.dot_general(a, b, (((0,), (0,)), ((), ())), preferred_element_type=F32)


def unit_of(values):
    centre = values - jnp.mean(values, -1, keepdims=True)
    scaled = lax.rsqrt(jnp.mean(centre * centre, -1, keepdims=True) + EPS)
    return centre * scaled, scaled


def norm_backward(upstream, unit, scaled, gain):
    through = upstream * gain
    return scaled * (
        through - jnp.mean(through, -1, keepdims=True) - unit * jnp.mean(through * unit, -1, keepdims=True)
    )


def head_masks(width):
    lane = lax.broadcasted_iota(jnp.int32, (1, width), 1) // HD
    return [(lane == head).astype(F32).astype(BF) for head in range(width // HD)]


def stacked(values, masks):
    return jnp.concatenate([values * mask for mask in masks], 0)


def own_blocks(values):
    lane = lax.broadcasted_iota(jnp.int32, (HD, QUAD), 1) // HD
    total = values[:HD]
    for head in range(1, 4):
        total = jnp.where(lane == head, values[head * HD : (head + 1) * HD], total)
    return total


def load(source, target, sem):
    return pltpu.make_async_copy(source, target, sem)


def call(kernel, name, outs, ins, specs, scratch, flops, out_specs=None, cid=None, limit=56 << 20):
    params = dict(vmem_limit_bytes=limit)
    if cid is not None:
        params.update(collective_id=cid, has_side_effects=True)
    size = lambda a: a.size * a.dtype.itemsize
    return pl.pallas_call(
        kernel,
        out_shape=outs,
        in_specs=specs,
        out_specs=out_specs or [VM] * len(outs),
        scratch_shapes=scratch,
        compiler_params=pltpu.CompilerParams(**params),
        cost_estimate=pl.CostEstimate(flops=int(flops), transcendentals=0, bytes_accessed=sum(map(size, ins)) + sum(map(size, outs))),
        name=name,
    )(*ins)


def arr(shape, dtype=BF):
    return jax.ShapeDtypeStruct(shape, dtype)


def text_forward_kernel(text, packed, tail, h1, q1, k1, v1, p1, c1, x2, h2, q2, gains, w, gw, sem, between=lambda k: None):
    weights = [load(packed.at[:, pl.ds(j * D, D)] if j < 4 else tail.at[:, pl.ds(0, D)], w.at[j], sem.at[j]) for j in range(5)]
    gcopy = load(tail.at[:, pl.ds(D, 128)], gw, sem.at[5])
    gcopy.start()
    for copy in weights:
        copy.start()
    x = text[...].astype(F32)
    unit, _ = unit_of(x)
    gcopy.wait()
    gains[...] = gw[...].astype(F32).T[:8]
    h1[...] = (unit * gains[0:1]).astype(BF)
    for j, ref in enumerate((q1, k1, v1)):
        weights[j].wait()
        ref[...] = nn(h1[...], w[j]).astype(BF)
    between(0)
    rows = text.shape[0]
    first = lax.broadcasted_iota(jnp.int32, (rows, rows), 0)
    second = lax.broadcasted_iota(jnp.int32, (rows, rows), 1)
    allowed = jnp.logical_and(first >= second, first // SEQ == second // SEQ)
    masks = head_masks(128)
    for pair in range(HEADS // 2):
        lanes = slice(pair * 128, (pair + 1) * 128)
        total = None
        for j, mask in enumerate(masks):
            scores = nt(q1[:, lanes] * mask, k1[:, lanes]) * SCALE
            scores = jnp.where(allowed, scores, NEG)
            powers = jnp.exp(scores - jnp.max(scores, -1, keepdims=True))
            probs = (powers / jnp.sum(powers, -1, keepdims=True)).astype(BF)
            p1[2 * pair + j] = probs
            part = nn(probs, v1[:, lanes] * mask)
            total = part if total is None else total + part
        c1[:, lanes] = total.astype(BF)
    between(1)
    weights[3].wait()
    second_res = x + nn(c1[...], w[3])
    x2[...] = second_res
    unit, _ = unit_of(second_res)
    h2[...] = (unit * gains[1:2]).astype(BF)
    weights[4].wait()
    q2[...] = nn(h2[...], w[4]).astype(BF)


def text_forward(text, packed, tail):
    rows = text.shape[0]
    low = arr((rows, D))
    return call(
        text_forward_kernel, "text_forward",
        [low, low, low, low, arr((HEADS, rows, rows)), low, arr((rows, D), F32), low, low, arr((8, D), F32)],
        [text, packed, tail], [VM, ANY, ANY],
        [pltpu.VMEM((5, D, D), BF), pltpu.VMEM((D, 128), BF), DMA((6,))], 10 * rows * D * D)


TICKS = (3, 6, 8, 10)


def remote(src, dst, send, recv, device):
    return pltpu.make_async_remote_copy(
        src_ref=src, dst_ref=dst, send_sem=send, recv_sem=recv, device_id=device, device_id_type=MESH)


def cross_forward_kernel(NDP, KV, q2, image, lengths, patches, both, out_part, up_part, down_part,
                         c2, lse, keys, vals, e, stats, qall, second, third, down, w, obuf, ro, rst, usable, block, wide, down_block,
                         wsem, ssem, rsem, fsem, *gsems):
    at = place(NDP, KV)
    fills = fill_second(out_part, up_part, down_part, block, wide, down_block, fsem)
    found = cross_weights(both, w, wsem)
    own_copy = load(q2, qall.at[at.ki], wsem.at[2])
    own_copy.start()
    enter(at, True)
    for copy in fills:
        copy.wait()
    plane = PlaneGather(at, [wide], [third], gsems[6:], at.fixed)
    gather = Gather(at, [block, down_block], [second, down], gsems[:6], at.fixed)
    plane.start()
    gather.start()
    cross_forward_part(at, plane, gather, 0, lambda: found, own_copy, q2, image, lengths, patches,
                       c2, lse, keys, vals, e, stats, qall, w, obuf, ro, rst, usable, ssem, rsem)


def fill_second(out_part, up_part, down_part, block, wide, down_block, fsem):
    fills = fill_block([out_part, up_part.at[:, pl.ds(0, D)]], block, fsem)
    late = [load(down_part, down_block, fsem.at[2]), load(up_part.at[:, pl.ds(D, FF - D)], wide, fsem.at[3])]
    for copy in late:
        copy.start()
    return fills + late


def cross_weights(pair, w, sem):
    weights = [load(pair.at[:, pl.ds(j * D, D)], w.at[j], sem.at[j]) for j in range(2)]
    for copy in weights:
        copy.start()
    return weights


def cross_forward_part(at, plane, gather, done, weights, own_copy, q2, image, lengths, patches,
                       c2, lse, keys, vals, e, stats, qall, w, obuf, ro, rst, usable, ssem, rsem, after=lambda: None):
    di, ki, x, c = at.di, at.ki, at.x, at.c
    caps, tokens = patches.shape
    own_caps = caps // 4
    core, over, diag = 2 * x + 1 - c, 2 * (1 - x) + c, 2 * (1 - x) + 1 - c
    to_core = remote(q2, qall.at[ki], ssem.at[0], rsem.at[ki], (di, core))
    to_over = remote(q2, qall.at[ki], ssem.at[1], rsem.at[ki], (di, over))
    to_over.start()
    to_core.start()
    weights = weights()
    row = lax.broadcasted_iota(jnp.int32, usable.shape, 0)
    limit = jnp.zeros(usable.shape, jnp.int32)
    for cap in range(caps):
        limit = jnp.where(row == cap, lengths[cap], limit)
    position = lax.broadcasted_iota(jnp.int32, usable.shape, 1) + ki * tokens
    usable[...] = jnp.zeros(usable.shape, BF)
    usable[0:caps, :] = jnp.where(jnp.logical_and(position < limit, True)[0:caps], (patches[...] == 1).astype(F32), 0.0).astype(BF)
    weights[0].wait()

    def project(j, ref, i):
        rows = pl.ds(pl.multiple_of(i * tokens, 16), tokens)
        ref[rows, :] = nn(image[rows, :], w[j]).astype(BF)

    lax.fori_loop(0, caps, lambda i, _: (project(0, keys, i), 0)[1], 0)
    load(qall.at[over], qall.at[over], rsem.at[over]).wait()
    relay = remote(qall.at[over], qall.at[over], ssem.at[2], rsem.at[over], (di, core))
    relay.start()
    plane.tick(done)
    gather.tick(done)
    weights[1].wait()
    lax.fori_loop(0, caps, lambda i, _: (project(1, vals, i), 0)[1], 0)
    plane.tick(done + 1)
    gather.tick(done + 1)
    load(qall.at[core], qall.at[core], rsem.at[core]).wait()
    load(qall.at[diag], qall.at[diag], rsem.at[diag]).wait()
    own_copy.wait()
    masks = head_masks(QUAD)

    def owner_of(step):
        return 2 * ((x + 1 + step // 2) % 2) + (c + 1 + step % 2) % 2

    def attend(i, _):
        owner, local = owner_of(i // own_caps), i % own_caps
        cap = owner * own_caps + local
        rows = pl.ds(pl.multiple_of(cap * tokens, 16), tokens)
        queries = pl.ds(pl.multiple_of(local * SEQ, 16), SEQ)
        for j, when in enumerate(TICKS):
            @pl.when(i == when * caps // 12)
            def _():
                plane.tick(done + 2 + j)
                gather.tick(done + 2 + j)
        chosen = (lax.broadcasted_iota(jnp.int32, (usable.shape[0], QUAD), 0) == cap).astype(F32).astype(BF)
        shift = tn(usable[...], chosen)
        for g in range(3):
            lanes = slice(g * QUAD, (g + 1) * QUAD)
            scores = nt(keys[rows, lanes], stacked(qall[owner, queries, lanes], masks)) * SCALE
            scores = jnp.where(shift > 0.5, scores, NEG)
            top = jnp.max(scores, 0, keepdims=True)
            powers = jnp.where(shift > 0.5, jnp.exp(scores - top), 0.0)
            low = powers.astype(BF)
            e[pl.ds(pl.multiple_of((cap * 3 + g) * tokens, 16), tokens), :] = low
            stats[owner, pl.ds(3 * local + g, 1), :] = top
            stats[owner, pl.ds(16 + 3 * local + g, 1), :] = jnp.sum(powers, 0, keepdims=True)
            obuf[owner, queries, lanes] = own_blocks(tn(low, vals[rows, lanes])).astype(BF)

        @pl.when(jnp.logical_and(local == own_caps - 1, owner != ki))
        def _():
            remote(obuf.at[owner], ro.at[ki], ssem.at[3 + owner], rsem.at[4 + ki], (di, owner)).start()
            remote(stats.at[owner], rst.at[ki], ssem.at[7 + owner], rsem.at[8 + ki], (di, owner)).start()

        return 0

    lax.fori_loop(0, caps, attend, 0)
    after()
    ro[ki] = obuf[ki]
    rst[ki] = stats[ki]
    for other in (core, over, diag):
        load(ro.at[other], ro.at[other], rsem.at[4 + other]).wait()
        load(rst.at[other], rst.at[other], rsem.at[8 + other]).wait()
    lane = lax.broadcasted_iota(jnp.int32, (HD, QUAD), 1) // HD

    def combine(local, _):
        queries = pl.ds(pl.multiple_of(local * SEQ, 16), SEQ)
        for g in range(3):
            row = pl.ds(3 * local + g, 1)
            row_sum = pl.ds(16 + 3 * local + g, 1)
            tops = [rst[k, row, :] for k in range(4)]
            top = jnp.maximum(jnp.maximum(tops[0], tops[1]), jnp.maximum(tops[2], tops[3]))
            parts = [jnp.exp(t - top) for t in tops]
            total = sum(part * rst[k, row_sum, :] for k, part in enumerate(parts))
            lse[row, :] = top + jnp.log(total)
            table = jnp.concatenate([part / total for part in parts] * 2, 0).T
            mixed = 0.0
            for k in range(4):
                column = table[:, k : k + 1]
                weight = column[:HD] * jnp.ones((HD, QUAD), F32)
                for head in range(1, 4):
                    weight = jnp.where(lane == head, column[head * HD : (head + 1) * HD], weight)
                mixed = mixed + weight * ro[k, queries, g * QUAD : (g + 1) * QUAD].astype(F32)
            c2[queries, g * QUAD : (g + 1) * QUAD] = mixed
        return 0

    lax.fori_loop(0, own_caps, combine, 0)
    to_core.wait_send()
    to_over.wait_send()
    relay.wait_send()
    for other in (core, over, diag):
        load(obuf.at[other], obuf.at[other], ssem.at[3 + other]).wait()
        load(stats.at[other], stats.at[other], ssem.at[7 + other]).wait()
    plane.finish(done + 2 + len(TICKS))
    gather.finish(done + 2 + len(TICKS))


def forward_kernel(NDP, KV, *refs):
    text, image, lengths, patches, *parts = refs[:15]
    firsts, crosses, (out_part, up_part, down_part) = parts[:6], parts[6:8], parts[8:]
    h1, q1, k1, v1, p1, c1, x2, h2, gains, c2, lse, stats, qall, *outs = refs[15:37]
    keys_out, vals_out, e_out, packed, tail, both, second, third, down = outs
    (q2, tw, gw, keys, vals, e, pixels, w, obuf, ro, rst, usable, block, wide, down_block, pack, pack_tail, pack_both,
     tsem, wsem, ssem, rsem, fsem, sem, osem) = refs[37:62]
    gsems = refs[62:]
    copies = fill_block(firsts[:-2], pack, sem) + fill_block(firsts[-2:], pack_tail, sem.at[pl.ds(4, 2)])
    copies += fill_block(crosses, pack_both, sem.at[pl.ds(6, 2)])
    fills = fill_second(out_part, up_part, down_part, block, wide, down_block, fsem)
    image_copy = load(image, pixels, osem.at[3])
    image_copy.start()
    at = place(NDP, KV)
    enter(at, True)
    for copy in copies:
        copy.wait()
    plane = PlaneGather(at, [pack_tail], [tail], gsems[0:6], at.split)
    gather = Gather(at, [pack], [packed], gsems[6:12], at.split)
    middle = Gather(at, [pack_both], [both], gsems[12:18], at.split)
    late_plane = PlaneGather(at, [wide], [third], gsems[18:24], at.fixed)
    late = Gather(at, [block, down_block], [second, down], gsems[24:30], at.fixed)
    plane.start()
    gather.start()
    plane.tick(0)
    for copy in fills:
        copy.wait()
    image_copy.wait()
    last = min(at.Z, 4)
    for k in range(1, last):
        gather.tick(k - 1)
        plane.tick(k)
        if k == 1:
            middle.start()
        else:
            middle.tick(k - 2)
    late_plane.start()
    late.start()
    gather.finish(last - 1)
    plane.finish(last)

    def between(k):
        middle.tick(last - 2 + k)
        late_plane.tick(k)
        late.tick(k)

    text_forward_kernel(text, packed, tail, h1, q1, k1, v1, p1, c1, x2, h2, q2, gains, tw, gw, tsem, between)
    own_copy = load(q2, qall.at[at.ki], wsem.at[2])
    own_copy.start()
    results = [load(keys, keys_out, osem.at[0]), load(vals, vals_out, osem.at[1]), load(e, e_out, osem.at[2])]

    def weights():
        middle.finish(last)
        return cross_weights(both, w, wsem)

    def after():
        for copy in results:
            copy.start()

    cross_forward_part(at, late_plane, late, 2, weights, own_copy, q2, pixels, lengths, patches,
                       c2, lse, keys, vals, e, stats, qall, w, obuf, ro, rst, usable, ssem, rsem, after)
    for copy in results:
        copy.wait()


def forward(text, image, lengths, patches, firsts, crosses, out_part, up_part, down_part, NDP, KV, cid):
    rows, (caps, tokens), ND = text.shape[0], patches.shape, NDP * KV
    lows = out_part.shape[0]
    low, wide_row = arr((rows, D)), arr((rows, D), F32)
    keys, scores = (caps * tokens, D), (caps * 3 * tokens, QUAD)
    ins = [text, image, lengths, patches, *firsts, *crosses, out_part, up_part, down_part]
    V = pltpu.VMEM
    return call(
        functools.partial(forward_kernel, NDP, KV), "forward",
        [low, low, low, low, arr((HEADS, rows, rows)), low, wide_row, low, arr((8, D), F32),
         wide_row, arr((16, QUAD), F32), arr((4, 32, QUAD), F32), arr((4, rows, D)),
         arr(keys), arr(keys), arr(scores), arr((D, 4 * D)), arr((D, D + 128)), arr((D, 2 * D)),
         arr((D, 2 * D)), arr((D, FF - D)), arr((FF, D))],
        ins, [VM, ANY, pl.BlockSpec(memory_space=pltpu.SMEM), VM] + [ANY] * 11,
        [V((rows, D), BF), V((5, D, D), BF), V((D, 128), BF), V(keys, BF), V(keys, BF), V(scores, BF), V(keys, BF),
         V((2, D, D), BF), V((4, rows, D), BF), V((4, rows, D), BF), V((4, 32, QUAD), F32),
         V((-(-caps // 16) * 16, tokens), BF), V((lows, 2 * D), BF), V((lows, FF - D), BF), V(down_part.shape, BF),
         V((lows, 4 * D), BF), V((lows, D + 128), BF), V((lows, 2 * D), BF),
         DMA((6,)), DMA((3,)), DMA((11,)), DMA((12,)), DMA((4,)), DMA((8,)), DMA((4,))]
        + PlaneGather.sems(1, ND) + Gather.sems(1, ND) + Gather.sems(1, ND) + PlaneGather.sems(1, ND) + Gather.sems(2, ND),
        6 * caps * tokens * D * D, out_specs=[VM] * 13 + [ANY] * 9, cid=cid, limit=62 << 20)


def cross_forward(q2, image, lengths, patches, both, out_part, up_part, down_part, NDP, KV, cid):
    rows, (caps, tokens), ND = q2.shape[0], patches.shape, NDP * KV
    lows = out_part.shape[0]
    return call(
        functools.partial(cross_forward_kernel, NDP, KV), "cross_forward",
        [arr((rows, D), F32), arr((16, QUAD), F32), arr((caps * tokens, D)), arr((caps * tokens, D)),
         arr((caps * 3 * tokens, QUAD)), arr((4, 32, QUAD), F32), arr((4, rows, D)),
         arr((ND, lows, 2 * D)), arr((ND, lows, FF - D)), arr((ND,) + down_part.shape)],
        [q2, image, lengths, patches, both, out_part, up_part, down_part],
        [VM, VM, pl.BlockSpec(memory_space=pltpu.SMEM), VM, ANY, ANY, ANY, ANY],
        [pltpu.VMEM((2, D, D), BF), pltpu.VMEM((4, rows, D), BF), pltpu.VMEM((4, rows, D), BF),
         pltpu.VMEM((4, 32, QUAD), F32), pltpu.VMEM((-(-caps // 16) * 16, tokens), BF),
         pltpu.VMEM((lows, 2 * D), BF), pltpu.VMEM((lows, FF - D), BF), pltpu.VMEM(down_part.shape, BF),
         DMA((3,)), DMA((11,)), DMA((12,)), DMA((4,))] + Gather.sems(2, ND) + PlaneGather.sems(1, ND),
        4 * caps * tokens * D * D, out_specs=[VM] * 7 + [ANY] * 3, cid=cid)


BACK_TICKS = (4, 9)


def text_backward_kernel(dq2, dx3, text, x2, h1, h2, c1, q1, k1, v1, p1, gains, ng3, packed, tail,
                         text_grad, wq, wk, wv, wo, wcq, ngs, w, dq, dk, dv, rows_t, sem, between):
    slots = (2, 0, 1, 1, 0)
    weights = [load(packed.at[:, pl.ds(j * D, D)] if j < 4 else tail.at[:, pl.ds(0, D)], w.at[slots[j]], sem.at[j]) for j in range(5)]
    for j in (4, 3, 0):
        weights[j].start()
    unit, scaled = unit_of(x2[...])
    weights[4].wait()
    upstream = nt(dq2[...], w[0])
    weights[1].start()
    ngs_two = jnp.sum(upstream * unit, 0, keepdims=True)
    grad_two = dx3[...] + norm_backward(upstream, unit, scaled, gains[1:2])
    wcq[...] = tn(h2[...], dq2[...]).astype(BF)
    branch = grad_two.astype(BF)
    weights[3].wait()
    dc1 = nt(branch, w[1]).astype(BF)
    weights[2].start()
    wo[...] = tn(c1[...], branch).astype(BF)
    between(0)
    masks = head_masks(128)
    for pair in range(HEADS // 2):
        lanes = slice(pair * 128, (pair + 1) * 128)
        sums = [None] * 3
        for j, mask in enumerate(masks):
            low = p1[2 * pair + j]
            probs = low.astype(F32)
            above = dc1[:, lanes] * mask
            grad = nt(above, v1[:, lanes])
            grad = (probs * (grad - jnp.sum(probs * grad, -1, keepdims=True))).astype(BF)
            parts = [nn(grad, k1[:, lanes] * mask), tn(grad, q1[:, lanes] * mask), tn(low, above)]
            sums = parts if j == 0 else [a + b for a, b in zip(sums, parts)]
        dq[:, lanes] = (sums[0] * SCALE).astype(BF)
        dk[:, lanes] = (sums[1] * SCALE).astype(BF)
        dv[:, lanes] = sums[2].astype(BF)
    between(1)
    upstream = None
    flipped = h1[...].T
    for j, (ref, out) in enumerate(((dq, wq), (dk, wk), (dv, wv))):
        weights[j].wait()
        part = nt(ref[...], w[slots[j]])
        upstream = part if j == 0 else upstream + part
        out[...] = nn(flipped, ref[...]).astype(BF)
    unit, scaled = unit_of(text[...].astype(F32))
    text_grad[...] = grad_two + norm_backward(upstream, unit, scaled, gains[0:1])
    rows_t[...] = jnp.zeros_like(rows_t)
    rows_t[0:1] = jnp.sum(upstream * unit, 0, keepdims=True)
    rows_t[1:2] = ngs_two
    rows_t[2:3] = ng3[0:1]
    ngs[...] = rows_t[...].T.astype(BF)


def backward_kernel(NDP, KV, dc2, c2, lse, stats, qall, keys, vals, e, image,
                    dx3, text, x2, h1, h2, c1, q1, k1, v1, p1, gains, ng3, packed, tail, both, dco, dup, ddown,
                    wk, wv, igrad, sum_a, sum_b, sum_c, text_grad, wsq, wsk, wsv, wso, wcq, ngs,
                    dq2, dk, dv, w, ibuf, tw, dq, dk1, dv1, rows_t, tsem,
                    dall, sall, qbuf, rq, csem, wsem, isem, ssem, rsem, *more):
    at = place(NDP, KV)
    di, ki, x, c = at.di, at.ki, at.x, at.c
    held = [load(keys, dk, wsem.at[2]), load(vals, dv, wsem.at[3])]
    for copy in held:
        copy.start()
    weights = cross_weights(both, w, wsem)
    rows_all = dk.shape[0]
    caps = 4 * (dc2.shape[0] // SEQ)
    own_caps = caps // 4
    tokens = rows_all // caps
    core, over, diag = 2 * x + 1 - c, 2 * (1 - x) + c, 2 * (1 - x) + 1 - c
    masks = head_masks(QUAD)
    sall[ki, 0:16, :] = lse[...]

    def dots(local, _):
        queries = pl.ds(pl.multiple_of(local * SEQ, 16), SEQ)
        for g in range(3):
            lanes = slice(g * QUAD, (g + 1) * QUAD)
            product = dc2[queries, lanes].astype(F32) * c2[queries, lanes]
            product = jnp.concatenate([product * mask.astype(F32) for mask in masks], 0)
            sums = lax.dot_general(
                jnp.ones((8, QUAD), F32), product, (((1,), (1,)), ((), ())),
                preferred_element_type=F32, precision=lax.Precision.HIGHEST)
            sall[ki, pl.ds(16 + 3 * local + g, 1), :] = sums[0:1]
        return 0

    own_copy = load(dc2, dall.at[ki], csem)
    own_copy.start()
    enter(at, True)
    plane = PlaneScatter(at, [(dup, 0, D, 0, FF - D)], more[0:5], more[5:14], at.fixed)
    scatter = Scatter(at, [(dco, 0, 0, 0, D), (dup, 0, 0, D, D), (ddown, 1, 0, 0, D)], more[14:24], more[24:], at.split)
    to_over = remote(dc2, dall.at[ki], ssem.at[1], rsem.at[ki], (di, over))
    to_core = remote(dc2, dall.at[ki], ssem.at[0], rsem.at[ki], (di, core))
    to_over.start()
    to_core.start()
    plane.start()
    scatter.start()
    lax.fori_loop(0, own_caps, dots, 0)
    small = [remote(sall.at[ki], sall.at[ki], ssem.at[2 + j], rsem.at[4 + ki], (di, other))
             for j, other in enumerate((core, over, diag))]
    for copy in small:
        copy.start()
    own_copy.wait()
    for copy in held:
        copy.wait()
    plane.tick(0)
    scatter.tick(0)
    relay = remote(dall.at[over], dall.at[over], ssem.at[5], rsem.at[over], (di, core))

    def attend(i, _):
        step, local = i // own_caps, i % own_caps
        owner = 2 * ((x + step // 2) % 2) + (c + step % 2) % 2

        @pl.when(i == own_caps)
        def _():
            load(dall.at[core], dall.at[core], rsem.at[core]).wait()
            load(sall.at[core], sall.at[core], rsem.at[4 + core]).wait()

        @pl.when(i == 2 * own_caps - 1)
        def _():
            load(dall.at[over], dall.at[over], rsem.at[over]).wait()
            relay.start()

        @pl.when(i == 2 * own_caps)
        def _():
            load(sall.at[over], sall.at[over], rsem.at[4 + over]).wait()

        @pl.when(i == 3 * own_caps)
        def _():
            load(dall.at[diag], dall.at[diag], rsem.at[diag]).wait()
            load(sall.at[diag], sall.at[diag], rsem.at[4 + diag]).wait()

        for j, when in enumerate(BACK_TICKS):
            @pl.when(i == when * caps // 12)
            def _():
                plane.tick(1 + j)
                scatter.tick(1 + j)

        cap = owner * own_caps + local
        rows = pl.ds(pl.multiple_of(cap * tokens, 16), tokens)
        queries = pl.ds(pl.multiple_of(local * SEQ, 16), SEQ)
        for g in range(3):
            lanes = slice(g * QUAD, (g + 1) * QUAD)
            factor = jnp.exp(stats[owner, pl.ds(3 * local + g, 1), :] - sall[owner, pl.ds(3 * local + g, 1), :])
            dots_row = sall[owner, pl.ds(16 + 3 * local + g, 1), :]
            probs = e[pl.ds(pl.multiple_of((cap * 3 + g) * tokens, 16), tokens), :].astype(F32) * factor
            upstream = stacked(dall[owner, queries, lanes], masks)
            queried = stacked(qall[owner, queries, lanes], masks)
            grad = nt(dv[rows, lanes], upstream)
            grad = (probs * (grad - dots_row)).astype(BF)
            qbuf[owner, queries, lanes] = (own_blocks(tn(grad, dk[rows, lanes])) * SCALE).astype(BF)
            dv[rows, lanes] = nn(probs.astype(BF), upstream).astype(BF)
            dk[rows, lanes] = (nn(grad, queried) * SCALE).astype(BF)

        @pl.when(jnp.logical_and(local == own_caps - 1, owner != ki))
        def _():
            remote(qbuf.at[owner], rq.at[ki], ssem.at[6 + owner], rsem.at[8 + ki], (di, owner)).start()

        return 0

    lax.fori_loop(0, caps, attend, 0)

    def weight(j, _):
        cols = pl.ds(pl.multiple_of(j * 256, 256), 256)
        flipped = image[:, cols].T
        wk[cols, :] = nn(flipped, dk[...]).astype(BF)
        wv[cols, :] = nn(flipped, dv[...]).astype(BF)
        return 0

    lax.fori_loop(0, D // 256, weight, 0)
    ticks = 1 + len(BACK_TICKS)
    plane.tick(ticks)
    scatter.tick(ticks)
    for copy in weights:
        copy.wait()

    def flush(i):
        return load(ibuf.at[i % 2], igrad.at[pl.ds(pl.multiple_of(i * tokens, 16), tokens), :], isem.at[i % 2])

    def image_rows(i, _):
        @pl.when(i >= 2)
        def _():
            flush(i - 2).wait()

        rows = pl.ds(pl.multiple_of(i * tokens, 16), tokens)
        ibuf[i % 2] = (nt(dk[rows, :], w[0]) + nt(dv[rows, :], w[1])).astype(BF)
        flush(i).start()
        return 0

    lax.fori_loop(0, caps, image_rows, 0)
    rq[ki] = qbuf[ki]
    for other in (core, over, diag):
        load(rq.at[other], rq.at[other], rsem.at[8 + other]).wait()
    dq2[...] = (rq[0].astype(F32) + rq[1].astype(F32) + rq[2].astype(F32) + rq[3].astype(F32)).astype(BF)

    def between(n):
        if n == 0:
            plane.tick(ticks + 1)
            scatter.tick(ticks + 1)

    text_backward_kernel(dq2, dx3, text, x2, h1, h2, c1, q1, k1, v1, p1, gains, ng3, packed, tail,
                         text_grad, wsq, wsk, wsv, wso, wcq, ngs, tw, dq, dk1, dv1, rows_t, tsem, between)
    to_core.wait_send()
    to_over.wait_send()
    relay.wait_send()
    for copy in small:
        copy.wait_send()
    for other in (core, over, diag):
        load(qbuf.at[other], qbuf.at[other], ssem.at[6 + other]).wait()
    flush(caps - 2).wait()
    flush(caps - 1).wait()
    plane.finish(ticks + 2, [sum_c])
    scatter.finish(ticks + 2, [sum_a, sum_b])


def backward(dc2, c2, lse, stats, qall, keys, vals, e, image, dx3, text, x2, h1, h2, c1, q1, k1, v1, p1, gains, ng3,
             packed, tail, both, dco, dup, ddown, NDP, KV, cid):
    rows, ND = dc2.shape[0], NDP * KV
    caps = 4 * (rows // SEQ)
    dco, dup, ddown = blocks(dco, ND), blocks(dup, ND), blocks(ddown, ND)
    ins = [dc2, c2, lse, stats, qall, keys, vals, e, image, dx3, text, x2, h1, h2, c1, q1, k1, v1, p1, gains, ng3,
           packed, tail, both, dco, dup, ddown]
    low = dco.shape[1]
    shapes = [(low, 2 * D), ddown.shape[1:], (low, FF - D)]
    V = pltpu.VMEM
    return call(
        functools.partial(backward_kernel, NDP, KV), "backward",
        [arr((D, D)), arr((D, D)), arr(keys.shape)] + [arr(s, F32) for s in shapes]
        + [arr((rows, D), F32)] + [arr((D, D))] * 5 + [arr((D, 128))],
        ins, [VM] * 5 + [ANY] * 2 + [VM] * 14 + [ANY] * 6,
        [V((rows, D), BF), V(keys.shape, BF), V(keys.shape, BF), V((2, D, D), BF), V((2, keys.shape[0] // caps, D), BF),
         V((3, D, D), BF), V((rows, D), BF), V((rows, D), BF), V((rows, D), BF), V((128, D), F32), DMA((5,)),
         V((4, rows, D), BF), V((4, 32, QUAD), F32), V((4, rows, D), BF), V((4, rows, D), BF),
         DMA, DMA((4,)), DMA((2,)), DMA((10,)), DMA((12,))]
        + PlaneScatter.bufs(shapes[2:], ND) + PlaneScatter.sems(1, ND) + Scatter.bufs(shapes[:2], ND) + Scatter.sems(2, ND),
        4 * keys.shape[0] * D * D, out_specs=[VM] * 2 + [ANY] + [VM] * 10, cid=cid, limit=65470 << 10)


def mlp_kernel(c2, x2, grad, gains, packed, wide, down, out, dx3, dc2, dup, ddown, dco, ng, wu, wd, wc, dh, acc, ht, sem):
    wcopy = load(packed.at[:, pl.ds(0, D)], wc, sem.at[8])
    wcopy.start()
    ups = [load(packed.at[:, pl.ds(D, D)] if j == 0 else wide.at[:, pl.ds((j - 1) * D, D)], wu.at[j], sem.at[j]) for j in range(4)]
    downs = [load(down.at[pl.ds(j * D, D), :], wd.at[j], sem.at[4 + j]) for j in range(4)]
    for j in range(4):
        ups[j].start()
        downs[j].start()
    low = c2[...].astype(BF)
    wcopy.wait()
    third = x2[...] + nn(low, wc[...])
    unit, scaled = unit_of(third)
    gain = gains[2:3]
    h3 = (unit * gain).astype(BF)
    ht[...] = h3.T
    g = grad[...]
    acc[...] = third
    for j in range(4):
        ups[j].wait()
        downs[j].wait()
        u = nn(h3, wu[j])
        square = u * u
        tanh_part = jnp.tanh(GELU_C * (u + GELU_A * square * u))
        active = (0.5 * u * (1.0 + tanh_part)).astype(BF)
        slope = 0.5 * (1.0 + tanh_part) + 0.5 * u * (1.0 - tanh_part * tanh_part) * GELU_C * (1.0 + 3.0 * GELU_A * square)
        acc[...] += nn(active, wd[j])
        du = (nt(g, wd[j]) * slope).astype(BF)
        part = nt(du, wu[j])
        dh[...] = part if j == 0 else dh[...] + part
        ddown[pl.ds(j * D, D), :] = tn(active, g).astype(BF)
        dup[:, pl.ds(j * D, D)] = nn(ht[...], du).astype(BF)
    out[...] = acc[...].astype(BF)
    upstream = dh[...]
    ng[...] = jnp.broadcast_to(jnp.sum(upstream * unit, 0, keepdims=True), ng.shape)
    total = g.astype(F32) + norm_backward(upstream, unit, scaled, gain)
    dx3[...] = total
    branch = total.astype(BF)
    dc2[...] = nt(branch, wc[...]).astype(BF)
    dco[...] = tn(low, branch).astype(BF)


def mlp(c2, x2, grad, gains, packed, wide, down):
    rows = c2.shape[0]
    return call(
        mlp_kernel, "feed_forward",
        [arr((rows, D)), arr((rows, D), F32), arr((rows, D)), arr((D, FF)), arr((FF, D)), arr((D, D)), arr((8, D), F32)],
        [c2, x2, grad, gains, packed, wide, down], [VM] * 4 + [ANY] * 3,
        [pltpu.VMEM((4, D, D), BF), pltpu.VMEM((4, D, D), BF), pltpu.VMEM((D, D), BF), pltpu.VMEM((rows, D), F32),
         pltpu.VMEM((rows, D), F32), pltpu.VMEM((D, rows), BF), DMA((9,))], 12 * rows * D * FF)


def deliver_kernel(widths, moves, gain, *refs):
    count = len(widths) + 3
    sources, outs = refs[: -count - 4], refs[-count - 4 : -4]
    narrow, moved, sem, msem = refs[-4:]
    *sources, text_grad, igrad = sources
    *outs, norms, text_out, image_out = outs
    size = igrad.shape[0] // 6
    pieces = [pl.ds(j * size, size) for j in range(6)]
    inward = [load(igrad.at[rows, :], narrow.at[rows, :], msem.at[j]) for j, rows in enumerate(pieces)]
    outward = [load(moved.at[rows, :], image_out.at[rows, :], msem.at[j]) for j, rows in enumerate(pieces)]
    copies = [load(text_grad, text_out, msem.at[6])]
    for (i, offset, width, j, to) in moves:
        copies.append(load(sources[i].at[:, pl.ds(offset, width)], outs[j].at[:, pl.ds(to, width)], sem.at[len(copies) - 1]))
    for copy in inward + copies:
        copy.start()
    i, offset = gain
    block = sources[i][:, offset : offset + 128]
    block = jnp.concatenate([block, jnp.zeros((128 - block.shape[0], 128), F32)], 0)
    norms[...] = block.T[:8]
    for there, back, rows in zip(inward, outward, pieces):
        there.wait()
        moved[rows, :] = narrow[rows, :].astype(F32)
        back.start()
    for copy in copies + outward:
        copy.wait()


def deliver(sources, text_grad, igrad, widths, moves, gain):
    outs = [arr((rows, width), F32) for rows, width in widths]
    return call(
        functools.partial(deliver_kernel, widths, moves, gain), "deliver_gradients",
        outs + [arr((8, 128), F32), arr(text_grad.shape, F32), arr(igrad.shape, F32)], [*sources, text_grad, igrad],
        [VM] * (len(sources) + 1) + [ANY],
        [pltpu.VMEM(igrad.shape, BF), pltpu.VMEM(igrad.shape, F32), DMA((len(moves),)), DMA((7,))], 1,
        out_specs=[ANY] * len(outs) + [VM, ANY, ANY], limit=60 << 20)


def apart(text, image, lengths, patches, firsts, crosses, out_part, up_part, down_part, ndp, nkv):
    packed, tail = (a.reshape(D, -1) for a in all_gather(firsts[:4] + crosses + firsts[4:], ndp, nkv, 1))
    packed, both = packed[:, : 4 * D], packed[:, 4 * D :]
    h1, q1, k1, v1, p1, c1, x2, h2, q2, gains = text_forward(text, packed, tail)
    c2, lse, keys, vals, e, stats, qall, second, third, down = cross_forward(
        q2, image, lengths, patches, both, out_part, up_part, down_part, ndp, nkv, 2)
    second, third, down = second.reshape(D, -1), third.reshape(D, -1), down.reshape(FF, D)
    return h1, q1, k1, v1, p1, c1, x2, h2, gains, c2, lse, stats, qall, keys, vals, e, packed, tail, both, second, third, down


def per_device(
    text_tokens, image_tokens, image_lengths, patch_mask, self_query, self_key, self_value, self_out, cross_query,
    cross_key, cross_value, cross_out, mlp_up, mlp_down, norm_self, norm_cross, norm_mlp, out_grad,
):
    ndp, nkv = lax.axis_size("dp"), lax.axis_size("kv")
    caps, tokens = image_tokens.shape[0], image_tokens.shape[1]
    gain_block = jnp.pad(jnp.stack([norm_self, norm_cross, norm_mlp], 1), ((0, 0), (0, 125)))
    parts = [self_query, self_key, self_value, self_out, cross_query, gain_block]
    crosses = [cross_key, cross_value]
    image = image_tokens.reshape(caps * tokens, D)
    if self_query.shape[0] % 8 == 0:
        (h1, q1, k1, v1, p1, c1, x2, h2, gains, c2, lse, stats, qall, keys, vals, e, packed, tail, both, second, third, down) = forward(
            text_tokens, image, image_lengths, patch_mask, parts, crosses, cross_out, mlp_up, mlp_down, ndp, nkv, 1)
    else:
        (h1, q1, k1, v1, p1, c1, x2, h2, gains, c2, lse, stats, qall, keys, vals, e, packed, tail, both, second, third, down) = apart(
            text_tokens, image, image_lengths, patch_mask, parts, crosses, cross_out, mlp_up, mlp_down, ndp, nkv)
    layer_out, dx3, dc2, d_up, d_down, d_co, ng3 = mlp(c2, x2, out_grad, gains, second, third, down)
    d_ck, d_cv, igrad, sum_a, sum_b, sum_c, text_grad, d_q, d_k, d_v, d_o, d_cq, ngs = backward(
        dc2, c2, lse, stats, qall, keys, vals, e, image, dx3, text_tokens, x2, h1, h2, c1, q1, k1, v1, p1, gains, ng3,
        packed, tail, both, d_co, d_up, d_down, ndp, nkv, 3)
    sum_d, sum_e = reduce_scatter([d_q, d_k, d_v, d_o, d_cq, d_ck, d_cv, ngs], ndp, nkv, 4)
    rows = norm_self.shape[0]
    moves = [(3, j * D, D, j, 0) for j in range(6)] + [(4, 0, D, 6, 0), (0, 0, D, 7, 0), (0, D, D, 8, 0), (2, 0, FF - D, 8, D), (1, 0, D, 9, 0)]
    *parts, norms, text_grad, image_grad = deliver(
        [sum_a, sum_b, sum_c, sum_d, sum_e], text_grad, igrad, [(rows, D)] * 8 + [(rows, FF), mlp_down.shape], moves, (4, D))
    return (layer_out, text_grad, image_grad.reshape(caps, tokens, D), *parts, norms[0, :rows], norms[1, :rows], norms[2, :rows])


def solution(mesh):
    in_specs = (
        P(("dp", "kv"), None),
        P("dp", "kv", None),
        P("dp"),
        P("dp", "kv"),
        P(("dp", "kv"), None),
        P(("dp", "kv"), None),
        P(("dp", "kv"), None),
        P(("dp", "kv"), None),
        P(("dp", "kv"), None),
        P(("dp", "kv"), None),
        P(("dp", "kv"), None),
        P(("dp", "kv"), None),
        P(("dp", "kv"), None),
        P(("dp", "kv"), None),
        P(("dp", "kv")),
        P(("dp", "kv")),
        P(("dp", "kv")),
        P(("dp", "kv"), None),
    )
    out_specs = (
        P(("dp", "kv"), None),
        P(("dp", "kv"), None),
        P("dp", "kv", None),
        P(("dp", "kv"), None),
        P(("dp", "kv"), None),
        P(("dp", "kv"), None),
        P(("dp", "kv"), None),
        P(("dp", "kv"), None),
        P(("dp", "kv"), None),
        P(("dp", "kv"), None),
        P(("dp", "kv"), None),
        P(("dp", "kv"), None),
        P(("dp", "kv"), None),
        P(("dp", "kv")),
        P(("dp", "kv")),
        P(("dp", "kv")),
    )
    return jax.shard_map(
        per_device, mesh=mesh, in_specs=in_specs, out_specs=out_specs, check_vma=False
    )
```

```python
import functools
import types

import jax
import jax.numpy as jnp
from jax import lax
from jax.experimental import pallas as pl
from jax.experimental.pallas import tpu as pltpu
from jax.sharding import PartitionSpec as P

MESH = pl.DeviceIdType.MESH
def place(NDP, KV):
    di, ki = lax.axis_index("dp"), lax.axis_index("kv")
    Y = 2
    z, y, x, c = di // Y, di % Y, ki // 2, ki % 2
    y2, x2 = y + c*(1-2*y), x + (1-c)*(1-2*x)
    y3, x3 = y + (1-c)*(1-2*y), x + c*(1-2*x)
    return types.SimpleNamespace(
        di=di, ki=ki, z=z, y=y, x=x, c=c, Y=Y, Z=NDP//Y, KV=KV,
        split=((y2, x2), (y3, x3)), fixed=((y, 1-x), (1-y, x)), up=(di + Y, ki), dn=(di - Y, ki),
        px=(di, 2*(1-x) + c), py=(z*Y+1-y, ki), pd=(di, ki + 1 - 2*c), diag=(di, 2*(1-x) + 1 - c))

def enter(at, group=False):
    bar = pltpu.get_barrier_semaphore()
    @pl.when(at.z < at.Z-1)
    def _(): pl.semaphore_signal(bar, 1, device_id=at.up, device_id_type=MESH)
    @pl.when(at.z > 0)
    def _(): pl.semaphore_signal(bar, 1, device_id=at.dn, device_id_type=MESH)
    peers = (at.px, at.py, at.pd) + ((at.diag,) if group else ())
    for p in peers: pl.semaphore_signal(bar, 1, device_id=p, device_id_type=MESH)
    pl.semaphore_wait(bar, len(peers) + jnp.where(at.z < at.Z-1, 1, 0) + jnp.where(at.z > 0, 1, 0))

class Gather:
    def __init__(self, at, ins, outs, sems, route):
        self.at, self.ins, self.outs = at, ins, outs
        self.recv, self.sz, self.s2, self.s3, self.sd, self.sl = sems
        self.n = len(ins)
        self.own = self.slot(at.z, at.y, at.x)
        (self.y2, self.x2), (self.y3, self.x3) = route
        self.p2, self.p3 = ((at.z*at.Y+yy, 2*xx+at.c) for yy, xx in route)

    @staticmethod
    def sems(n, ND):
        Z = ND // 8
        D = pltpu.SemaphoreType.DMA
        return [D((n, ND)), D((n, 2, Z)), D((n, Z)), D((n, 2*Z)), D((n, ND//2)), D((n,))]

    def at_slot(self, i, s):
        out, rows = self.outs[i], self.ins[i].shape[0]
        if len(out.shape) == 3: return out.at[s]
        return out.at[pl.ds(pl.multiple_of(s * rows, 8), rows), :]

    def slot(self, zz, yy, xx):
        return (zz*self.at.Y+yy)*self.at.KV + xx*2 + self.at.c

    def send(self, s, sems, dev, own=False):
        for i in range(self.n):
            pltpu.make_async_remote_copy(
                src_ref=self.ins[i] if own else self.at_slot(i, s), dst_ref=self.at_slot(i, s), send_sem=sems(i),
                recv_sem=self.recv.at[i, s], device_id=dev, device_id_type=MESH).start()

    def arrive(self, s):
        for i in range(self.n):
            pltpu.make_async_copy(self.at_slot(i, s), self.at_slot(i, s), self.recv.at[i, s]).wait()

    def spread(self, zz, own=False):
        s = self.slot(zz, self.at.y, self.at.x)
        self.send(s, lambda i: self.s2.at[i, zz], self.p2, own)
        self.send(s, lambda i: self.s3.at[i, zz], self.p3, own)
        self.send(s, lambda i: self.sd.at[i, s//2], self.at.pd, own)

    def start(self):
        at, own = self.at, self.own
        @pl.when(at.z < at.Z-1)
        def _(): self.send(own, lambda i: self.sz.at[i, 0, at.z], at.up, True)
        @pl.when(at.z > 0)
        def _(): self.send(own, lambda i: self.sz.at[i, 1, at.z], at.dn, True)
        self.spread(at.z, True)
        for i in range(self.n):
            pltpu.make_async_copy(self.ins[i], self.at_slot(i, own), self.sl.at[i]).start()

    def second(self, zz):
        at = self.at
        s = self.slot(zz, self.y2, self.x2)
        self.arrive(s)
        self.send(s, lambda i: self.s3.at[i, at.Z+zz], self.p3)
        self.send(s, lambda i: self.sd.at[i, s//2], at.pd)

    def near(self, t):
        at = self.at
        @pl.when(at.z >= t)
        def _():
            s = self.slot(at.z-t, at.y, at.x); self.arrive(s)
            @pl.when(at.z < at.Z-1)
            def _(): self.send(s, lambda i: self.sz.at[i, 0, at.z-t], at.up)
            self.spread(at.z-t)
        @pl.when(at.z + t < at.Z)
        def _():
            s = self.slot(at.z+t, at.y, at.x); self.arrive(s)
            @pl.when(at.z > 0)
            def _(): self.send(s, lambda i: self.sz.at[i, 1, at.z+t], at.dn)
            self.spread(at.z+t)
        @pl.when(at.z >= t-1)
        def _(): self.second(at.z-t+1)
        @pl.when(jnp.logical_and(t > 1, at.z+t-1 < at.Z))
        def _(): self.second(at.z+t-1)

    def third(self, zz):
        at = self.at
        for yy, xx in ((self.y3, self.x3), (1-at.y, 1-at.x)):
            s = self.slot(zz, yy, xx)
            self.arrive(s)
            self.send(s, lambda i: self.sd.at[i, s//2], at.pd)

    def far(self, t):
        at = self.at
        @pl.when(at.z >= t)
        def _(): self.third(at.z-t)
        @pl.when(jnp.logical_and(t > 0, at.z+t < at.Z))
        def _(): self.third(at.z+t)

    def tick(self, k):
        if k < self.at.Z: self.near(jnp.int32(k+1))
        elif k < 2*self.at.Z: self.far(jnp.int32(k-self.at.Z))

    def finish(self, k=0):
        at, Z, n = self.at, self.at.Z, self.n
        lax.fori_loop(min(k, Z)+1, Z+1, lambda t, _: (self.near(t), 0)[1], 0)
        lax.fori_loop(max(k-Z, 0), Z, lambda t, _: (self.far(t), 0)[1], 0)
        def fin(h, _):
            self.arrive(2*h + 1 - at.c)
            for i in range(n):
                o = self.at_slot(i, 0)
                pltpu.make_async_copy(o, o, self.sd.at[i, h]).wait()
            return 0
        lax.fori_loop(0, at.KV*Z, fin, 0)
        def finz(zz, _):
            for i in range(n):
                o = self.at_slot(i, 0)
                pltpu.make_async_copy(o, o, self.s2.at[i, zz]).wait()
                pltpu.make_async_copy(o, o, self.s3.at[i, zz]).wait()
                pltpu.make_async_copy(o, o, self.s3.at[i, Z+zz]).wait()
                @pl.when(jnp.logical_and(at.z < Z-1, zz <= at.z))
                def _(): pltpu.make_async_copy(o, o, self.sz.at[i, 0, zz]).wait()
                @pl.when(jnp.logical_and(at.z > 0, zz >= at.z))
                def _(): pltpu.make_async_copy(o, o, self.sz.at[i, 1, zz]).wait()
            return 0
        lax.fori_loop(0, Z, finz, 0)
        for i in range(n):
            pltpu.make_async_copy(self.ins[i], self.at_slot(i, self.own), self.sl.at[i]).wait()

class PlaneGather(Gather):
    @staticmethod
    def sems(n, ND):
        D = pltpu.SemaphoreType.DMA
        return [D((n, ND)), D((n, 2, ND)), D((n, 1)), D((n, 2)), D((n, ND//2)), D((n,))]

    def onward(self, s, up, down, own=False):
        at = self.at
        if up:
            @pl.when(at.z < at.Z-1)
            def _(): self.send(s, lambda i: self.sz.at[i, 0, s], at.up, own)
        if down:
            @pl.when(at.z > 0)
            def _(): self.send(s, lambda i: self.sz.at[i, 1, s], at.dn, own)
        self.send(s, lambda i: self.sd.at[i, s//2], at.pd, own)

    def start(self):
        own = self.own
        self.send(own, lambda i: self.s2.at[i, 0], self.p2, True)
        self.send(own, lambda i: self.s3.at[i, 0], self.p3, True)
        self.onward(own, True, True, True)
        for i in range(self.n):
            pltpu.make_async_copy(self.ins[i], self.at_slot(i, own), self.sl.at[i]).start()

    def lines(self):
        at = self.at
        return ((at.y, at.x), (self.y2, self.x2), (self.y3, self.x3), (1-at.y, 1-at.x))

    def plane(self):
        at = self.at
        for j, (yy, xx) in enumerate(self.lines()[1:]):
            s = self.slot(at.z, yy, xx)
            self.arrive(s)
            if j == 0: self.send(s, lambda i: self.s3.at[i, 1], self.p3)
            self.onward(s, True, True)

    def level(self, t):
        at = self.at
        @pl.when(at.z >= t)
        def _():
            for yy, xx in self.lines():
                s = self.slot(at.z-t, yy, xx)
                self.arrive(s)
                self.onward(s, True, False)
        @pl.when(at.z + t < at.Z)
        def _():
            for yy, xx in self.lines():
                s = self.slot(at.z+t, yy, xx)
                self.arrive(s)
                self.onward(s, False, True)

    def tick(self, k):
        if k == 0: self.plane()
        elif k < self.at.Z: self.level(jnp.int32(k))

    def finish(self, k=0):
        at, Z, n = self.at, self.at.Z, self.n
        if k == 0: self.plane()
        lax.fori_loop(max(k, 1), Z, lambda t, _: (self.level(t), 0)[1], 0)
        def wait(i, sem):
            o = self.at_slot(i, 0)
            pltpu.make_async_copy(o, o, sem).wait()
        def fin(h, _):
            self.arrive(2*h + 1 - at.c)
            s = 2*h + at.c
            level = s // (at.Y * at.KV)
            for i in range(n):
                wait(i, self.sd.at[i, h])
                @pl.when(jnp.logical_and(at.z < Z-1, level <= at.z))
                def _(): wait(i, self.sz.at[i, 0, s])
                @pl.when(jnp.logical_and(at.z > 0, level >= at.z))
                def _(): wait(i, self.sz.at[i, 1, s])
            return 0
        lax.fori_loop(0, at.KV*Z, fin, 0)
        for i in range(n):
            for sem in (self.s2.at[i, 0], self.s3.at[i, 0], self.s3.at[i, 1]): wait(i, sem)
            pltpu.make_async_copy(self.ins[i], self.at_slot(i, self.own), self.sl.at[i]).wait()

def fill_block(parts, block, sem):
    copies, offset = [], 0
    for j, part in enumerate(parts):
        copies.append(pltpu.make_async_copy(part, block.at[:, pl.ds(offset, part.shape[1])], sem.at[j]))
        offset += part.shape[1]
    for copy in copies: copy.start()
    return copies

def ag_kernel(NDP, KV, count, *refs):
    parts, outs, packs, fill = refs[:count], refs[count:count+2], refs[count+2:count+4], refs[count+4]
    copies = fill_block(parts[:-2], packs[0], fill)
    copies += fill_block(parts[-2:], packs[1], fill.at[pl.ds(count-2, 2)])
    at = place(NDP, KV)
    enter(at)
    for copy in copies: copy.wait()
    k = count+5
    plane = PlaneGather(at, [packs[1]], [outs[1]], refs[k+6:], at.split)
    gather = Gather(at, [packs[0]], [outs[0]], refs[k:k+6], at.split)
    plane.start()
    gather.start()
    plane.tick(0)
    for k in range(1, min(at.Z, 4)):
        gather.tick(k-1)
        plane.tick(k)
    gather.finish(min(at.Z, 4)-1)
    plane.finish(min(at.Z, 4))

def all_gather(parts, NDP, KV, cid):
    ND = NDP*KV
    rows = parts[0].shape[0]
    widths = [sum(p.shape[1] for p in some) for some in (parts[:-2], parts[-2:])]
    return pl.pallas_call(
        functools.partial(ag_kernel, NDP, KV, len(parts)),
        out_shape=[jax.ShapeDtypeStruct((ND, rows, width), jnp.bfloat16) for width in widths],
        in_specs=[pl.BlockSpec(memory_space=pl.ANY)]*len(parts),
        out_specs=[pl.BlockSpec(memory_space=pl.ANY)]*2,
        scratch_shapes=[pltpu.VMEM((rows, width), jnp.bfloat16) for width in widths] + [pltpu.SemaphoreType.DMA((len(parts),))]
            + Gather.sems(1, ND) + PlaneGather.sems(1, ND),
        compiler_params=pltpu.CompilerParams(collective_id=cid, has_side_effects=True, vmem_limit_bytes=60<<20),
        name="gather_weights",
    )(*parts)


class Scatter:
    count = 9

    def __init__(self, at, sources, bufs, sems, route):
        self.at, self.sources = at, sources
        self.n = n = len(bufs) // 5
        self.loc, self.r1, self.r2, self.r3, self.rz = (bufs[j*n:(j+1)*n] for j in range(5))
        self.sl, self.sd, self.qd, self.s2, self.q2, self.s3, self.q3, self.sz, self.qz = sems
        (self.y2, self.x2), (self.y3, self.x3) = route
        self.p2, self.p3 = ((at.z*at.Y+yy, 2*xx+at.c) for yy, xx in route)
        self.lines = ((at.y, at.x), (self.y2, self.x2), (self.y3, self.x3), (1-at.y, 1-at.x))

    @staticmethod
    def bufs(shapes, ND):
        Z = ND // 8
        return [pltpu.VMEM(lead + tuple(s), jnp.bfloat16)
                for lead in ((ND//2,), (ND//2,), (2*Z,), (Z,), (2, Z)) for s in shapes]

    @staticmethod
    def sems(n, ND):
        Z = ND // 8
        D = pltpu.SemaphoreType.DMA
        return [D((n, ND//2))]*3 + [D((n, 2*Z))]*2 + [D((n, Z))]*2 + [D((n, 2, Z))]*2

    def half(self, zz, yy, xx): return (zz*self.at.Y+yy)*(self.at.KV//2) + xx

    def send(self, src, dst, ss, rsem, dev):
        pltpu.make_async_remote_copy(
            src_ref=src, dst_ref=dst, send_sem=ss, recv_sem=rsem, device_id=dev, device_id_type=MESH).start()

    def wait(self, ref, sem): pltpu.make_async_copy(ref, ref, sem).wait()

    def both(self, t, f):
        at = self.at
        @pl.when(at.z >= t)
        def _(): f(at.z-t)
        @pl.when(jnp.logical_and(t > 0, at.z+t < at.Z))
        def _(): f(at.z+t)

    def every(self, f):
        Z = self.at.Z
        lax.fori_loop(0, Z, lambda k, _: (self.both(Z-1-k, f), 0)[1], 0)

    def start(self):
        c = self.at.c
        def one(zz):
            for yy, xx in self.lines[::-1]:
                h = self.half(zz, yy, xx)
                for ref, i, off, dst, width in self.sources:
                    to, cols = pl.ds(dst, width), pl.ds(off, width)
                    self.send(ref.at[2*h+1-c, :, cols], self.r1[i].at[h, :, to], self.sd.at[i, h], self.qd.at[i, h], self.at.pd)
                    pltpu.make_async_copy(ref.at[2*h+c, :, cols], self.loc[i].at[h, :, to], self.sl.at[i, h]).start()
        self.every(one)

    def pair(self, h):
        for i in range(self.n):
            self.wait(self.loc[i].at[h], self.sl.at[i, h]); self.wait(self.r1[i].at[h], self.qd.at[i, h])
            self.loc[i][h] = self.loc[i][h] + self.r1[i][h]

    def first(self):
        def one(zz):
            for j, (yy, xx) in enumerate((self.lines[3], self.lines[2])):
                h = self.half(zz, yy, xx)
                self.pair(h)
                for i in range(self.n):
                    self.send(self.loc[i].at[h], self.r2[i].at[2*zz+j], self.s2.at[i, 2*zz+j], self.q2.at[i, 2*zz+j], self.p3)
            for yy, xx in self.lines[:2]: self.pair(self.half(zz, yy, xx))
        self.every(one)

    def second(self, t):
        at, Z = self.at, self.at.Z
        def one(zz):
            for j, (yy, xx) in enumerate((self.lines[1], self.lines[0])):
                h = self.half(zz, yy, xx)
                for i in range(self.n):
                    self.wait(self.r2[i].at[2*zz+j], self.q2.at[i, 2*zz+j])
                    self.loc[i][h] = self.loc[i][h] + self.r2[i][2*zz+j]
                    if j == 0:
                        self.send(self.loc[i].at[h], self.r3[i].at[zz], self.s3.at[i, zz], self.q3.at[i, zz], self.p2)
        self.both(t, one)
        def along(zz, d, dev, has):
            h = self.half(zz, at.y, at.x)
            for i in range(self.n):
                loc, rz = self.loc[i], self.rz[i]
                self.wait(self.r3[i].at[zz], self.q3.at[i, zz])
                @pl.when(has)
                def _():
                    self.wait(rz.at[d, zz], self.qz.at[i, d, zz])
                    loc[h] = loc[h] + self.r3[i][zz] + rz[d, zz]
                @pl.when(jnp.logical_not(has))
                def _(): loc[h] = loc[h] + self.r3[i][zz]
                self.send(loc.at[h], rz.at[d, zz], self.sz.at[i, d, zz], self.qz.at[i, d, zz], dev)
        u = t + 1
        @pl.when(at.z + u < Z)
        def _(): along(at.z+u, 0, at.up, at.z > 0)
        @pl.when(at.z >= u)
        def _(): along(at.z-u, 1, at.dn, at.z < Z-1)

    def tick(self, k):
        if k == 0: self.first()
        elif k <= self.at.Z: self.second(jnp.int32(self.at.Z-k))

    def rest(self, k):
        Z = self.at.Z
        if k == 0: self.first()
        lax.fori_loop(max(k, 1), Z+1, lambda j, _: (self.second(Z-j), 0)[1], 0)

    def finish(self, k, outs):
        at, Z, z = self.at, self.at.Z, self.at.z
        self.rest(k)
        h = self.half(z, at.y, at.x)
        for i, out in enumerate(outs):
            self.wait(self.r3[i].at[z], self.q3.at[i, z])
            out[...] = self.loc[i][h].astype(jnp.float32) + self.r3[i][z].astype(jnp.float32)
            for d, has in ((0, z > 0), (1, z < Z-1)):
                @pl.when(has)
                def _():
                    self.wait(self.rz[i].at[d, z], self.qz.at[i, d, z])
                    out[...] += self.rz[i][d, z].astype(jnp.float32)
        def fin(h, _):
            for i in range(self.n): self.wait(self.r1[i].at[h], self.sd.at[i, h])
            return 0
        lax.fori_loop(0, at.KV*Z, fin, 0)
        def fin2(zz, _):
            for i in range(self.n):
                self.wait(self.r3[i].at[zz], self.s3.at[i, zz])
                for j in range(2): self.wait(self.r2[i].at[2*zz+j], self.s2.at[i, 2*zz+j])
                @pl.when(zz > z)
                def _(): self.wait(self.rz[i].at[0, zz], self.sz.at[i, 0, zz])
                @pl.when(zz < z)
                def _(): self.wait(self.rz[i].at[1, zz], self.sz.at[i, 1, zz])
            return 0
        lax.fori_loop(0, Z, fin2, 0)

class PlaneScatter(Scatter):
    @staticmethod
    def bufs(shapes, ND):
        Z = ND // 8
        return [pltpu.VMEM(lead + tuple(s), jnp.bfloat16)
                for lead in ((ND//2,), (ND//2,), (2,), (1,), (2, 4*Z)) for s in shapes]

    @staticmethod
    def sems(n, ND):
        Z = ND // 8
        D = pltpu.SemaphoreType.DMA
        return [D((n, ND//2))]*3 + [D((n, 2))]*2 + [D((n, 1))]*2 + [D((n, 2, 4*Z))]*2

    def chain(self, t):
        at, Z = self.at, self.at.Z
        def along(zz, d, dev, has):
            for l, (yy, xx) in enumerate(self.lines):
                h = self.half(zz, yy, xx)
                k = 4*zz + l
                self.pair(h)
                for i in range(self.n):
                    loc, rz = self.loc[i], self.rz[i]
                    @pl.when(has)
                    def _():
                        self.wait(rz.at[d, k], self.qz.at[i, d, k])
                        loc[h] = loc[h] + rz[d, k]
                    self.send(loc.at[h], rz.at[d, k], self.sz.at[i, d, k], self.qz.at[i, d, k], dev)
        @pl.when(at.z + t < Z)
        def _(): along(at.z+t, 0, at.up, at.z > 0)
        @pl.when(at.z >= t)
        def _(): along(at.z-t, 1, at.dn, at.z < Z-1)

    def level(self):
        at, z = self.at, self.at.z
        for l, (yy, xx) in reversed(list(enumerate(self.lines))):
            h = self.half(z, yy, xx)
            k = 4*z + l
            self.pair(h)
            for i in range(self.n):
                loc, rz = self.loc[i], self.rz[i]
                for d, has in ((0, z > 0), (1, z < at.Z-1)):
                    @pl.when(has)
                    def _():
                        self.wait(rz.at[d, k], self.qz.at[i, d, k])
                        loc[h] = loc[h] + rz[d, k]
                if l >= 2:
                    self.send(loc.at[h], self.r2[i].at[3-l], self.s2.at[i, 3-l], self.q2.at[i, 3-l], self.p3)

    def plane(self):
        for j, (yy, xx) in enumerate((self.lines[1], self.lines[0])):
            h = self.half(self.at.z, yy, xx)
            for i in range(self.n):
                self.wait(self.r2[i].at[j], self.q2.at[i, j])
                self.loc[i][h] = self.loc[i][h] + self.r2[i][j]
                if j == 0: self.send(self.loc[i].at[h], self.r3[i].at[0], self.s3.at[i, 0], self.q3.at[i, 0], self.p2)

    def tick(self, k):
        Z = self.at.Z
        if k < Z-1: self.chain(jnp.int32(Z-1-k))
        elif k == Z-1: self.level()
        elif k == Z: self.plane()

    def finish(self, k, outs):
        at, Z, z = self.at, self.at.Z, self.at.z
        lax.fori_loop(min(k, Z-1), Z-1, lambda j, _: (self.chain(Z-1-j), 0)[1], 0)
        if k <= Z-1: self.level()
        if k <= Z: self.plane()
        h = self.half(z, at.y, at.x)
        for i, out in enumerate(outs):
            self.wait(self.r3[i].at[0], self.q3.at[i, 0])
            out[...] = self.loc[i][h].astype(jnp.float32) + self.r3[i][0].astype(jnp.float32)
        def fin(h, _):
            zz = h // (at.Y * at.KV // 2)
            for i in range(self.n):
                self.wait(self.r1[i].at[h], self.sd.at[i, h])
                for d, cond in ((0, zz > z), (1, zz < z)):
                    @pl.when(cond)
                    def _(): self.wait(self.rz[i].at[d, h], self.sz.at[i, d, h])
            return 0
        lax.fori_loop(0, at.KV*Z, fin, 0)
        for i in range(self.n):
            self.wait(self.r3[i].at[0], self.s3.at[i, 0])
            for j in range(2): self.wait(self.r2[i].at[j], self.s2.at[i, j])

def rs_kernel(NDP, KV, count, *refs):
    parts, outs, k = refs[:count], refs[count:count+2], count+2
    at = place(NDP, KV)
    enter(at)
    def sources(some):
        found, offset = [], 0
        for ref in some:
            found.append((ref, 0, 0, offset, ref.shape[2]))
            offset += ref.shape[2]
        return found
    plane = PlaneScatter(at, sources(parts[-2:]), refs[k:k+5], refs[k+5:k+14], at.split)
    scatter = Scatter(at, sources(parts[:-2]), refs[k+14:k+19], refs[k+19:], at.split)
    plane.start()
    scatter.start()
    last = min(at.Z, 4)
    for j in range(last):
        plane.tick(j)
        scatter.tick(j)
    plane.finish(last, outs[1:])
    scatter.finish(last, outs[:1])

def blocks(g, ND): return g.reshape(ND, g.shape[0]//ND, g.shape[1])

def reduce_scatter(grads, NDP, KV, cid):
    ND = NDP*KV
    parts = [blocks(g, ND) for g in grads]
    rows = parts[0].shape[1]
    shapes = [(rows, sum(g.shape[2] for g in some)) for some in (parts[:-2], parts[-2:])]
    return pl.pallas_call(
        functools.partial(rs_kernel, NDP, KV, len(parts)),
        out_shape=[jax.ShapeDtypeStruct(s, jnp.float32) for s in shapes],
        in_specs=[pl.BlockSpec(memory_space=pl.ANY)]*len(parts),
        out_specs=[pl.BlockSpec(memory_space=pltpu.VMEM)]*2,
        scratch_shapes=PlaneScatter.bufs(shapes[1:], ND) + PlaneScatter.sems(1, ND) + Scatter.bufs(shapes[:1], ND) + Scatter.sems(1, ND),
        compiler_params=pltpu.CompilerParams(collective_id=cid, has_side_effects=True, vmem_limit_bytes=60<<20),
        name="scatter_gradients",
    )(*parts)


D = 768
FF = 3072
HEADS = 12
HD = 64
SEQ = 64
QUAD = 4 * HD
EPS = 1e-05
NEG = -1e30
GELU_C = 0.7978845608028654
GELU_A = 0.044715
SCALE = 0.125
BF = jnp.bfloat16
F32 = jnp.float32
VM = pl.BlockSpec(memory_space=pltpu.VMEM)
ANY = pl.BlockSpec(memory_space=pl.ANY)
DMA = pltpu.SemaphoreType.DMA


def nn(a, b):
    return lax.dot_general(a, b, (((1,), (0,)), ((), ())), preferred_element_type=F32)


def nt(a, b):
    return lax.dot_general(a, b, (((1,), (1,)), ((), ())), preferred_element_type=F32)


def tn(a, b):
    return lax.dot_general(a, b, (((0,), (0,)), ((), ())), preferred_element_type=F32)


def unit_of(values):
    centre = values - jnp.mean(values, -1, keepdims=True)
    scaled = lax.rsqrt(jnp.mean(centre * centre, -1, keepdims=True) + EPS)
    return centre * scaled, scaled


def norm_backward(upstream, unit, scaled, gain):
    through = upstream * gain
    return scaled * (
        through - jnp.mean(through, -1, keepdims=True) - unit * jnp.mean(through * unit, -1, keepdims=True)
    )


def head_masks(width):
    lane = lax.broadcasted_iota(jnp.int32, (1, width), 1) // HD
    return [(lane == head).astype(F32).astype(BF) for head in range(width // HD)]


def stacked(values, masks):
    return jnp.concatenate([values * mask for mask in masks], 0)


def own_blocks(values):
    lane = lax.broadcasted_iota(jnp.int32, (HD, QUAD), 1) // HD
    total = values[:HD]
    for head in range(1, 4):
        total = jnp.where(lane == head, values[head * HD : (head + 1) * HD], total)
    return total


def load(source, target, sem):
    return pltpu.make_async_copy(source, target, sem)


def call(kernel, name, outs, ins, specs, scratch, flops, out_specs=None, cid=None, limit=56 << 20):
    params = dict(vmem_limit_bytes=limit)
    if cid is not None:
        params.update(collective_id=cid, has_side_effects=True)
    size = lambda a: a.size * a.dtype.itemsize
    return pl.pallas_call(
        kernel,
        out_shape=outs,
        in_specs=specs,
        out_specs=out_specs or [VM] * len(outs),
        scratch_shapes=scratch,
        compiler_params=pltpu.CompilerParams(**params),
        cost_estimate=pl.CostEstimate(flops=int(flops), transcendentals=0, bytes_accessed=sum(map(size, ins)) + sum(map(size, outs))),
        name=name,
    )(*ins)


def arr(shape, dtype=BF):
    return jax.ShapeDtypeStruct(shape, dtype)


def text_forward_kernel(text, packed, tail, h1, q1, k1, v1, p1, c1, x2, h2, q2, gains, w, gw, sem, between=lambda k: None):
    weights = [load(packed.at[:, pl.ds(j * D, D)] if j < 4 else tail.at[:, pl.ds(0, D)], w.at[j], sem.at[j]) for j in range(5)]
    gcopy = load(tail.at[:, pl.ds(D, 128)], gw, sem.at[5])
    gcopy.start()
    for copy in weights:
        copy.start()
    x = text[...].astype(F32)
    unit, _ = unit_of(x)
    gcopy.wait()
    gains[...] = gw[...].astype(F32).T[:8]
    h1[...] = (unit * gains[0:1]).astype(BF)
    for j, ref in enumerate((q1, k1, v1)):
        weights[j].wait()
        ref[...] = nn(h1[...], w[j]).astype(BF)
    between(0)
    rows = text.shape[0]
    first = lax.broadcasted_iota(jnp.int32, (rows, rows), 0)
    second = lax.broadcasted_iota(jnp.int32, (rows, rows), 1)
    allowed = jnp.logical_and(first >= second, first // SEQ == second // SEQ)
    masks = head_masks(128)
    for pair in range(HEADS // 2):
        lanes = slice(pair * 128, (pair + 1) * 128)
        total = None
        for j, mask in enumerate(masks):
            scores = nt(q1[:, lanes] * mask, k1[:, lanes]) * SCALE
            scores = jnp.where(allowed, scores, NEG)
            powers = jnp.exp(scores - jnp.max(scores, -1, keepdims=True))
            probs = (powers / jnp.sum(powers, -1, keepdims=True)).astype(BF)
            p1[2 * pair + j] = probs
            part = nn(probs, v1[:, lanes] * mask)
            total = part if total is None else total + part
        c1[:, lanes] = total.astype(BF)
    between(1)
    weights[3].wait()
    second_res = x + nn(c1[...], w[3])
    x2[...] = second_res
    unit, _ = unit_of(second_res)
    h2[...] = (unit * gains[1:2]).astype(BF)
    weights[4].wait()
    q2[...] = nn(h2[...], w[4]).astype(BF)


def text_forward(text, packed, tail):
    rows = text.shape[0]
    low = arr((rows, D))
    return call(
        text_forward_kernel, "text_forward",
        [low, low, low, low, arr((HEADS, rows, rows)), low, arr((rows, D), F32), low, low, arr((8, D), F32)],
        [text, packed, tail], [VM, ANY, ANY],
        [pltpu.VMEM((5, D, D), BF), pltpu.VMEM((D, 128), BF), DMA((6,))], 10 * rows * D * D)


TICKS = (3, 6, 8, 10)


def remote(src, dst, send, recv, device):
    return pltpu.make_async_remote_copy(
        src_ref=src, dst_ref=dst, send_sem=send, recv_sem=recv, device_id=device, device_id_type=MESH)


def cross_forward_kernel(NDP, KV, q2, image, lengths, patches, both, out_part, up_part, down_part,
                         c2, lse, keys, vals, e, stats, qall, second, third, down, w, obuf, ro, rst, usable, block, wide, down_block,
                         wsem, ssem, rsem, fsem, *gsems):
    at = place(NDP, KV)
    fills = fill_second(out_part, up_part, down_part, block, wide, down_block, fsem)
    found = cross_weights(both, w, wsem)
    own_copy = load(q2, qall.at[at.ki], wsem.at[2])
    own_copy.start()
    enter(at, True)
    for copy in fills:
        copy.wait()
    plane = PlaneGather(at, [wide], [third], gsems[6:], at.fixed)
    gather = Gather(at, [block, down_block], [second, down], gsems[:6], at.fixed)
    plane.start()
    gather.start()
    cross_forward_part(at, plane, gather, 0, lambda: found, own_copy, q2, image, lengths, patches,
                       c2, lse, keys, vals, e, stats, qall, w, obuf, ro, rst, usable, ssem, rsem)


def fill_second(out_part, up_part, down_part, block, wide, down_block, fsem):
    fills = fill_block([out_part, up_part.at[:, pl.ds(0, D)]], block, fsem)
    late = [load(down_part, down_block, fsem.at[2]), load(up_part.at[:, pl.ds(D, FF - D)], wide, fsem.at[3])]
    for copy in late:
        copy.start()
    return fills + late


def cross_weights(pair, w, sem):
    weights = [load(pair.at[:, pl.ds(j * D, D)], w.at[j], sem.at[j]) for j in range(2)]
    for copy in weights:
        copy.start()
    return weights


def cross_forward_part(at, plane, gather, done, weights, own_copy, q2, image, lengths, patches,
                       c2, lse, keys, vals, e, stats, qall, w, obuf, ro, rst, usable, ssem, rsem, after=lambda: None):
    di, ki, x, c = at.di, at.ki, at.x, at.c
    caps, tokens = patches.shape
    own_caps = caps // 4
    core, over, diag = 2 * x + 1 - c, 2 * (1 - x) + c, 2 * (1 - x) + 1 - c
    to_core = remote(q2, qall.at[ki], ssem.at[0], rsem.at[ki], (di, core))
    to_over = remote(q2, qall.at[ki], ssem.at[1], rsem.at[ki], (di, over))
    to_over.start()
    to_core.start()
    weights = weights()
    row = lax.broadcasted_iota(jnp.int32, usable.shape, 0)
    limit = jnp.zeros(usable.shape, jnp.int32)
    for cap in range(caps):
        limit = jnp.where(row == cap, lengths[cap], limit)
    position = lax.broadcasted_iota(jnp.int32, usable.shape, 1) + ki * tokens
    usable[...] = jnp.zeros(usable.shape, BF)
    usable[0:caps, :] = jnp.where(jnp.logical_and(position < limit, True)[0:caps], (patches[...] == 1).astype(F32), 0.0).astype(BF)
    weights[0].wait()

    def project(j, ref, i):
        rows = pl.ds(pl.multiple_of(i * tokens, 16), tokens)
        ref[rows, :] = nn(image[rows, :], w[j]).astype(BF)

    lax.fori_loop(0, caps, lambda i, _: (project(0, keys, i), 0)[1], 0)
    load(qall.at[over], qall.at[over], rsem.at[over]).wait()
    relay = remote(qall.at[over], qall.at[over], ssem.at[2], rsem.at[over], (di, core))
    relay.start()
    plane.tick(done)
    gather.tick(done)
    weights[1].wait()
    lax.fori_loop(0, caps, lambda i, _: (project(1, vals, i), 0)[1], 0)
    plane.tick(done + 1)
    gather.tick(done + 1)
    load(qall.at[core], qall.at[core], rsem.at[core]).wait()
    load(qall.at[diag], qall.at[diag], rsem.at[diag]).wait()
    own_copy.wait()
    masks = head_masks(QUAD)

    def owner_of(step):
        return 2 * ((x + 1 + step // 2) % 2) + (c + 1 + step % 2) % 2

    def attend(i, _):
        owner, local = owner_of(i // own_caps), i % own_caps
        cap = owner * own_caps + local
        rows = pl.ds(pl.multiple_of(cap * tokens, 16), tokens)
        queries = pl.ds(pl.multiple_of(local * SEQ, 16), SEQ)
        for j, when in enumerate(TICKS):
            @pl.when(i == when * caps // 12)
            def _():
                plane.tick(done + 2 + j)
                gather.tick(done + 2 + j)
        chosen = (lax.broadcasted_iota(jnp.int32, (usable.shape[0], QUAD), 0) == cap).astype(F32).astype(BF)
        shift = tn(usable[...], chosen)
        for g in range(3):
            lanes = slice(g * QUAD, (g + 1) * QUAD)
            scores = nt(keys[rows, lanes], stacked(qall[owner, queries, lanes], masks)) * SCALE
            scores = jnp.where(shift > 0.5, scores, NEG)
            top = jnp.max(scores, 0, keepdims=True)
            powers = jnp.where(shift > 0.5, jnp.exp(scores - top), 0.0)
            low = powers.astype(BF)
            e[pl.ds(pl.multiple_of((cap * 3 + g) * tokens, 16), tokens), :] = low
            stats[owner, pl.ds(3 * local + g, 1), :] = top
            stats[owner, pl.ds(16 + 3 * local + g, 1), :] = jnp.sum(powers, 0, keepdims=True)
            obuf[owner, queries, lanes] = own_blocks(tn(low, vals[rows, lanes])).astype(BF)

        @pl.when(jnp.logical_and(local == own_caps - 1, owner != ki))
        def _():
            remote(obuf.at[owner], ro.at[ki], ssem.at[3 + owner], rsem.at[4 + ki], (di, owner)).start()
            remote(stats.at[owner], rst.at[ki], ssem.at[7 + owner], rsem.at[8 + ki], (di, owner)).start()

        return 0

    lax.fori_loop(0, caps, attend, 0)
    after()
    ro[ki] = obuf[ki]
    rst[ki] = stats[ki]
    for other in (core, over, diag):
        load(ro.at[other], ro.at[other], rsem.at[4 + other]).wait()
        load(rst.at[other], rst.at[other], rsem.at[8 + other]).wait()
    lane = lax.broadcasted_iota(jnp.int32, (HD, QUAD), 1) // HD

    def combine(local, _):
        queries = pl.ds(pl.multiple_of(local * SEQ, 16), SEQ)
        for g in range(3):
            row = pl.ds(3 * local + g, 1)
            row_sum = pl.ds(16 + 3 * local + g, 1)
            tops = [rst[k, row, :] for k in range(4)]
            top = jnp.maximum(jnp.maximum(tops[0], tops[1]), jnp.maximum(tops[2], tops[3]))
            parts = [jnp.exp(t - top) for t in tops]
            total = sum(part * rst[k, row_sum, :] for k, part in enumerate(parts))
            lse[row, :] = top + jnp.log(total)
            table = jnp.concatenate([part / total for part in parts] * 2, 0).T
            mixed = 0.0
            for k in range(4):
                column = table[:, k : k + 1]
                weight = column[:HD] * jnp.ones((HD, QUAD), F32)
                for head in range(1, 4):
                    weight = jnp.where(lane == head, column[head * HD : (head + 1) * HD], weight)
                mixed = mixed + weight * ro[k, queries, g * QUAD : (g + 1) * QUAD].astype(F32)
            c2[queries, g * QUAD : (g + 1) * QUAD] = mixed
        return 0

    lax.fori_loop(0, own_caps, combine, 0)
    to_core.wait_send()
    to_over.wait_send()
    relay.wait_send()
    for other in (core, over, diag):
        load(obuf.at[other], obuf.at[other], ssem.at[3 + other]).wait()
        load(stats.at[other], stats.at[other], ssem.at[7 + other]).wait()
    plane.finish(done + 2 + len(TICKS))
    gather.finish(done + 2 + len(TICKS))


def forward_kernel(NDP, KV, *refs):
    text, image, lengths, patches, *parts = refs[:15]
    firsts, crosses, (out_part, up_part, down_part) = parts[:6], parts[6:8], parts[8:]
    h1, q1, k1, v1, p1, c1, x2, h2, gains, c2, lse, stats, qall, *outs = refs[15:37]
    keys_out, vals_out, e_out, packed, tail, both, second, third, down = outs
    (q2, tw, gw, keys, vals, e, pixels, w, obuf, ro, rst, usable, block, wide, down_block, pack, pack_tail, pack_both,
     tsem, wsem, ssem, rsem, fsem, sem, osem) = refs[37:62]
    gsems = refs[62:]
    copies = fill_block(firsts[:-2], pack, sem) + fill_block(firsts[-2:], pack_tail, sem.at[pl.ds(4, 2)])
    copies += fill_block(crosses, pack_both, sem.at[pl.ds(6, 2)])
    fills = fill_second(out_part, up_part, down_part, block, wide, down_block, fsem)
    image_copy = load(image, pixels, osem.at[3])
    image_copy.start()
    at = place(NDP, KV)
    enter(at, True)
    for copy in copies:
        copy.wait()
    plane = PlaneGather(at, [pack_tail], [tail], gsems[0:6], at.split)
    gather = Gather(at, [pack], [packed], gsems[6:12], at.split)
    middle = Gather(at, [pack_both], [both], gsems[12:18], at.split)
    late_plane = PlaneGather(at, [wide], [third], gsems[18:24], at.fixed)
    late = Gather(at, [block, down_block], [second, down], gsems[24:30], at.fixed)
    plane.start()
    gather.start()
    plane.tick(0)
    for copy in fills:
        copy.wait()
    image_copy.wait()
    last = min(at.Z, 4)
    for k in range(1, last):
        gather.tick(k - 1)
        plane.tick(k)
        if k == 1:
            middle.start()
        else:
            middle.tick(k - 2)
    gather.finish(last - 1)
    late_plane.start()
    late.start()
    plane.finish(last)

    def between(k):
        middle.tick(last - 2 + k)
        late_plane.tick(k)
        late.tick(k)

    text_forward_kernel(text, packed, tail, h1, q1, k1, v1, p1, c1, x2, h2, q2, gains, tw, gw, tsem, between)
    own_copy = load(q2, qall.at[at.ki], wsem.at[2])
    own_copy.start()
    results = [load(keys, keys_out, osem.at[0]), load(vals, vals_out, osem.at[1]), load(e, e_out, osem.at[2])]

    def weights():
        middle.finish(last)
        return cross_weights(both, w, wsem)

    def after():
        for copy in results:
            copy.start()

    cross_forward_part(at, late_plane, late, 2, weights, own_copy, q2, pixels, lengths, patches,
                       c2, lse, keys, vals, e, stats, qall, w, obuf, ro, rst, usable, ssem, rsem, after)
    for copy in results:
        copy.wait()


def forward(text, image, lengths, patches, firsts, crosses, out_part, up_part, down_part, NDP, KV, cid):
    rows, (caps, tokens), ND = text.shape[0], patches.shape, NDP * KV
    lows = out_part.shape[0]
    low, wide_row = arr((rows, D)), arr((rows, D), F32)
    keys, scores = (caps * tokens, D), (caps * 3 * tokens, QUAD)
    ins = [text, image, lengths, patches, *firsts, *crosses, out_part, up_part, down_part]
    V = pltpu.VMEM
    return call(
        functools.partial(forward_kernel, NDP, KV), "forward",
        [low, low, low, low, arr((HEADS, rows, rows)), low, wide_row, low, arr((8, D), F32),
         wide_row, arr((16, QUAD), F32), arr((4, 32, QUAD), F32), arr((4, rows, D)),
         arr(keys), arr(keys), arr(scores), arr((D, 4 * D)), arr((D, D + 128)), arr((D, 2 * D)),
         arr((D, 2 * D)), arr((D, FF - D)), arr((FF, D))],
        ins, [VM, ANY, pl.BlockSpec(memory_space=pltpu.SMEM), VM] + [ANY] * 11,
        [V((rows, D), BF), V((5, D, D), BF), V((D, 128), BF), V(keys, BF), V(keys, BF), V(scores, BF), V(keys, BF),
         V((2, D, D), BF), V((4, rows, D), BF), V((4, rows, D), BF), V((4, 32, QUAD), F32),
         V((-(-caps // 16) * 16, tokens), BF), V((lows, 2 * D), BF), V((lows, FF - D), BF), V(down_part.shape, BF),
         V((lows, 4 * D), BF), V((lows, D + 128), BF), V((lows, 2 * D), BF),
         DMA((6,)), DMA((3,)), DMA((11,)), DMA((12,)), DMA((4,)), DMA((8,)), DMA((4,))]
        + PlaneGather.sems(1, ND) + Gather.sems(1, ND) + Gather.sems(1, ND) + PlaneGather.sems(1, ND) + Gather.sems(2, ND),
        6 * caps * tokens * D * D, out_specs=[VM] * 13 + [ANY] * 9, cid=cid, limit=62 << 20)


def cross_forward(q2, image, lengths, patches, both, out_part, up_part, down_part, NDP, KV, cid):
    rows, (caps, tokens), ND = q2.shape[0], patches.shape, NDP * KV
    lows = out_part.shape[0]
    return call(
        functools.partial(cross_forward_kernel, NDP, KV), "cross_forward",
        [arr((rows, D), F32), arr((16, QUAD), F32), arr((caps * tokens, D)), arr((caps * tokens, D)),
         arr((caps * 3 * tokens, QUAD)), arr((4, 32, QUAD), F32), arr((4, rows, D)),
         arr((ND, lows, 2 * D)), arr((ND, lows, FF - D)), arr((ND,) + down_part.shape)],
        [q2, image, lengths, patches, both, out_part, up_part, down_part],
        [VM, VM, pl.BlockSpec(memory_space=pltpu.SMEM), VM, ANY, ANY, ANY, ANY],
        [pltpu.VMEM((2, D, D), BF), pltpu.VMEM((4, rows, D), BF), pltpu.VMEM((4, rows, D), BF),
         pltpu.VMEM((4, 32, QUAD), F32), pltpu.VMEM((-(-caps // 16) * 16, tokens), BF),
         pltpu.VMEM((lows, 2 * D), BF), pltpu.VMEM((lows, FF - D), BF), pltpu.VMEM(down_part.shape, BF),
         DMA((3,)), DMA((11,)), DMA((12,)), DMA((4,))] + Gather.sems(2, ND) + PlaneGather.sems(1, ND),
        4 * caps * tokens * D * D, out_specs=[VM] * 7 + [ANY] * 3, cid=cid)


BACK_TICKS = (4, 9)


def text_backward_kernel(dq2, dx3, text, x2, h1, h2, c1, q1, k1, v1, p1, gains, ng3, packed, tail,
                         text_grad, wq, wk, wv, wo, wcq, ngs, w, dq, dk, dv, rows_t, sem, between):
    slots = (2, 0, 1, 1, 0)
    weights = [load(packed.at[:, pl.ds(j * D, D)] if j < 4 else tail.at[:, pl.ds(0, D)], w.at[slots[j]], sem.at[j]) for j in range(5)]
    for j in (4, 3, 0):
        weights[j].start()
    unit, scaled = unit_of(x2[...])
    weights[4].wait()
    upstream = nt(dq2[...], w[0])
    weights[1].start()
    ngs_two = jnp.sum(upstream * unit, 0, keepdims=True)
    grad_two = dx3[...] + norm_backward(upstream, unit, scaled, gains[1:2])
    wcq[...] = tn(h2[...], dq2[...]).astype(BF)
    branch = grad_two.astype(BF)
    weights[3].wait()
    dc1 = nt(branch, w[1]).astype(BF)
    weights[2].start()
    wo[...] = tn(c1[...], branch).astype(BF)
    between(0)
    masks = head_masks(128)
    for pair in range(HEADS // 2):
        lanes = slice(pair * 128, (pair + 1) * 128)
        sums = [None] * 3
        for j, mask in enumerate(masks):
            low = p1[2 * pair + j]
            probs = low.astype(F32)
            above = dc1[:, lanes] * mask
            grad = nt(above, v1[:, lanes])
            grad = (probs * (grad - jnp.sum(probs * grad, -1, keepdims=True))).astype(BF)
            parts = [nn(grad, k1[:, lanes] * mask), tn(grad, q1[:, lanes] * mask), tn(low, above)]
            sums = parts if j == 0 else [a + b for a, b in zip(sums, parts)]
        dq[:, lanes] = (sums[0] * SCALE).astype(BF)
        dk[:, lanes] = (sums[1] * SCALE).astype(BF)
        dv[:, lanes] = sums[2].astype(BF)
    between(1)
    upstream = None
    flipped = h1[...].T
    for j, (ref, out) in enumerate(((dq, wq), (dk, wk), (dv, wv))):
        weights[j].wait()
        part = nt(ref[...], w[slots[j]])
        upstream = part if j == 0 else upstream + part
        out[...] = nn(flipped, ref[...]).astype(BF)
    unit, scaled = unit_of(text[...].astype(F32))
    text_grad[...] = grad_two + norm_backward(upstream, unit, scaled, gains[0:1])
    rows_t[...] = jnp.zeros_like(rows_t)
    rows_t[0:1] = jnp.sum(upstream * unit, 0, keepdims=True)
    rows_t[1:2] = ngs_two
    rows_t[2:3] = ng3[0:1]
    ngs[...] = rows_t[...].T.astype(BF)


def backward_kernel(NDP, KV, dc2, c2, lse, stats, qall, keys, vals, e, image,
                    dx3, text, x2, h1, h2, c1, q1, k1, v1, p1, gains, ng3, packed, tail, both, dco, dup, ddown,
                    wk, wv, igrad, sum_a, sum_b, sum_c, text_grad, wsq, wsk, wsv, wso, wcq, ngs,
                    dq2, dk, dv, w, ibuf, tw, dq, dk1, dv1, rows_t, tsem,
                    dall, sall, qbuf, rq, csem, wsem, isem, ssem, rsem, *more):
    at = place(NDP, KV)
    di, ki, x, c = at.di, at.ki, at.x, at.c
    held = [load(keys, dk, wsem.at[2]), load(vals, dv, wsem.at[3])]
    for copy in held:
        copy.start()
    weights = cross_weights(both, w, wsem)
    rows_all = dk.shape[0]
    caps = 4 * (dc2.shape[0] // SEQ)
    own_caps = caps // 4
    tokens = rows_all // caps
    core, over, diag = 2 * x + 1 - c, 2 * (1 - x) + c, 2 * (1 - x) + 1 - c
    masks = head_masks(QUAD)
    sall[ki, 0:16, :] = lse[...]

    def dots(local, _):
        queries = pl.ds(pl.multiple_of(local * SEQ, 16), SEQ)
        for g in range(3):
            lanes = slice(g * QUAD, (g + 1) * QUAD)
            product = dc2[queries, lanes].astype(F32) * c2[queries, lanes]
            product = jnp.concatenate([product * mask.astype(F32) for mask in masks], 0)
            sums = lax.dot_general(
                jnp.ones((8, QUAD), F32), product, (((1,), (1,)), ((), ())),
                preferred_element_type=F32, precision=lax.Precision.HIGHEST)
            sall[ki, pl.ds(16 + 3 * local + g, 1), :] = sums[0:1]
        return 0

    own_copy = load(dc2, dall.at[ki], csem)
    own_copy.start()
    enter(at, True)
    plane = PlaneScatter(at, [(dup, 0, D, 0, FF - D)], more[0:5], more[5:14], at.fixed)
    scatter = Scatter(at, [(dco, 0, 0, 0, D), (dup, 0, 0, D, D), (ddown, 1, 0, 0, D)], more[14:24], more[24:], at.split)
    to_over = remote(dc2, dall.at[ki], ssem.at[1], rsem.at[ki], (di, over))
    to_core = remote(dc2, dall.at[ki], ssem.at[0], rsem.at[ki], (di, core))
    to_over.start()
    to_core.start()
    plane.start()
    scatter.start()
    lax.fori_loop(0, own_caps, dots, 0)
    small = [remote(sall.at[ki], sall.at[ki], ssem.at[2 + j], rsem.at[4 + ki], (di, other))
             for j, other in enumerate((core, over, diag))]
    for copy in small:
        copy.start()
    own_copy.wait()
    for copy in held:
        copy.wait()
    plane.tick(0)
    scatter.tick(0)
    relay = remote(dall.at[over], dall.at[over], ssem.at[5], rsem.at[over], (di, core))

    def attend(i, _):
        step, local = i // own_caps, i % own_caps
        owner = 2 * ((x + step // 2) % 2) + (c + step % 2) % 2

        @pl.when(i == own_caps)
        def _():
            load(dall.at[core], dall.at[core], rsem.at[core]).wait()
            load(sall.at[core], sall.at[core], rsem.at[4 + core]).wait()

        @pl.when(i == 2 * own_caps - 1)
        def _():
            load(dall.at[over], dall.at[over], rsem.at[over]).wait()
            relay.start()

        @pl.when(i == 2 * own_caps)
        def _():
            load(sall.at[over], sall.at[over], rsem.at[4 + over]).wait()

        @pl.when(i == 3 * own_caps)
        def _():
            load(dall.at[diag], dall.at[diag], rsem.at[diag]).wait()
            load(sall.at[diag], sall.at[diag], rsem.at[4 + diag]).wait()

        for j, when in enumerate(BACK_TICKS):
            @pl.when(i == when * caps // 12)
            def _():
                plane.tick(1 + j)
                scatter.tick(1 + j)

        cap = owner * own_caps + local
        rows = pl.ds(pl.multiple_of(cap * tokens, 16), tokens)
        queries = pl.ds(pl.multiple_of(local * SEQ, 16), SEQ)
        for g in range(3):
            lanes = slice(g * QUAD, (g + 1) * QUAD)
            factor = jnp.exp(stats[owner, pl.ds(3 * local + g, 1), :] - sall[owner, pl.ds(3 * local + g, 1), :])
            dots_row = sall[owner, pl.ds(16 + 3 * local + g, 1), :]
            probs = e[pl.ds(pl.multiple_of((cap * 3 + g) * tokens, 16), tokens), :].astype(F32) * factor
            upstream = stacked(dall[owner, queries, lanes], masks)
            queried = stacked(qall[owner, queries, lanes], masks)
            grad = nt(dv[rows, lanes], upstream)
            grad = (probs * (grad - dots_row)).astype(BF)
            qbuf[owner, queries, lanes] = (own_blocks(tn(grad, dk[rows, lanes])) * SCALE).astype(BF)
            dv[rows, lanes] = nn(probs.astype(BF), upstream).astype(BF)
            dk[rows, lanes] = (nn(grad, queried) * SCALE).astype(BF)

        @pl.when(jnp.logical_and(local == own_caps - 1, owner != ki))
        def _():
            remote(qbuf.at[owner], rq.at[ki], ssem.at[6 + owner], rsem.at[8 + ki], (di, owner)).start()

        return 0

    lax.fori_loop(0, caps, attend, 0)

    def weight(j, _):
        cols = pl.ds(pl.multiple_of(j * 256, 256), 256)
        flipped = image[:, cols].T
        wk[cols, :] = nn(flipped, dk[...]).astype(BF)
        wv[cols, :] = nn(flipped, dv[...]).astype(BF)
        return 0

    lax.fori_loop(0, D // 256, weight, 0)
    ticks = 1 + len(BACK_TICKS)
    plane.tick(ticks)
    scatter.tick(ticks)
    for copy in weights:
        copy.wait()

    def flush(i):
        return load(ibuf.at[i % 2], igrad.at[pl.ds(pl.multiple_of(i * tokens, 16), tokens), :], isem.at[i % 2])

    def image_rows(i, _):
        @pl.when(i >= 2)
        def _():
            flush(i - 2).wait()

        rows = pl.ds(pl.multiple_of(i * tokens, 16), tokens)
        ibuf[i % 2] = (nt(dk[rows, :], w[0]) + nt(dv[rows, :], w[1])).astype(BF)
        flush(i).start()
        return 0

    lax.fori_loop(0, caps, image_rows, 0)
    rq[ki] = qbuf[ki]
    for other in (core, over, diag):
        load(rq.at[other], rq.at[other], rsem.at[8 + other]).wait()
    dq2[...] = (rq[0].astype(F32) + rq[1].astype(F32) + rq[2].astype(F32) + rq[3].astype(F32)).astype(BF)

    def between(n):
        if n == 0:
            plane.tick(ticks + 1)
            scatter.tick(ticks + 1)

    text_backward_kernel(dq2, dx3, text, x2, h1, h2, c1, q1, k1, v1, p1, gains, ng3, packed, tail,
                         text_grad, wsq, wsk, wsv, wso, wcq, ngs, tw, dq, dk1, dv1, rows_t, tsem, between)
    to_core.wait_send()
    to_over.wait_send()
    relay.wait_send()
    for copy in small:
        copy.wait_send()
    for other in (core, over, diag):
        load(qbuf.at[other], qbuf.at[other], ssem.at[6 + other]).wait()
    flush(caps - 2).wait()
    flush(caps - 1).wait()
    plane.finish(ticks + 2, [sum_c])
    scatter.finish(ticks + 2, [sum_a, sum_b])


def backward(dc2, c2, lse, stats, qall, keys, vals, e, image, dx3, text, x2, h1, h2, c1, q1, k1, v1, p1, gains, ng3,
             packed, tail, both, dco, dup, ddown, NDP, KV, cid):
    rows, ND = dc2.shape[0], NDP * KV
    caps = 4 * (rows // SEQ)
    dco, dup, ddown = blocks(dco, ND), blocks(dup, ND), blocks(ddown, ND)
    ins = [dc2, c2, lse, stats, qall, keys, vals, e, image, dx3, text, x2, h1, h2, c1, q1, k1, v1, p1, gains, ng3,
           packed, tail, both, dco, dup, ddown]
    low = dco.shape[1]
    shapes = [(low, 2 * D), ddown.shape[1:], (low, FF - D)]
    V = pltpu.VMEM
    return call(
        functools.partial(backward_kernel, NDP, KV), "backward",
        [arr((D, D)), arr((D, D)), arr(keys.shape)] + [arr(s, F32) for s in shapes]
        + [arr((rows, D), F32)] + [arr((D, D))] * 5 + [arr((D, 128))],
        ins, [VM] * 5 + [ANY] * 2 + [VM] * 14 + [ANY] * 6,
        [V((rows, D), BF), V(keys.shape, BF), V(keys.shape, BF), V((2, D, D), BF), V((2, keys.shape[0] // caps, D), BF),
         V((3, D, D), BF), V((rows, D), BF), V((rows, D), BF), V((rows, D), BF), V((128, D), F32), DMA((5,)),
         V((4, rows, D), BF), V((4, 32, QUAD), F32), V((4, rows, D), BF), V((4, rows, D), BF),
         DMA, DMA((4,)), DMA((2,)), DMA((10,)), DMA((12,))]
        + PlaneScatter.bufs(shapes[2:], ND) + PlaneScatter.sems(1, ND) + Scatter.bufs(shapes[:2], ND) + Scatter.sems(2, ND),
        4 * keys.shape[0] * D * D, out_specs=[VM] * 2 + [ANY] + [VM] * 10, cid=cid, limit=65470 << 10)


def mlp_kernel(c2, x2, grad, gains, packed, wide, down, out, dx3, dc2, dup, ddown, dco, ng, wu, wd, wc, dh, acc, ht, sem):
    wcopy = load(packed.at[:, pl.ds(0, D)], wc, sem.at[8])
    wcopy.start()
    ups = [load(packed.at[:, pl.ds(D, D)] if j == 0 else wide.at[:, pl.ds((j - 1) * D, D)], wu.at[j], sem.at[j]) for j in range(4)]
    downs = [load(down.at[pl.ds(j * D, D), :], wd.at[j], sem.at[4 + j]) for j in range(4)]
    for j in range(4):
        ups[j].start()
        downs[j].start()
    low = c2[...].astype(BF)
    wcopy.wait()
    third = x2[...] + nn(low, wc[...])
    unit, scaled = unit_of(third)
    gain = gains[2:3]
    h3 = (unit * gain).astype(BF)
    ht[...] = h3.T
    g = grad[...]
    acc[...] = third
    for j in range(4):
        ups[j].wait()
        downs[j].wait()
        u = nn(h3, wu[j])
        square = u * u
        tanh_part = jnp.tanh(GELU_C * (u + GELU_A * square * u))
        active = (0.5 * u * (1.0 + tanh_part)).astype(BF)
        slope = 0.5 * (1.0 + tanh_part) + 0.5 * u * (1.0 - tanh_part * tanh_part) * GELU_C * (1.0 + 3.0 * GELU_A * square)
        acc[...] += nn(active, wd[j])
        du = (nt(g, wd[j]) * slope).astype(BF)
        part = nt(du, wu[j])
        dh[...] = part if j == 0 else dh[...] + part
        ddown[pl.ds(j * D, D), :] = tn(active, g).astype(BF)
        dup[:, pl.ds(j * D, D)] = nn(ht[...], du).astype(BF)
    out[...] = acc[...].astype(BF)
    upstream = dh[...]
    ng[...] = jnp.broadcast_to(jnp.sum(upstream * unit, 0, keepdims=True), ng.shape)
    total = g.astype(F32) + norm_backward(upstream, unit, scaled, gain)
    dx3[...] = total
    branch = total.astype(BF)
    dc2[...] = nt(branch, wc[...]).astype(BF)
    dco[...] = tn(low, branch).astype(BF)


def mlp(c2, x2, grad, gains, packed, wide, down):
    rows = c2.shape[0]
    return call(
        mlp_kernel, "feed_forward",
        [arr((rows, D)), arr((rows, D), F32), arr((rows, D)), arr((D, FF)), arr((FF, D)), arr((D, D)), arr((8, D), F32)],
        [c2, x2, grad, gains, packed, wide, down], [VM] * 4 + [ANY] * 3,
        [pltpu.VMEM((4, D, D), BF), pltpu.VMEM((4, D, D), BF), pltpu.VMEM((D, D), BF), pltpu.VMEM((rows, D), F32),
         pltpu.VMEM((rows, D), F32), pltpu.VMEM((D, rows), BF), DMA((9,))], 12 * rows * D * FF)


def deliver_kernel(widths, moves, gain, *refs):
    count = len(widths) + 3
    sources, outs = refs[: -count - 4], refs[-count - 4 : -4]
    narrow, moved, sem, msem = refs[-4:]
    *sources, text_grad, igrad = sources
    *outs, norms, text_out, image_out = outs
    size = igrad.shape[0] // 6
    pieces = [pl.ds(j * size, size) for j in range(6)]
    inward = [load(igrad.at[rows, :], narrow.at[rows, :], msem.at[j]) for j, rows in enumerate(pieces)]
    outward = [load(moved.at[rows, :], image_out.at[rows, :], msem.at[j]) for j, rows in enumerate(pieces)]
    copies = [load(text_grad, text_out, msem.at[6])]
    for (i, offset, width, j, to) in moves:
        copies.append(load(sources[i].at[:, pl.ds(offset, width)], outs[j].at[:, pl.ds(to, width)], sem.at[len(copies) - 1]))
    for copy in inward + copies:
        copy.start()
    i, offset = gain
    block = sources[i][:, offset : offset + 128]
    block = jnp.concatenate([block, jnp.zeros((128 - block.shape[0], 128), F32)], 0)
    norms[...] = block.T[:8]
    for there, back, rows in zip(inward, outward, pieces):
        there.wait()
        moved[rows, :] = narrow[rows, :].astype(F32)
        back.start()
    for copy in copies + outward:
        copy.wait()


def deliver(sources, text_grad, igrad, widths, moves, gain):
    outs = [arr((rows, width), F32) for rows, width in widths]
    return call(
        functools.partial(deliver_kernel, widths, moves, gain), "deliver_gradients",
        outs + [arr((8, 128), F32), arr(text_grad.shape, F32), arr(igrad.shape, F32)], [*sources, text_grad, igrad],
        [VM] * (len(sources) + 1) + [ANY],
        [pltpu.VMEM(igrad.shape, BF), pltpu.VMEM(igrad.shape, F32), DMA((len(moves),)), DMA((7,))], 1,
        out_specs=[ANY] * len(outs) + [VM, ANY, ANY], limit=60 << 20)


def apart(text, image, lengths, patches, firsts, crosses, out_part, up_part, down_part, ndp, nkv):
    packed, tail = (a.reshape(D, -1) for a in all_gather(firsts[:4] + crosses + firsts[4:], ndp, nkv, 1))
    packed, both = packed[:, : 4 * D], packed[:, 4 * D :]
    h1, q1, k1, v1, p1, c1, x2, h2, q2, gains = text_forward(text, packed, tail)
    c2, lse, keys, vals, e, stats, qall, second, third, down = cross_forward(
        q2, image, lengths, patches, both, out_part, up_part, down_part, ndp, nkv, 2)
    second, third, down = second.reshape(D, -1), third.reshape(D, -1), down.reshape(FF, D)
    return h1, q1, k1, v1, p1, c1, x2, h2, gains, c2, lse, stats, qall, keys, vals, e, packed, tail, both, second, third, down


def per_device(
    text_tokens, image_tokens, image_lengths, patch_mask, self_query, self_key, self_value, self_out, cross_query,
    cross_key, cross_value, cross_out, mlp_up, mlp_down, norm_self, norm_cross, norm_mlp, out_grad,
):
    ndp, nkv = lax.axis_size("dp"), lax.axis_size("kv")
    caps, tokens = image_tokens.shape[0], image_tokens.shape[1]
    gain_block = jnp.pad(jnp.stack([norm_self, norm_cross, norm_mlp], 1), ((0, 0), (0, 125)))
    parts = [self_query, self_key, self_value, self_out, cross_query, gain_block]
    crosses = [cross_key, cross_value]
    image = image_tokens.reshape(caps * tokens, D)
    if self_query.shape[0] % 8 == 0:
        (h1, q1, k1, v1, p1, c1, x2, h2, gains, c2, lse, stats, qall, keys, vals, e, packed, tail, both, second, third, down) = forward(
            text_tokens, image, image_lengths, patch_mask, parts, crosses, cross_out, mlp_up, mlp_down, ndp, nkv, 1)
    else:
        (h1, q1, k1, v1, p1, c1, x2, h2, gains, c2, lse, stats, qall, keys, vals, e, packed, tail, both, second, third, down) = apart(
            text_tokens, image, image_lengths, patch_mask, parts, crosses, cross_out, mlp_up, mlp_down, ndp, nkv)
    layer_out, dx3, dc2, d_up, d_down, d_co, ng3 = mlp(c2, x2, out_grad, gains, second, third, down)
    d_ck, d_cv, igrad, sum_a, sum_b, sum_c, text_grad, d_q, d_k, d_v, d_o, d_cq, ngs = backward(
        dc2, c2, lse, stats, qall, keys, vals, e, image, dx3, text_tokens, x2, h1, h2, c1, q1, k1, v1, p1, gains, ng3,
        packed, tail, both, d_co, d_up, d_down, ndp, nkv, 3)
    sum_d, sum_e = reduce_scatter([d_q, d_k, d_v, d_o, d_cq, d_ck, d_cv, ngs], ndp, nkv, 4)
    rows = norm_self.shape[0]
    moves = [(3, j * D, D, j, 0) for j in range(6)] + [(4, 0, D, 6, 0), (0, 0, D, 7, 0), (0, D, D, 8, 0), (2, 0, FF - D, 8, D), (1, 0, D, 9, 0)]
    *parts, norms, text_grad, image_grad = deliver(
        [sum_a, sum_b, sum_c, sum_d, sum_e], text_grad, igrad, [(rows, D)] * 8 + [(rows, FF), mlp_down.shape], moves, (4, D))
    return (layer_out, text_grad, image_grad.reshape(caps, tokens, D), *parts, norms[0, :rows], norms[1, :rows], norms[2, :rows])


def solution(mesh):
    in_specs = (
        P(("dp", "kv"), None),
        P("dp", "kv", None),
        P("dp"),
        P("dp", "kv"),
        P(("dp", "kv"), None),
        P(("dp", "kv"), None),
        P(("dp", "kv"), None),
        P(("dp", "kv"), None),
        P(("dp", "kv"), None),
        P(("dp", "kv"), None),
        P(("dp", "kv"), None),
        P(("dp", "kv"), None),
        P(("dp", "kv"), None),
        P(("dp", "kv"), None),
        P(("dp", "kv")),
        P(("dp", "kv")),
        P(("dp", "kv")),
        P(("dp", "kv"), None),
    )
    out_specs = (
        P(("dp", "kv"), None),
        P(("dp", "kv"), None),
        P("dp", "kv", None),
        P(("dp", "kv"), None),
        P(("dp", "kv"), None),
        P(("dp", "kv"), None),
        P(("dp", "kv"), None),
        P(("dp", "kv"), None),
        P(("dp", "kv"), None),
        P(("dp", "kv"), None),
        P(("dp", "kv"), None),
        P(("dp", "kv"), None),
        P(("dp", "kv"), None),
        P(("dp", "kv")),
        P(("dp", "kv")),
        P(("dp", "kv")),
    )
    return jax.shard_map(
        per_device, mesh=mesh, in_specs=in_specs, out_specs=out_specs, check_vma=False
    )
```
